32 devices in a mesh: row: 4 (over y, x), col: 8 (over z, core).
Axes of the slice: x: 2, y: 2, z: 4, core: 2. Of those that a mesh axis runs over, the one named last changes fastest.
Arguments:
- final_sens: float32 [32, 2048, 1024], P(None, 'col', 'row'), may hold values from -6 to 6
- courant: float32 [2, 2, 8, 2048, 1024], P(None, None, None, 'col', 'row'), may hold values from 0.03 to 0.45
- limiter: int32 [2, 4, 2048, 1024], P(None, None, 'col', 'row'), may hold values from 0 to 1
- directions: int32 [2, 2, 2048, 1024], P(None, None, 'col', 'row'), may hold values from 0 to 1
- nest_sens: float32 [32, 768, 96], P(None, 'col', 'row'), may hold values from -6 to 6
- box_lon: int32 [1], replicated, may hold values from 0 to 1792
- box_lat: int32 [1], replicated, may hold values from 0 to 992
- eof: float32 [32, 32], replicated, may hold values from -1.1 to 2.1
- lat_filter: bfloat16 [1024, 1024], replicated, may hold values from -1.1 to 2.1
- lon_filter: bfloat16 [2048, 2048], P('row'), may hold values from -1.1 to 2.1
Outputs:
- gradient: float32 [1024, 32, 2048], P('col', 'row')
The draws below stay inside these ranges and needn't reach their ends.
All inputs are finite; a program needn't handle non-finite values.
Results may differ from the reference program's by a relative error of at most 0.00065.
The reference program's roundings to bfloat16 on the way (of `control` and `smoothed`) count: a program that leaves them out, or rounds other values in their place, can miss the bound.
Values may be sent and summed in bfloat16 or wider, within the bound.
No kernel may reach another device: no remote copies, remote signals or barrier semaphores. Data moves between devices by JAX's collectives and lax.ppermute only.
A program may use at most 192 MiB of HBM per device.

```python
import math
import jax
import jax.numpy as jnp
from jax import lax

NF = 4
NL = 8
NLON = 2048
NLAT = 1024
STEPS = 2
RATIO = 3
BOXX = 256
BOXY = 32
CH = 32


def dominant(key, order, marker):
    key_diag, key_off = jax.random.split(jax.random.fold_in(key, marker))
    diagonal = jax.random.uniform(key_diag, (order,), jnp.float32, 0.6, 1.0)
    off_part = jnp.clip(jax.random.normal(key_off, (order, order), jnp.float32), -6.0, 6.0) * (0.5 / math.sqrt(order))
    return off_part + jnp.diag(diagonal)


def draw_eof(key, part):
    return dominant(key, CH, 1117)


def draw_lat_filter(key, part):
    return dominant(key, NLAT, 2239).astype(jnp.bfloat16)


def draw_lon_filter(key, part):
    return dominant(key, NLON, 3361).astype(jnp.bfloat16)


def with_ends(array, stream_key, least, top_value):
    shape = array.shape
    place = [jax.random.randint(jax.random.fold_in(stream_key, axis), (), 0, shape[axis]) for axis in range(len(shape))]
    array = array.at[tuple(place)].set(least)
    longest = shape.index(max(shape))
    place[longest] = (place[longest] + 1) % shape[longest]
    return array.at[tuple(place)].set(top_value)


def block_scale(rng, dims, cuts, low, largest):
    def one(dim, shards_of):
        steps = jax.random.uniform(jax.random.fold_in(jax.random.fold_in(rng, 6), dim), (shards_of,), jnp.float32, low / len(cuts), largest / len(cuts))
        return jnp.repeat(jnp.exp(steps), dims[dim] // shards_of).reshape((-1,) + (1,) * (len(dims) - dim - 1))

    level = one(*cuts[0])
    for cut in cuts[1:]:
        level = level * one(*cut)
    return level


def bell_draw(key, extent, scale, reach, cuts=(), kind=jnp.bfloat16):
    values = jax.random.normal(key, extent, jnp.float32) * scale
    if len(cuts) > 0:
        values = block_scale(key, extent, cuts, -0.22, 0.18) * values
    return jnp.clip(values, min=-reach, max=reach).astype(kind)


def setup_inputs(seed: int = 0) -> dict:
    arg_keys = jax.random.split(jax.random.key(seed), 11)
    return {
        "final_sens": bell_draw(arg_keys[0], (CH, NLON, NLAT), 1.0, 6.0, ((1, 8), (2, 4)), jnp.float32),
        "courant": jnp.clip(jnp.exp(math.log(0.45) - 2.7080502 * jax.random.uniform(arg_keys[1], (STEPS, 2, NL, NLON, NLAT), jnp.float32) ** block_scale(arg_keys[1], (STEPS, 2, NL, NLON, NLAT), ((3, 8), (4, 4)), -0.2, 0.2)), 0.03, 0.45),
        "limiter": with_ends(jax.random.randint(arg_keys[2], (STEPS, NF, NLON, NLAT), 0, 2), jax.random.fold_in(arg_keys[2], 1), 0, 1).astype(jnp.int32),
        "directions": with_ends(jax.random.randint(arg_keys[3], (STEPS, 2, NLON, NLAT), 0, 2), jax.random.fold_in(arg_keys[3], 1), 0, 1).astype(jnp.int32),
        "nest_sens": bell_draw(arg_keys[4], (CH, RATIO * BOXX, RATIO * BOXY), 1.0, 6.0, ((1, 8), (2, 4)), jnp.float32),
        "box_lon": jax.random.randint(arg_keys[5], (1,), 0, NLON - BOXX + 1).astype(jnp.int32),
        "box_lat": jax.random.randint(arg_keys[6], (1,), 0, NLAT - BOXY + 1).astype(jnp.int32),
        "eof": draw_eof(jax.random.fold_in(arg_keys[10], 71), 0),
        "lat_filter": draw_lat_filter(jax.random.fold_in(arg_keys[10], 71), 0),
        "lon_filter": draw_lon_filter(jax.random.fold_in(arg_keys[10], 71), 0),
    }


def combine(center, terms):
    inner = center - terms[0][:, 1:-1, 1:-1] + terms[1][:, 1:-1, 1:-1] - terms[2][:, 1:-1, 1:-1] + terms[3][:, 1:-1, 1:-1]
    return inner + terms[0][:, 2:, 1:-1] - terms[1][:, :-2, 1:-1] + terms[2][:, 1:-1, 2:] - terms[3][:, 1:-1, :-2]


def reference(final_sens, courant, limiter, directions, nest_sens, box_lon, box_lat, eof, lat_filter, lon_filter):
    def field_adjoint(inputs):
        current, field_limiter = inputs
        for step_index in reversed(range(STEPS)):
            damping = 0.5 + 0.5 * field_limiter[step_index].astype(jnp.float32)
            coef_x = damping[None] * courant[step_index, 0]
            coef_y = damping[None] * courant[step_index, 1]
            eastward = directions[step_index, 0].astype(jnp.float32)[None]
            northward = directions[step_index, 1].astype(jnp.float32)[None]
            weights = (eastward * coef_x, (1.0 - eastward) * coef_x, northward * coef_y, (1.0 - northward) * coef_y)
            terms = jnp.stack([w_part * current for w_part in weights])
            padded = jnp.pad(terms, ((0, 0), (0, 0), (1, 1), (1, 1)))
            current = combine(current, padded)
        return current

    adjoint = lax.map(field_adjoint, (final_sens.reshape(NF, NL, NLON, NLAT), jnp.swapaxes(limiter, 0, 1)))
    total = adjoint.reshape(CH, NLON, NLAT)
    lon_index = lax.broadcasted_iota(jnp.int32, (RATIO * BOXX, 1), 0)
    lat_index = lax.broadcasted_iota(jnp.int32, (1, RATIO * BOXY), 1)
    cycle = (lon_index < RATIO) | (lon_index >= RATIO * BOXX - RATIO) | (lat_index < RATIO) | (lat_index >= RATIO * BOXY - RATIO)
    weight = jnp.where(cycle, jnp.float32(1.0), jnp.float32(1.0 / (RATIO * RATIO)))
    coarse = (nest_sens * weight[None]).reshape(CH, BOXX, RATIO, BOXY, RATIO).sum(axis=(2, 4))
    anchor = (jnp.zeros((), jnp.int32), box_lon[0].astype(jnp.int32), box_lat[0].astype(jnp.int32))
    before = lax.dynamic_slice(total, anchor, (CH, BOXX, BOXY))
    total = lax.dynamic_update_slice(total, before + coarse, anchor)
    control = jnp.dot(eof, total.reshape(CH, NLON * NLAT), precision=lax.Precision.HIGHEST)
    control = control.astype(jnp.bfloat16).reshape(CH, NLON, NLAT)
    smoothed = jnp.dot(control.reshape(CH * NLON, NLAT).astype(jnp.float32), lat_filter.astype(jnp.float32).T)
    smoothed = smoothed.astype(jnp.bfloat16).reshape(CH, NLON, NLAT)
    lines = jnp.transpose(smoothed, (2, 0, 1)).reshape(NLAT * CH, NLON).astype(jnp.float32)
    gradient = jnp.dot(lines, lon_filter.astype(jnp.float32).T)
    return gradient.reshape(NLAT, CH, NLON)
```

```python
import functools

import jax
import jax.numpy as jnp
from jax import lax
from jax.experimental import pallas as pl
from jax.experimental.pallas import tpu as pltpu
from jax.sharding import PartitionSpec as P

RATIO = 3
BOXX = 256
BOXY = 32
LANES = 128
SUB = 8
BAND = 128
GROUP = 32
F32 = jnp.float32
BF16 = jnp.bfloat16
NT = (((1,), (1,)), ((), ()))
HIGHEST = lax.Precision.HIGHEST


def lanes_of(shape):
    return lax.broadcasted_iota(jnp.int32, shape, len(shape) - 1)


def sublanes_of(shape):
    return lax.broadcasted_iota(jnp.int32, shape, len(shape) - 2)


def split(value):
    return [value[:, k * LANES : (k + 1) * LANES] for k in range(value.shape[1] // LANES)]


def rows_at(start):
    return pl.ds(pl.multiple_of(start, SUB), SUB)


def x_fluxes(mu, coef, damp, east):
    flux = coef * damp * mu
    part = east * flux
    return part, flux - part


def stencil(mu, px, qx, up_x, down_x, coef, damp, north, halo_up, halo_down):
    flux = coef * damp * mu
    py = north * flux
    qy = flux - py
    base = mu - px + qx - py + qy + up_x - down_x
    lane = lanes_of((SUB, LANES))
    last, first = lane == LANES - 1, lane == 0
    py, qy, base = split(py), split(qy), split(base)
    rolled_up = [pltpu.roll(v, LANES - 1, 1) for v in py]
    rolled_down = [pltpu.roll(v, 1, 1) for v in qy]
    count = len(base)
    out = []
    for k in range(count):
        above = rolled_up[k + 1] if k + 1 < count else halo_up
        below = rolled_down[k - 1] if k > 0 else halo_down
        out.append(base[k] + jnp.where(last, above, rolled_up[k]) - jnp.where(first, below, rolled_down[k]))
    return out, py, qy


def shifted(px_here, px_next, qx_prev, qx_here):
    sub = sublanes_of(px_here.shape)
    up = jnp.where(sub == SUB - 1, pltpu.roll(px_next, SUB - 1, 0), pltpu.roll(px_here, SUB - 1, 0))
    down = jnp.where(sub == 0, pltpu.roll(qx_prev, 1, 0), pltpu.roll(qx_here, 1, 0))
    return up, down


def first_step(mu_ref, cour_ref, lim_ref, dir_ref, out_ref, ef_ref, em_ref, ew_ref, xr_ref, xm_ref, xw_ref, damp, east, north, rim):
    level = pl.program_id(0)
    fields, _, rows, width = mu_ref.shape
    tiles = width // LANES
    groups = rows // GROUP
    tall = ef_ref.shape[0]
    lane = lanes_of((SUB, LANES))
    last = lane == LANES - 1
    edge = slice((tiles - 1) * LANES, tiles * LANES)

    @pl.when(level == 0)
    def _():
        for ref in (ef_ref, em_ref, ew_ref, xr_ref):
            ref[...] = jnp.zeros_like(ref)

        def prepare(tile, carry):
            at = rows_at(tile * SUB)
            east[at] = dir_ref[1, 0, at].astype(F32)
            north[at] = dir_ref[1, 1, at].astype(F32)
            side = jnp.where(last, 1 - dir_ref[0, 1, at, edge], dir_ref[0, 1, at, :LANES]).astype(F32)
            for f in range(fields):
                damp[f, at] = 0.5 + 0.5 * lim_ref[1, f, at].astype(F32)
                flag = jnp.where(last, lim_ref[0, f, at, edge], lim_ref[0, f, at, :LANES]).astype(F32)
                rim[f, at] = side * (0.5 + 0.5 * flag)
            return carry

        lax.fori_loop(0, rows // SUB, prepare, 0)

    def group(g, carry):
        base = g * GROUP
        inside = GROUP // SUB
        starts = [jnp.maximum(base - SUB, 0)] + [base + SUB * t for t in range(inside)] + [jnp.minimum(base + GROUP, rows - SUB)]
        keep_low = jnp.where(g > 0, 1.0, 0.0).astype(F32)
        keep_high = jnp.where(g < groups - 1, 1.0, 0.0).astype(F32)
        band = base // tall
        held = [[ref[rows_at(lax.rem(base, tall) + SUB * t)] for t in range(inside)] for ref in (ef_ref, em_ref, ew_ref)]
        for f in range(fields):
            slot = level * fields + f
            turn = lax.rem(2 * slot + 1 + band * 64, LANES)
            mine = (lane // 2) == slot + 32 * band
            mus = [mu_ref[f, 0, rows_at(s)] for s in starts]
            pq = [
                x_fluxes(m, cour_ref[1, 0, 0, rows_at(s)], damp[f, rows_at(s)], east[rows_at(s)])
                for m, s in zip(mus, starts)
            ]
            px = [v[0] for v in pq]
            qx = [v[1] for v in pq]
            qx[0] = qx[0] * keep_low
            px[-1] = px[-1] * keep_high
            for t in range(inside):
                at = rows_at(starts[t + 1])
                up, down = shifted(px[t + 1], px[t + 2], qx[t], qx[t + 1])
                new, py, qy = stencil(
                    mus[t + 1], px[t + 1], qx[t + 1], up, down, cour_ref[1, 1, 0, at], damp[f, at], north[at],
                    jnp.zeros((SUB, LANES), F32), jnp.zeros((SUB, LANES), F32),
                )
                for k in range(tiles):
                    out_ref[f, 0, at, k * LANES : (k + 1) * LANES] = new[k]
                weight = jnp.where(last, cour_ref[0, 1, 0, at, edge], cour_ref[0, 1, 0, at, :LANES]) * rim[f, at]
                for which, value in enumerate((jnp.where(last, qy[-1], py[0]), jnp.where(last, new[-1], new[0]), weight)):
                    held[which][t] = jnp.where(mine, pltpu.roll(value, turn, 1), held[which][t])
        for which, ref in enumerate((ef_ref, em_ref, ew_ref)):
            for t in range(inside):
                ref[rows_at(lax.rem(base, tall) + SUB * t)] = held[which][t]
        return carry

    lax.fori_loop(0, groups, group, 0)

    low, high = slice(0, SUB), slice(rows - SUB, rows)
    for f in range(fields):
        slot = level * fields + f
        turn = 2 * slot + 1
        mine = (lane // 2) == slot
        px, _ = x_fluxes(mu_ref[f, 0, low], cour_ref[1, 0, 0, low], damp[f, low], east[low])
        _, qx = x_fluxes(mu_ref[f, 0, high], cour_ref[1, 0, 0, high], damp[f, high], east[high])
        xr_ref[level, f : f + 1] = px[:1]
        xr_ref[level, fields + f : fields + f + 1] = qx[SUB - 1 :]
        px_edge = pltpu.roll(jnp.where(last, px[:, edge], px[:, :LANES]), turn, 1)
        qx_edge = pltpu.roll(jnp.where(last, qx[:, edge], qx[:, :LANES]), turn, 1)
        corner = xr_ref.shape[0] - 1
        xr_ref[corner, 0:1, :LANES] = jnp.where(mine, px_edge, jnp.broadcast_to(xr_ref[corner, 0:1, :LANES], (SUB, LANES)))[:1]
        xr_ref[corner, 4:5, :LANES] = jnp.where(mine, qx_edge, jnp.broadcast_to(xr_ref[corner, 4:5, :LANES], (SUB, LANES)))[SUB - 1 :]
        xm_ref[level, f : f + 1] = out_ref[f, 0, low][:1]
        xm_ref[level, fields + f : fields + f + 1] = out_ref[f, 0, high][SUB - 1 :]
        for at, part, row in ((low, 0, 0), (high, 1, SUB - 1)):
            way = dir_ref[0, 0, at].astype(F32)
            way = 1.0 - way if part else way
            value = way * (0.5 + 0.5 * lim_ref[0, f, at].astype(F32)) * cour_ref[0, 0, 0, at]
            xw_ref[level, part * fields + f : part * fields + f + 1] = value[row : row + 1]


def pick(first, a, b):
    return jnp.where(first, a, b)


def rims(rows, parts, ids, efa_ref, efb_ref, xra_ref, xrb_ref, em_ref, ew_ref, xm_ref, xw_ref, eof_ref, e2_ref, x2_ref, m1_ref, x1_ref, kh_ref, kl_ref):
    me_row = ids[0]
    even_row, even_col = ids[2] == 0, ids[3] == 0
    levels, twice, width = xm_ref.shape
    fields = twice // 2
    tiles = width // LANES
    tall = em_ref.shape[0]
    top_band = (rows - 1) // tall
    lane = lanes_of((tall, LANES))
    sub = sublanes_of((tall, LANES))
    up = pick(even_row, efa_ref[...], efb_ref[...])
    down = pick(even_row, efb_ref[...], efa_ref[...])
    merged = jnp.where(lane % 2 == 1, up, -pltpu.roll(down, 2, 1))
    m1_ref[...] = merged
    fixed = em_ref[...] + jnp.where(lane % 2 == 0, pltpu.roll(up, LANES - 1, 1), -pltpu.roll(down, 1, 1))
    corner = xra_ref.shape[0] - 1
    ca, cb = xra_ref[corner, :, :LANES], xrb_ref[corner, :, :LANES]
    corner_up = pick(even_col, ca, cb)[0:1]
    corner_down = pick(even_col, cb, ca)[4:5]
    if top_band:
        corner_up = pltpu.roll(jnp.broadcast_to(corner_up, (SUB, LANES)), 64 * top_band, 1)[:1]
    fixed = fixed + jnp.where(sub == tall - 1, corner_up, 0.0) - jnp.where(sub == 0, corner_down, 0.0)
    e2_ref[...] = ew_ref[...] * fixed

    lane8 = lanes_of((twice, LANES))
    sub8 = sublanes_of((twice, LANES))
    ends = jnp.where(sub8 < fields, jnp.broadcast_to(merged[0:1], (twice, LANES)), jnp.broadcast_to(merged[tall - 1 :], (twice, LANES)))
    wide = sublanes_of((twice, width))
    for level in range(levels):
        a, b = xra_ref[level], xrb_ref[level]
        halo = jnp.where(wide < fields, pick(even_col, a, b), -pick(even_col, b, a))
        x1_ref[level] = halo
        target = 2 * (level * fields + sub8 % fields) + 1 + jnp.where(sub8 >= fields, 64 * top_band, 0)
        at_last = jnp.sum(jnp.where(lane8 == target, ends, 0.0), axis=1, keepdims=True)
        at_first = jnp.sum(jnp.where(lane8 == (target + 1) % LANES, ends, 0.0), axis=1, keepdims=True)
        here = split(xm_ref[level] + pltpu.roll(halo, fields, 0))
        here[-1] = here[-1] + jnp.where(lane8 == LANES - 1, at_last, 0.0)
        here[0] = here[0] + jnp.where(lane8 == 0, at_first, 0.0)
        for k in range(tiles):
            at = slice(k * LANES, (k + 1) * LANES)
            x2_ref[level, :, at] = xw_ref[level, :, at] * here[k]

    channels = eof_ref.shape[0]
    size = kh_ref.shape[0]
    share = channels // parts
    i = lax.broadcasted_iota(jnp.int32, (size, channels), 0) // SUB
    chosen = ((i // share) ^ me_row) * share + i % share
    left = (lax.broadcasted_iota(jnp.int32, (size, channels), 1) == chosen).astype(F32)
    j = lax.broadcasted_iota(jnp.int32, (channels, size), 1) // SUB
    right = (lax.broadcasted_iota(jnp.int32, (channels, size), 0) == j).astype(F32)
    mixed = jnp.dot(left, eof_ref[...], precision=HIGHEST, preferred_element_type=F32)
    spread = jnp.dot(mixed, right, precision=HIGHEST, preferred_element_type=F32)
    same = (lax.broadcasted_iota(jnp.int32, (size, size), 0) - lax.broadcasted_iota(jnp.int32, (size, size), 1)) % SUB == 0
    spread = jnp.where(same, spread, 0.0)
    high = spread.astype(BF16)
    kh_ref[...] = high
    kl_ref[...] = (spread - high.astype(F32)).astype(BF16)


def second_step(
    band, parts, ids, mu_ref, mu_low, mu_high, cour_ref, cx_low, cx_high, lim_ref, lim_low, lim_high, dir_ref, dir_low, dir_high,
    m1_ref, x1_ref, e2a_ref, e2b_ref, x2a_ref, x2b_ref, box_ref, kh_ref, kl_ref, *rest,
):
    outs, (damp, east, north, m2_ref, mixed) = rest[:-5], rest[-5:]
    g = pl.program_id(0)
    fields, levels, _, width = mu_ref.shape
    rows = ids[5]
    tall = m1_ref.shape[0]
    even_row, even_col = ids[2] == 0, ids[3] == 0
    tiles = width // LANES
    inside = GROUP // SUB
    lane = lanes_of((SUB, LANES))
    sub = sublanes_of((SUB, width))
    last, first = lane == LANES - 1, lane == 0

    @pl.when(g == 0)
    def _():
        wide = lanes_of((tall, LANES))
        up = pick(even_row, e2a_ref[...], e2b_ref[...])
        down = pick(even_row, e2b_ref[...], e2a_ref[...])
        m2_ref[...] = jnp.where(wide % 2 == 1, up, -pltpu.roll(down, 2, 1))

    lims = [(lim_low, 0)] + [(lim_ref, SUB * t) for t in range(inside)] + [(lim_high, 0)]
    dirs = [(dir_low, 0)] + [(dir_ref, SUB * t) for t in range(inside)] + [(dir_high, 0)]
    mus = [(mu_low, 0)] + [(mu_ref, SUB * t) for t in range(inside)] + [(mu_high, 0)]
    cxs = [(cx_low, 0)] + [(cour_ref, SUB * t) for t in range(inside)] + [(cx_high, 0)]
    for t in range(inside + 2):
        put = slice(SUB * t, SUB * (t + 1))
        ref, r = dirs[t]
        east[put] = ref[0, 0, r : r + SUB].astype(F32)
        if 0 < t <= inside:
            north[SUB * (t - 1) : SUB * t] = ref[0, 1, r : r + SUB].astype(F32)
        ref, r = lims[t]
        for f in range(fields):
            damp[f, put] = 0.5 + 0.5 * ref[0, f, r : r + SUB].astype(F32)

    base = band * tall + g * GROUP
    starts = [jnp.maximum(base - SUB, 0)] + [base + SUB * t for t in range(inside)] + [jnp.minimum(base + GROUP, rows - SUB)]
    bands = [s // tall for s in starts]
    places = [lax.rem(s, tall) for s in starts]
    at_start = base == 0
    at_end = base + GROUP == rows
    lat_at = ids[7]
    box_lats = box_ref.shape[1] // (fields * levels * parts)
    away = (lane - lat_at) & (LANES - 1)
    piece = away // box_lats
    total = parts * box_lats
    span = fields * levels * box_lats // LANES
    inner = [((lane + LANES * k - lat_at) >= 0) & ((lane + LANES * k - lat_at) < total) for k in range(tiles)]

    def channel_group(level, carry):
        for f in range(fields):
            slot = level * fields + f
            vals, px, qx = [], [], []
            for t in range(inside + 2):
                ref, r = mus[t]
                value = ref[f, level, r : r + SUB]
                fix = pltpu.roll(m1_ref[rows_at(places[t])], (126 - 2 * slot - 64 * bands[t]) & (LANES - 1), 1)
                pieces = split(value)
                pieces[-1] = pieces[-1] + jnp.where(last, fix, 0.0)
                pieces[0] = pieces[0] + jnp.where(first, fix, 0.0)
                value = jnp.concatenate(pieces, axis=1)
                if t == 1:
                    value = value + jnp.where((sub == 0) & at_start, x1_ref[level, fields + f : fields + f + 1], 0.0)
                if t == inside:
                    value = value + jnp.where((sub == SUB - 1) & at_end, x1_ref[level, f : f + 1], 0.0)
                ref, r = cxs[t]
                p, q = x_fluxes(value, ref[0, 0, level, r : r + SUB], damp[f, SUB * t : SUB * (t + 1)], east[SUB * t : SUB * (t + 1)])
                vals.append(value)
                px.append(p)
                qx.append(q)
            halo_low = pick(even_col, x2b_ref[level, fields + f : fields + f + 1], x2a_ref[level, fields + f : fields + f + 1])
            halo_high = pick(even_col, x2a_ref[level, f : f + 1], x2b_ref[level, f : f + 1])
            qx[0] = jnp.where(at_start, jnp.broadcast_to(halo_low, (SUB, width)), qx[0])
            px[-1] = jnp.where(at_end, jnp.broadcast_to(halo_high, (SUB, width)), px[-1])
            for t in range(inside):
                here = slice(SUB * (t + 1), SUB * (t + 2))
                mine = slice(SUB * t, SUB * (t + 1))
                up, down = shifted(px[t + 1], px[t + 2], qx[t], qx[t + 1])
                halo = pltpu.roll(m2_ref[rows_at(places[t + 1])], (126 - 2 * slot - 64 * bands[t + 1]) & (LANES - 1), 1)
                new, _, _ = stencil(
                    vals[t + 1], px[t + 1], qx[t + 1], up, down, cour_ref[0, 1, level, mine], damp[f, here], north[mine], halo, -halo
                )
                gathered = jnp.zeros((SUB, LANES), F32)
                for r in range(parts):
                    block = r * span + f * levels * box_lats // LANES
                    begin = (f * levels * box_lats) % LANES + level * box_lats
                    source = box_ref[mine, block * LANES : (block + 1) * LANES]
                    moved = pltpu.roll(source, (lat_at + box_lats * r - begin) & (LANES - 1), 1)
                    gathered = jnp.where(piece == r, moved, gathered)
                put = rows_at((f * levels + level) * SUB)
                for k in range(tiles):
                    mixed[t, put, k * LANES : (k + 1) * LANES] = new[k] + jnp.where(inner[k], gathered, 0.0)
        return carry

    lax.fori_loop(0, levels, channel_group, 0)

    channels = fields * levels
    share = channels // parts
    per = len(outs) // parts
    depth = share // per
    for v in range(inside // 2):
        both = []
        for t in (2 * v, 2 * v + 1):
            full = mixed[t]
            high = full.astype(BF16)
            low = (full - high.astype(F32)).astype(BF16)
            result = jnp.dot(kh_ref[...], high, preferred_element_type=F32)
            result += jnp.dot(kl_ref[...], high, preferred_element_type=F32)
            result += jnp.dot(kh_ref[...], low, preferred_element_type=F32)
            both.append(result)
        for c in range(channels):
            at = slice(c * SUB, (c + 1) * SUB)
            pair = jnp.concatenate([both[0][at], both[1][at]], axis=0).astype(BF16)
            outs[(c // share) * per + (c % share) // depth][c % depth, 2 * SUB * v : 2 * SUB * (v + 1)] = pair


def coarse_sums(ids, nest_ref, out_ref, held):
    channels, fine_lat, fine_lon = nest_ref.shape
    lon = ids[1] * fine_lon + lax.broadcasted_iota(jnp.int32, (fine_lat, fine_lon), 1)
    lat = ids[0] * fine_lat + lax.broadcasted_iota(jnp.int32, (fine_lat, fine_lon), 0)
    edge = (lon < RATIO) | (lon >= RATIO * BOXX - RATIO) | (lat < RATIO) | (lat >= RATIO * BOXY - RATIO)
    weight = jnp.where(edge, 1.0, 1.0 / (RATIO * RATIO)).astype(F32)
    for c in range(channels):
        held[c * fine_lat : (c + 1) * fine_lat] = nest_ref[c] * weight
    count = channels * fine_lat // RATIO
    sums = held[pl.ds(0, count, stride=RATIO)]
    for a in range(1, RATIO):
        sums = sums + held[pl.ds(a, count, stride=RATIO)]
    shape = (fine_lon // RATIO, fine_lon)
    select = (lax.broadcasted_iota(jnp.int32, shape, 1) // RATIO == lax.broadcasted_iota(jnp.int32, shape, 0)).astype(F32)
    out_ref[...] = lax.dot_general(select, sums, NT, precision=HIGHEST, preferred_element_type=F32)


def arrange(masks, ids, near_ref, far_ref, out_ref, box):
    half, slab, wide = near_ref.shape
    rows = out_ref.shape[0]
    for p, (row_mask, col_mask) in enumerate(masks):
        at = pl.multiple_of((ids[1] ^ col_mask) * slab, SUB)
        to = pl.multiple_of((ids[0] ^ row_mask) * wide, LANES)
        box[pl.ds(at, slab), pl.ds(to, wide)] = near_ref[p] if p < half else far_ref[p - half]
    height = box.shape[0]
    away = ids[6]
    row = lax.broadcasted_iota(jnp.int32, (rows, LANES), 0) - away
    inside = (row >= 0) & (row < height)
    turn = lax.rem(lax.rem(away, height) + height, height)
    for k in range(box.shape[1] // LANES):
        at = slice(k * LANES, (k + 1) * LANES)
        out_ref[:, at] = jnp.where(inside, pltpu.roll(box[:, at], turn, 0)[:rows], 0.0)


def lat_filter_part(start, height, count, parts, cols, ids, *refs):
    pieces, filt, outs = refs[:parts], refs[parts], refs[parts + 1 :]
    lat_block = pieces[0].shape[2]
    lon = pieces[0].shape[1]
    lat_part = filt.shape[0] // cols
    step = 2
    for p in range(count // step):
        right = [ref[step * p : step * (p + 1)].reshape(step * lon, lat_block) for ref in pieces]
        for s0 in range(0, cols, 4):
            acc = None
            for r in range(parts):
                at = pl.ds(pl.multiple_of((ids[0] ^ r) * lat_block, LANES), lat_block)
                left = jnp.concatenate(
                    [
                        filt[pl.ds(pl.multiple_of((ids[1] ^ s) * lat_part + start, 16), height), at]
                        for s in range(s0, min(s0 + 4, cols))
                    ],
                    axis=0,
                )
                term = lax.dot_general(left, right[r], NT, preferred_element_type=F32)
                acc = term if acc is None else acc + term
            for s in range(s0, min(s0 + 4, cols)):
                for c in range(step):
                    value = acc[(s - s0) * height : (s - s0 + 1) * height, c * lon : (c + 1) * lon]
                    outs[s][step * p + c] = value.astype(BF16)


def lon_filter_part(half, height, cols, parts, n_first, aliased, ids, *refs):
    firsts = refs[:n_first]
    lasts = refs[n_first : n_first + cols]
    filters = refs[n_first + cols : n_first + cols + 2 * parts]
    rest = refs[n_first + cols + 2 * parts + (1 if aliased else 0) :]
    out, lines, buffer, stage, in_sem, out_sem = rest
    channels, _, lon = lasts[0].shape
    wide = lines.shape[1] // cols
    rows = channels * height
    block = filters[0].shape[0]
    steps = 2 * parts
    strips = block // LANES

    def fetch(j):
        return pltpu.make_async_copy(filters[j], buffer.at[j % 2], in_sem.at[j % 2])

    def owner(j):
        row = ids[0] ^ (j // 2)
        return row * 2 + (ids[8] if j % 2 == 0 else 1 - ids[8])

    def flush(j, k):
        at = pl.ds(pl.multiple_of(owner(j) * block + k * LANES, LANES), LANES)
        return pltpu.make_async_copy(stage.at[j % 2, k], out.at[pl.ds(half * rows, rows), at], out_sem.at[j % 2, k])

    fetch(0).start()
    for s in range(cols):
        base = pl.multiple_of((ids[1] ^ s) * wide, LANES)
        for c in range(channels):
            put = slice(c * height, (c + 1) * height)
            for b in range(wide // lon - 1):
                groups = n_first // cols // (wide // lon - 1)
                each = channels // groups
                ref = firsts[(b * groups + c // each) * cols + s]
                lines[put, pl.ds(base + b * lon, lon)] = ref[c % each, half * height : (half + 1) * height]
            lines[put, pl.ds(base + wide - lon, lon)] = lasts[s][c]
    for j in range(steps):
        if j + 1 < steps:
            fetch(j + 1).start()
        fetch(j).wait()
        if j >= 2:
            for k in range(strips):
                flush(j - 2, k).wait()
        acc = lax.dot_general(lines[...], buffer[j % 2], NT, preferred_element_type=F32)
        for c in range(channels):
            for k in range(strips):
                at = slice(k * LANES, (k + 1) * LANES)
                stage[j % 2, k, pl.ds(c, height, stride=channels), :] = acc[c * height : (c + 1) * height, at]
        for k in range(strips):
            flush(j, k).start()
    for j in (steps - 2, steps - 1):
        for k in range(strips):
            flush(j, k).wait()


def swap(value, axis, mask):
    count = lax.axis_size(axis)
    return lax.ppermute(value, axis, [(i, i ^ mask) for i in range(count)])


def neighbours(value, axis, parity):
    count = lax.axis_size(axis)
    pairs = []
    for i in range(parity, count - 1, 2):
        pairs += [(i, i + 1), (i + 1, i)]
    return lax.ppermute(value, axis, pairs)


def shape_of(shape, dtype=F32):
    return jax.ShapeDtypeStruct(shape, dtype)


def whole(shape):
    return pl.BlockSpec(shape, lambda *_: (0,) * len(shape))


VMEM_SPEC = pl.BlockSpec(memory_space=pltpu.VMEM)
SMEM_SPEC = pl.BlockSpec(memory_space=pltpu.SMEM)
ANY_SPEC = pl.BlockSpec(memory_space=pl.ANY)


def shards(final_sens, courant, limiter, directions, nest_sens, box_lon, box_lat, eof, lat_filter, lon_filter):
    channels, lon_block, lat_block = final_sens.shape
    fields, levels = limiter.shape[1], courant.shape[2]
    rows_count, cols_count = lax.axis_size("row"), lax.axis_size("col")
    me_row, me_col = lax.axis_index("row"), lax.axis_index("col")
    ids = jnp.stack(
        [
            me_row,
            me_col,
            me_row % 2,
            me_col % 2,
            me_row * 0,
            me_row * 0 + lon_block,
            box_lon[0] - me_col * lon_block,
            box_lat[0] - me_row * lat_block,
            me_col % 2,
        ]
    ).astype(jnp.int32)
    lat_part = lat_filter.shape[0] // cols_count
    share = channels // rows_count
    tall = min(BAND, lon_block)
    n_bands = lon_block // tall

    nest = jnp.transpose(nest_sens, (0, 2, 1))
    fine_lat, fine_lon = nest.shape[1:]
    coarse = pl.pallas_call(
        coarse_sums,
        out_shape=shape_of((fine_lon // RATIO, channels * fine_lat // RATIO)),
        in_specs=[SMEM_SPEC, VMEM_SPEC],
        out_specs=VMEM_SPEC,
        scratch_shapes=[pltpu.VMEM((channels * fine_lat, fine_lon), F32)],
        name="coarse",
    )(ids, nest)
    masks = [(0, 0)]
    stages = [("col", m) for m in (2**k for k in range(1, 10)) if m < cols_count]
    stages += [("row", m) for m in (2**k for k in range(10)) if m < rows_count]
    stages += [("col", 1)]

    def spread(held, count, last=False):
        nonlocal stages, masks
        for axis, mask in stages[:count]:
            other = swap(held, axis, mask)
            held = (held, other) if last else jnp.concatenate([held, other], axis=0)
            masks = masks + [(r ^ mask, c) if axis == "row" else (r, c ^ mask) for r, c in masks]
        stages = stages[count:]
        return held

    def after(value, *others):
        return lax.optimization_barrier((value, *others))[0]

    held = spread(coarse[None], 1)

    mu = final_sens.reshape(fields, levels, lon_block, lat_block)
    mu1, ef, em, ew, xr, xm, xw = pl.pallas_call(
        first_step,
        grid=(levels,),
        out_shape=(
            shape_of(mu.shape),
            shape_of((tall, LANES)),
            shape_of((tall, LANES)),
            shape_of((tall, LANES)),
            shape_of((levels + 1, 2 * fields, lat_block)),
            shape_of((levels, 2 * fields, lat_block)),
            shape_of((levels, 2 * fields, lat_block)),
        ),
        in_specs=[
            pl.BlockSpec((fields, 1, lon_block, lat_block), lambda l: (0, l, 0, 0)),
            pl.BlockSpec((2, 2, 1, lon_block, lat_block), lambda l: (0, 0, l, 0, 0)),
            whole(limiter.shape),
            whole(directions.shape),
        ],
        out_specs=(
            pl.BlockSpec((fields, 1, lon_block, lat_block), lambda l: (0, l, 0, 0)),
            whole((tall, LANES)),
            whole((tall, LANES)),
            whole((tall, LANES)),
            whole((levels + 1, 2 * fields, lat_block)),
            whole((levels, 2 * fields, lat_block)),
            whole((levels, 2 * fields, lat_block)),
        ),
        scratch_shapes=[
            pltpu.VMEM((fields, lon_block, lat_block), F32),
            pltpu.VMEM((lon_block, lat_block), F32),
            pltpu.VMEM((lon_block, lat_block), F32),
            pltpu.VMEM((fields, lon_block, LANES), F32),
        ],
        name="first_step",
    )(mu, courant, limiter, directions)
    held = spread(after(held, ef), 1)
    efa, efb = neighbours(ef, "row", 0), neighbours(ef, "row", 1)
    xra, xrb = neighbours(xr, "col", 0), neighbours(xr, "col", 1)
    held = spread(after(held, efb, xrb), 1)
    size = channels * SUB
    e2, x2, m1, x1, kh, kl = pl.pallas_call(
        functools.partial(rims, lon_block, rows_count),
        out_shape=(
            shape_of(ef.shape),
            shape_of(xm.shape),
            shape_of(ef.shape),
            shape_of(xm.shape),
            shape_of((size, size), BF16),
            shape_of((size, size), BF16),
        ),
        in_specs=[SMEM_SPEC] + [VMEM_SPEC] * 9,
        out_specs=(VMEM_SPEC,) * 6,
        name="rims",
    )(ids, efa, efb, xra, xrb, em, ew, xm, xw, eof)
    e2a, e2b = neighbours(e2, "row", 0), neighbours(e2, "row", 1)
    x2a, x2b = neighbours(x2, "col", 0), neighbours(x2, "col", 1)
    held = spread(after(held, e2), len(stages) - 1)
    held = spread(held, 1, True)
    box = pl.pallas_call(
        functools.partial(arrange, masks),
        out_shape=shape_of((lon_block, rows_count * coarse.shape[1])),
        in_specs=[SMEM_SPEC, VMEM_SPEC, VMEM_SPEC],
        out_specs=VMEM_SPEC,
        scratch_shapes=[pltpu.VMEM((cols_count * coarse.shape[0], rows_count * coarse.shape[1]), F32)],
        name="arrange",
    )(ids, *held)

    groups = tall // GROUP
    fine = GROUP // SUB
    top = lon_block // SUB - 1

    def control(band, halves):
        def at(g):
            return band * groups + g

        def low(g):
            return jnp.maximum((band * groups + g) * fine - 1, 0)

        def high(g):
            return jnp.minimum((band * groups + g) * fine + fine, top)

        depth = share // halves
        return pl.pallas_call(
            functools.partial(second_step, band, rows_count),
            grid=(groups,),
            out_shape=(shape_of((depth, tall, lat_block), BF16),) * (rows_count * halves),
            in_specs=[
                SMEM_SPEC,
                pl.BlockSpec((fields, levels, GROUP, lat_block), lambda g: (0, 0, at(g), 0)),
                pl.BlockSpec((fields, levels, SUB, lat_block), lambda g: (0, 0, low(g), 0)),
                pl.BlockSpec((fields, levels, SUB, lat_block), lambda g: (0, 0, high(g), 0)),
                pl.BlockSpec((1, 2, levels, GROUP, lat_block), lambda g: (0, 0, 0, at(g), 0)),
                pl.BlockSpec((1, 1, levels, SUB, lat_block), lambda g: (0, 0, 0, low(g), 0)),
                pl.BlockSpec((1, 1, levels, SUB, lat_block), lambda g: (0, 0, 0, high(g), 0)),
                pl.BlockSpec((1, fields, GROUP, lat_block), lambda g: (0, 0, at(g), 0)),
                pl.BlockSpec((1, fields, SUB, lat_block), lambda g: (0, 0, low(g), 0)),
                pl.BlockSpec((1, fields, SUB, lat_block), lambda g: (0, 0, high(g), 0)),
                pl.BlockSpec((1, 2, GROUP, lat_block), lambda g: (0, 0, at(g), 0)),
                pl.BlockSpec((1, 1, SUB, lat_block), lambda g: (0, 0, low(g), 0)),
                pl.BlockSpec((1, 1, SUB, lat_block), lambda g: (0, 0, high(g), 0)),
                whole(m1.shape),
                whole(x1.shape),
                whole(e2.shape),
                whole(e2.shape),
                whole(x2.shape),
                whole(x2.shape),
                pl.BlockSpec((GROUP, box.shape[1]), lambda g: (at(g), 0)),
                whole(kh.shape),
                whole(kl.shape),
            ],
            out_specs=(pl.BlockSpec((depth, GROUP, lat_block), lambda g: (0, g, 0)),) * (rows_count * halves),
            scratch_shapes=[
                pltpu.VMEM((fields, GROUP + 2 * SUB, lat_block), F32),
                pltpu.VMEM((GROUP + 2 * SUB, lat_block), F32),
                pltpu.VMEM((GROUP, lat_block), F32),
                pltpu.VMEM((tall, LANES), F32),
                pltpu.VMEM((fine, channels * SUB, lat_block), F32),
            ],
            name="second_step",
        )(ids, mu1, mu1, mu1, courant, courant, courant, limiter, limiter, limiter, directions, directions, directions,
          m1, x1, e2a, e2b, x2a, x2b, box, kh, kl)

    def to_rows(pieces):
        return [pieces[0]] + [swap(pieces[s], "row", s) for s in range(1, rows_count)]

    def smooth(pieces, start, height):
        count = pieces[0].shape[0]
        outs = pl.pallas_call(
            functools.partial(lat_filter_part, start, height, count, rows_count, cols_count),
            out_shape=(shape_of((count, height, tall), BF16),) * cols_count,
            in_specs=[SMEM_SPEC] + [VMEM_SPEC] * (rows_count + 1),
            out_specs=(VMEM_SPEC,) * cols_count,
            name="lat_filter",
        )(ids, *pieces, lat_filter)
        order = list(range(1, cols_count))[::-1]
        moved = {s: swap(outs[s], "col", s) for s in order}
        return [outs[0]] + [moved[s] for s in range(1, cols_count)], outs[-1]

    firsts = []
    sent = []
    for band in range(n_bands):
        final = band == n_bands - 1
        halves = 1 if final else 2
        outs = control(band, halves)
        order = outs[-1]
        for h in range(halves):
            sent.append(to_rows([outs[s * halves + h] for s in range(rows_count)]))

    height = lon_filter.shape[0] // 2
    own = lax.dynamic_slice_in_dim(lon_filter, (me_col % 2) * height, height, 0)
    own = after(own, order)
    gathered = [own] + [swap(own, "row", s) for s in range(1, rows_count)]

    token = None
    for pieces in sent[:-1]:
        moved, token = smooth(pieces, 0, lat_part)
        firsts += moved
    half_height = lat_part // 2
    lasts = []
    for h in range(2):
        moved, token = smooth(sent[-1], h * half_height, half_height)
        lasts.append(moved)
    filters = []
    for piece in gathered:
        filters += [piece, swap(after(piece, token), "col", 1)]

    n_lon = cols_count * lon_block
    rows = share * half_height
    if lon_block % LANES:
        stacked = jnp.stack([jnp.concatenate([lasts[0][s], lasts[1][s]], axis=1) for s in range(cols_count)])
        lines = jnp.take(stacked, me_col ^ jnp.arange(cols_count), axis=0)
        lines = jnp.transpose(lines, (2, 1, 0, 3)).reshape(lat_part, share, n_lon)
        whole_filter = jnp.stack(filters).reshape(rows_count, 2, height, n_lon)
        whole_filter = jnp.take(whole_filter, me_row ^ jnp.arange(rows_count), axis=0)
        whole_filter = jnp.take(whole_filter, me_col % 2 ^ jnp.arange(2), axis=1).reshape(n_lon, n_lon)
        return jnp.einsum("lci,oi->lco", lines, whole_filter, preferred_element_type=F32)
    out = None
    for h in range(2):
        aliased = out is not None
        operands = (ids, *firsts, *lasts[h], *filters) + ((out,) if aliased else ())
        out = pl.pallas_call(
            functools.partial(lon_filter_part, h, half_height, cols_count, rows_count, len(firsts), aliased),
            out_shape=shape_of((2 * rows, n_lon)),
            in_specs=[SMEM_SPEC] + [VMEM_SPEC] * (len(firsts) + cols_count) + [ANY_SPEC] * (2 * rows_count + aliased),
            out_specs=ANY_SPEC,
            scratch_shapes=[
                pltpu.VMEM((rows, n_lon), BF16),
                pltpu.VMEM((2, height, n_lon), BF16),
                pltpu.VMEM((2, height // LANES, rows, LANES), F32),
                pltpu.SemaphoreType.DMA((2,)),
                pltpu.SemaphoreType.DMA((2, height // LANES)),
            ],
            input_output_aliases={len(operands) - 1: 0} if aliased else {},
            name="lon_filter",
        )(*operands)
    return out.reshape(lat_part, share, n_lon)


def solution(mesh):
    placed = (
        P(None, "col", "row"),
        P(None, None, None, "col", "row"),
        P(None, None, "col", "row"),
        P(None, None, "col", "row"),
        P(None, "col", "row"),
        P(),
        P(),
        P(),
        P(),
        P("row", None),
    )
    return jax.shard_map(
        shards, mesh=mesh, in_specs=placed, out_specs=P("col", "row", None), check_vma=False
    )
```

```python
import functools

import jax
import jax.numpy as jnp
from jax import lax
from jax.experimental import pallas as pl
from jax.experimental.pallas import tpu as pltpu
from jax.sharding import PartitionSpec as P


RATIO = 3
BOXX = 256
BOXY = 32
LANES = 128
SUB = 8
BAND = 128
GROUP = 32
F32 = jnp.float32
BF16 = jnp.bfloat16
NT = (((1,), (1,)), ((), ()))
HIGHEST = lax.Precision.HIGHEST


def lanes_of(shape):
    return lax.broadcasted_iota(jnp.int32, shape, len(shape) - 1)


def sublanes_of(shape):
    return lax.broadcasted_iota(jnp.int32, shape, len(shape) - 2)


def split(value):
    return [value[:, k * LANES : (k + 1) * LANES] for k in range(value.shape[1] // LANES)]


def rows_at(start):
    return pl.ds(pl.multiple_of(start, SUB), SUB)


def x_fluxes(mu, coef, damp, east):
    flux = coef * damp * mu
    part = east * flux
    return part, flux - part


def stencil(mu, px, qx, up_x, down_x, coef, damp, north, halo_up, halo_down):
    flux = coef * damp * mu
    py = north * flux
    qy = flux - py
    base = mu - px + qx - py + qy + up_x - down_x
    lane = lanes_of((SUB, LANES))
    last, first = lane == LANES - 1, lane == 0
    py, qy, base = split(py), split(qy), split(base)
    rolled_up = [pltpu.roll(v, LANES - 1, 1) for v in py]
    rolled_down = [pltpu.roll(v, 1, 1) for v in qy]
    count = len(base)
    out = []
    for k in range(count):
        above = rolled_up[k + 1] if k + 1 < count else halo_up
        below = rolled_down[k - 1] if k > 0 else halo_down
        out.append(base[k] + jnp.where(last, above, rolled_up[k]) - jnp.where(first, below, rolled_down[k]))
    return out, py, qy


def shifted(px_here, px_next, qx_prev, qx_here):
    sub = sublanes_of(px_here.shape)
    up = jnp.where(sub == SUB - 1, pltpu.roll(px_next, SUB - 1, 0), pltpu.roll(px_here, SUB - 1, 0))
    down = jnp.where(sub == 0, pltpu.roll(qx_prev, 1, 0), pltpu.roll(qx_here, 1, 0))
    return up, down


def first_step(mu_ref, cour_ref, lim_ref, dir_ref, out_ref, ef_ref, em_ref, ew_ref, xr_ref, xm_ref, xw_ref, damp, east, north, rim):
    level = pl.program_id(0)
    fields, _, rows, width = mu_ref.shape
    tiles = width // LANES
    groups = rows // GROUP
    tall = ef_ref.shape[0]
    lane = lanes_of((SUB, LANES))
    last = lane == LANES - 1
    edge = slice((tiles - 1) * LANES, tiles * LANES)

    @pl.when(level == 0)
    def _():
        for ref in (ef_ref, em_ref, ew_ref, xr_ref):
            ref[...] = jnp.zeros_like(ref)

        def prepare(tile, carry):
            at = rows_at(tile * SUB)
            east[at] = dir_ref[1, 0, at].astype(F32)
            north[at] = dir_ref[1, 1, at].astype(F32)
            side = jnp.where(last, 1 - dir_ref[0, 1, at, edge], dir_ref[0, 1, at, :LANES]).astype(F32)
            for f in range(fields):
                damp[f, at] = 0.5 + 0.5 * lim_ref[1, f, at].astype(F32)
                flag = jnp.where(last, lim_ref[0, f, at, edge], lim_ref[0, f, at, :LANES]).astype(F32)
                rim[f, at] = side * (0.5 + 0.5 * flag)
            return carry

        lax.fori_loop(0, rows // SUB, prepare, 0)

    def group(g, carry):
        base = g * GROUP
        inside = GROUP // SUB
        starts = [jnp.maximum(base - SUB, 0)] + [base + SUB * t for t in range(inside)] + [jnp.minimum(base + GROUP, rows - SUB)]
        keep_low = jnp.where(g > 0, 1.0, 0.0).astype(F32)
        keep_high = jnp.where(g < groups - 1, 1.0, 0.0).astype(F32)
        band = base // tall
        held = [[ref[rows_at(lax.rem(base, tall) + SUB * t)] for t in range(inside)] for ref in (ef_ref, em_ref, ew_ref)]
        for f in range(fields):
            slot = level * fields + f
            turn = lax.rem(2 * slot + 1 + band * 64, LANES)
            mine = (lane // 2) == slot + 32 * band
            mus = [mu_ref[f, 0, rows_at(s)] for s in starts]
            pq = [
                x_fluxes(m, cour_ref[1, 0, 0, rows_at(s)], damp[f, rows_at(s)], east[rows_at(s)])
                for m, s in zip(mus, starts)
            ]
            px = [v[0] for v in pq]
            qx = [v[1] for v in pq]
            qx[0] = qx[0] * keep_low
            px[-1] = px[-1] * keep_high
            for t in range(inside):
                at = rows_at(starts[t + 1])
                up, down = shifted(px[t + 1], px[t + 2], qx[t], qx[t + 1])
                new, py, qy = stencil(
                    mus[t + 1], px[t + 1], qx[t + 1], up, down, cour_ref[1, 1, 0, at], damp[f, at], north[at],
                    jnp.zeros((SUB, LANES), F32), jnp.zeros((SUB, LANES), F32),
                )
                for k in range(tiles):
                    out_ref[f, 0, at, k * LANES : (k + 1) * LANES] = new[k]
                weight = jnp.where(last, cour_ref[0, 1, 0, at, edge], cour_ref[0, 1, 0, at, :LANES]) * rim[f, at]
                for which, value in enumerate((jnp.where(last, qy[-1], py[0]), jnp.where(last, new[-1], new[0]), weight)):
                    held[which][t] = jnp.where(mine, pltpu.roll(value, turn, 1), held[which][t])
        for which, ref in enumerate((ef_ref, em_ref, ew_ref)):
            for t in range(inside):
                ref[rows_at(lax.rem(base, tall) + SUB * t)] = held[which][t]
        return carry

    lax.fori_loop(0, groups, group, 0)

    low, high = slice(0, SUB), slice(rows - SUB, rows)
    for f in range(fields):
        slot = level * fields + f
        turn = 2 * slot + 1
        mine = (lane // 2) == slot
        px, _ = x_fluxes(mu_ref[f, 0, low], cour_ref[1, 0, 0, low], damp[f, low], east[low])
        _, qx = x_fluxes(mu_ref[f, 0, high], cour_ref[1, 0, 0, high], damp[f, high], east[high])
        xr_ref[level, f : f + 1] = px[:1]
        xr_ref[level, fields + f : fields + f + 1] = qx[SUB - 1 :]
        px_edge = pltpu.roll(jnp.where(last, px[:, edge], px[:, :LANES]), turn, 1)
        qx_edge = pltpu.roll(jnp.where(last, qx[:, edge], qx[:, :LANES]), turn, 1)
        corner = xr_ref.shape[0] - 1
        xr_ref[corner, 0:1, :LANES] = jnp.where(mine, px_edge, jnp.broadcast_to(xr_ref[corner, 0:1, :LANES], (SUB, LANES)))[:1]
        xr_ref[corner, 4:5, :LANES] = jnp.where(mine, qx_edge, jnp.broadcast_to(xr_ref[corner, 4:5, :LANES], (SUB, LANES)))[SUB - 1 :]
        xm_ref[level, f : f + 1] = out_ref[f, 0, low][:1]
        xm_ref[level, fields + f : fields + f + 1] = out_ref[f, 0, high][SUB - 1 :]
        for at, part, row in ((low, 0, 0), (high, 1, SUB - 1)):
            way = dir_ref[0, 0, at].astype(F32)
            way = 1.0 - way if part else way
            value = way * (0.5 + 0.5 * lim_ref[0, f, at].astype(F32)) * cour_ref[0, 0, 0, at]
            xw_ref[level, part * fields + f : part * fields + f + 1] = value[row : row + 1]


def pick(first, a, b):
    return jnp.where(first, a, b)


def rims(rows, parts, ids, efa_ref, efb_ref, xra_ref, xrb_ref, em_ref, ew_ref, xm_ref, xw_ref, eof_ref, e2_ref, x2_ref, m1_ref, x1_ref, kh_ref, kl_ref):
    me_row = ids[0]
    even_row, even_col = ids[2] == 0, ids[3] == 0
    levels, twice, width = xm_ref.shape
    fields = twice // 2
    tiles = width // LANES
    tall = em_ref.shape[0]
    top_band = (rows - 1) // tall
    lane = lanes_of((tall, LANES))
    sub = sublanes_of((tall, LANES))
    up = pick(even_row, efa_ref[...], efb_ref[...])
    down = pick(even_row, efb_ref[...], efa_ref[...])
    merged = jnp.where(lane % 2 == 1, up, -pltpu.roll(down, 2, 1))
    m1_ref[...] = merged
    fixed = em_ref[...] + jnp.where(lane % 2 == 0, pltpu.roll(up, LANES - 1, 1), -pltpu.roll(down, 1, 1))
    corner = xra_ref.shape[0] - 1
    ca, cb = xra_ref[corner, :, :LANES], xrb_ref[corner, :, :LANES]
    corner_up = pick(even_col, ca, cb)[0:1]
    corner_down = pick(even_col, cb, ca)[4:5]
    if top_band:
        corner_up = pltpu.roll(jnp.broadcast_to(corner_up, (SUB, LANES)), 64 * top_band, 1)[:1]
    fixed = fixed + jnp.where(sub == tall - 1, corner_up, 0.0) - jnp.where(sub == 0, corner_down, 0.0)
    e2_ref[...] = ew_ref[...] * fixed

    lane8 = lanes_of((twice, LANES))
    sub8 = sublanes_of((twice, LANES))
    ends = jnp.where(sub8 < fields, jnp.broadcast_to(merged[0:1], (twice, LANES)), jnp.broadcast_to(merged[tall - 1 :], (twice, LANES)))
    wide = sublanes_of((twice, width))
    for level in range(levels):
        a, b = xra_ref[level], xrb_ref[level]
        halo = jnp.where(wide < fields, pick(even_col, a, b), -pick(even_col, b, a))
        x1_ref[level] = halo
        target = 2 * (level * fields + sub8 % fields) + 1 + jnp.where(sub8 >= fields, 64 * top_band, 0)
        at_last = jnp.sum(jnp.where(lane8 == target, ends, 0.0), axis=1, keepdims=True)
        at_first = jnp.sum(jnp.where(lane8 == (target + 1) % LANES, ends, 0.0), axis=1, keepdims=True)
        here = split(xm_ref[level] + pltpu.roll(halo, fields, 0))
        here[-1] = here[-1] + jnp.where(lane8 == LANES - 1, at_last, 0.0)
        here[0] = here[0] + jnp.where(lane8 == 0, at_first, 0.0)
        for k in range(tiles):
            at = slice(k * LANES, (k + 1) * LANES)
            x2_ref[level, :, at] = xw_ref[level, :, at] * here[k]

    channels = eof_ref.shape[0]
    size = kh_ref.shape[0]
    share = channels // parts
    i = lax.broadcasted_iota(jnp.int32, (size, channels), 0) // SUB
    chosen = ((i // share) ^ me_row) * share + i % share
    left = (lax.broadcasted_iota(jnp.int32, (size, channels), 1) == chosen).astype(F32)
    j = lax.broadcasted_iota(jnp.int32, (channels, size), 1) // SUB
    right = (lax.broadcasted_iota(jnp.int32, (channels, size), 0) == j).astype(F32)
    mixed = jnp.dot(left, eof_ref[...], precision=HIGHEST, preferred_element_type=F32)
    spread = jnp.dot(mixed, right, precision=HIGHEST, preferred_element_type=F32)
    same = (lax.broadcasted_iota(jnp.int32, (size, size), 0) - lax.broadcasted_iota(jnp.int32, (size, size), 1)) % SUB == 0
    spread = jnp.where(same, spread, 0.0)
    high = spread.astype(BF16)
    kh_ref[...] = high
    kl_ref[...] = (spread - high.astype(F32)).astype(BF16)


def second_step(
    band, parts, ids, mu_ref, mu_low, mu_high, cour_ref, cx_low, cx_high, lim_ref, lim_low, lim_high, dir_ref, dir_low, dir_high,
    m1_ref, x1_ref, e2a_ref, e2b_ref, x2a_ref, x2b_ref, box_ref, kh_ref, kl_ref, *rest,
):
    outs, (damp, east, north, m2_ref, mixed) = rest[:-5], rest[-5:]
    g = pl.program_id(0)
    fields, levels, _, width = mu_ref.shape
    rows = ids[5]
    tall = m1_ref.shape[0]
    even_row, even_col = ids[2] == 0, ids[3] == 0
    tiles = width // LANES
    inside = GROUP // SUB
    lane = lanes_of((SUB, LANES))
    sub = sublanes_of((SUB, width))
    last, first = lane == LANES - 1, lane == 0

    @pl.when(g == 0)
    def _():
        wide = lanes_of((tall, LANES))
        up = pick(even_row, e2a_ref[...], e2b_ref[...])
        down = pick(even_row, e2b_ref[...], e2a_ref[...])
        m2_ref[...] = jnp.where(wide % 2 == 1, up, -pltpu.roll(down, 2, 1))

    lims = [(lim_low, 0)] + [(lim_ref, SUB * t) for t in range(inside)] + [(lim_high, 0)]
    dirs = [(dir_low, 0)] + [(dir_ref, SUB * t) for t in range(inside)] + [(dir_high, 0)]
    mus = [(mu_low, 0)] + [(mu_ref, SUB * t) for t in range(inside)] + [(mu_high, 0)]
    cxs = [(cx_low, 0)] + [(cour_ref, SUB * t) for t in range(inside)] + [(cx_high, 0)]
    for t in range(inside + 2):
        put = slice(SUB * t, SUB * (t + 1))
        ref, r = dirs[t]
        east[put] = ref[0, 0, r : r + SUB].astype(F32)
        if 0 < t <= inside:
            north[SUB * (t - 1) : SUB * t] = ref[0, 1, r : r + SUB].astype(F32)
        ref, r = lims[t]
        for f in range(fields):
            damp[f, put] = 0.5 + 0.5 * ref[0, f, r : r + SUB].astype(F32)

    base = band * tall + g * GROUP
    starts = [jnp.maximum(base - SUB, 0)] + [base + SUB * t for t in range(inside)] + [jnp.minimum(base + GROUP, rows - SUB)]
    bands = [s // tall for s in starts]
    places = [lax.rem(s, tall) for s in starts]
    at_start = base == 0
    at_end = base + GROUP == rows
    lat_at = ids[7]
    box_lats = box_ref.shape[1] // (fields * levels * parts)
    away = (lane - lat_at) & (LANES - 1)
    piece = away // box_lats
    total = parts * box_lats
    span = fields * levels * box_lats // LANES
    inner = [((lane + LANES * k - lat_at) >= 0) & ((lane + LANES * k - lat_at) < total) for k in range(tiles)]

    def channel_group(level, carry):
        for f in range(fields):
            slot = level * fields + f
            vals, px, qx = [], [], []
            for t in range(inside + 2):
                ref, r = mus[t]
                value = ref[f, level, r : r + SUB]
                fix = pltpu.roll(m1_ref[rows_at(places[t])], (126 - 2 * slot - 64 * bands[t]) & (LANES - 1), 1)
                pieces = split(value)
                pieces[-1] = pieces[-1] + jnp.where(last, fix, 0.0)
                pieces[0] = pieces[0] + jnp.where(first, fix, 0.0)
                value = jnp.concatenate(pieces, axis=1)
                if t == 1:
                    value = value + jnp.where((sub == 0) & at_start, x1_ref[level, fields + f : fields + f + 1], 0.0)
                if t == inside:
                    value = value + jnp.where((sub == SUB - 1) & at_end, x1_ref[level, f : f + 1], 0.0)
                ref, r = cxs[t]
                p, q = x_fluxes(value, ref[0, 0, level, r : r + SUB], damp[f, SUB * t : SUB * (t + 1)], east[SUB * t : SUB * (t + 1)])
                vals.append(value)
                px.append(p)
                qx.append(q)
            halo_low = pick(even_col, x2b_ref[level, fields + f : fields + f + 1], x2a_ref[level, fields + f : fields + f + 1])
            halo_high = pick(even_col, x2a_ref[level, f : f + 1], x2b_ref[level, f : f + 1])
            qx[0] = jnp.where(at_start, jnp.broadcast_to(halo_low, (SUB, width)), qx[0])
            px[-1] = jnp.where(at_end, jnp.broadcast_to(halo_high, (SUB, width)), px[-1])
            for t in range(inside):
                here = slice(SUB * (t + 1), SUB * (t + 2))
                mine = slice(SUB * t, SUB * (t + 1))
                up, down = shifted(px[t + 1], px[t + 2], qx[t], qx[t + 1])
                halo = pltpu.roll(m2_ref[rows_at(places[t + 1])], (126 - 2 * slot - 64 * bands[t + 1]) & (LANES - 1), 1)
                new, _, _ = stencil(
                    vals[t + 1], px[t + 1], qx[t + 1], up, down, cour_ref[0, 1, level, mine], damp[f, here], north[mine], halo, -halo
                )
                gathered = jnp.zeros((SUB, LANES), F32)
                for r in range(parts):
                    block = r * span + f * levels * box_lats // LANES
                    begin = (f * levels * box_lats) % LANES + level * box_lats
                    source = box_ref[mine, block * LANES : (block + 1) * LANES]
                    moved = pltpu.roll(source, (lat_at + box_lats * r - begin) & (LANES - 1), 1)
                    gathered = jnp.where(piece == r, moved, gathered)
                put = rows_at((f * levels + level) * SUB)
                for k in range(tiles):
                    mixed[t, put, k * LANES : (k + 1) * LANES] = new[k] + jnp.where(inner[k], gathered, 0.0)
        return carry

    lax.fori_loop(0, levels, channel_group, 0)

    channels = fields * levels
    share = channels // parts
    per = len(outs) // parts
    depth = share // per
    for v in range(inside // 2):
        both = []
        for t in (2 * v, 2 * v + 1):
            full = mixed[t]
            high = full.astype(BF16)
            low = (full - high.astype(F32)).astype(BF16)
            result = jnp.dot(kh_ref[...], high, preferred_element_type=F32)
            result += jnp.dot(kl_ref[...], high, preferred_element_type=F32)
            result += jnp.dot(kh_ref[...], low, preferred_element_type=F32)
            both.append(result)
        for c in range(channels):
            at = slice(c * SUB, (c + 1) * SUB)
            pair = jnp.concatenate([both[0][at], both[1][at]], axis=0).astype(BF16)
            outs[(c // share) * per + (c % share) // depth][c % depth, 2 * SUB * v : 2 * SUB * (v + 1)] = pair


def coarse_sums(ids, nest_ref, out_ref, held):
    channels, fine_lat, fine_lon = nest_ref.shape
    lon = ids[1] * fine_lon + lax.broadcasted_iota(jnp.int32, (fine_lat, fine_lon), 1)
    lat = ids[0] * fine_lat + lax.broadcasted_iota(jnp.int32, (fine_lat, fine_lon), 0)
    edge = (lon < RATIO) | (lon >= RATIO * BOXX - RATIO) | (lat < RATIO) | (lat >= RATIO * BOXY - RATIO)
    weight = jnp.where(edge, 1.0, 1.0 / (RATIO * RATIO)).astype(F32)
    for c in range(channels):
        held[c * fine_lat : (c + 1) * fine_lat] = nest_ref[c] * weight
    count = channels * fine_lat // RATIO
    sums = held[pl.ds(0, count, stride=RATIO)]
    for a in range(1, RATIO):
        sums = sums + held[pl.ds(a, count, stride=RATIO)]
    shape = (fine_lon // RATIO, fine_lon)
    select = (lax.broadcasted_iota(jnp.int32, shape, 1) // RATIO == lax.broadcasted_iota(jnp.int32, shape, 0)).astype(F32)
    out_ref[...] = lax.dot_general(select, sums, NT, precision=HIGHEST, preferred_element_type=F32)


def arrange(masks, ids, near_ref, far_ref, out_ref, box):
    half, slab, wide = near_ref.shape
    rows = out_ref.shape[0]
    for p, (row_mask, col_mask) in enumerate(masks):
        at = pl.multiple_of((ids[1] ^ col_mask) * slab, SUB)
        to = pl.multiple_of((ids[0] ^ row_mask) * wide, LANES)
        box[pl.ds(at, slab), pl.ds(to, wide)] = near_ref[p] if p < half else far_ref[p - half]
    height = box.shape[0]
    away = ids[6]
    row = lax.broadcasted_iota(jnp.int32, (rows, LANES), 0) - away
    inside = (row >= 0) & (row < height)
    turn = lax.rem(lax.rem(away, height) + height, height)
    for k in range(box.shape[1] // LANES):
        at = slice(k * LANES, (k + 1) * LANES)
        out_ref[:, at] = jnp.where(inside, pltpu.roll(box[:, at], turn, 0)[:rows], 0.0)


def lat_filter_part(start, height, count, parts, cols, ids, *refs):
    pieces, filt, outs = refs[:parts], refs[parts], refs[parts + 1 :]
    lat_block = pieces[0].shape[2]
    lon = pieces[0].shape[1]
    lat_part = filt.shape[0] // cols
    step = 2
    for p in range(count // step):
        right = [ref[step * p : step * (p + 1)].reshape(step * lon, lat_block) for ref in pieces]
        for s0 in range(0, cols, 4):
            acc = None
            for r in range(parts):
                at = pl.ds(pl.multiple_of((ids[0] ^ r) * lat_block, LANES), lat_block)
                left = jnp.concatenate(
                    [
                        filt[pl.ds(pl.multiple_of((ids[1] ^ s) * lat_part + start, 16), height), at]
                        for s in range(s0, min(s0 + 4, cols))
                    ],
                    axis=0,
                )
                term = lax.dot_general(left, right[r], NT, preferred_element_type=F32)
                acc = term if acc is None else acc + term
            for s in range(s0, min(s0 + 4, cols)):
                for c in range(step):
                    value = acc[(s - s0) * height : (s - s0 + 1) * height, c * lon : (c + 1) * lon]
                    outs[s][step * p + c] = value.astype(BF16)


def lon_filter_part(half, height, cols, parts, n_first, aliased, ids, *refs):
    firsts = refs[:n_first]
    lasts = refs[n_first : n_first + cols]
    filters = refs[n_first + cols : n_first + cols + 2 * parts]
    rest = refs[n_first + cols + 2 * parts + (1 if aliased else 0) :]
    out, lines, buffer, stage, in_sem, out_sem = rest
    channels, _, lon = lasts[0].shape
    wide = lines.shape[1] // cols
    rows = channels * height
    block = filters[0].shape[0]
    steps = 2 * parts
    strips = block // LANES

    def fetch(j):
        return pltpu.make_async_copy(filters[j], buffer.at[j % 2], in_sem.at[j % 2])

    def owner(j):
        row = ids[0] ^ (j // 2)
        return row * 2 + (ids[8] if j % 2 == 0 else 1 - ids[8])

    def flush(j, k):
        at = pl.ds(pl.multiple_of(owner(j) * block + k * LANES, LANES), LANES)
        return pltpu.make_async_copy(stage.at[j % 2, k], out.at[pl.ds(half * rows, rows), at], out_sem.at[j % 2, k])

    fetch(0).start()
    for s in range(cols):
        base = pl.multiple_of((ids[1] ^ s) * wide, LANES)
        for c in range(channels):
            put = slice(c * height, (c + 1) * height)
            for b in range(wide // lon - 1):
                groups = n_first // cols // (wide // lon - 1)
                each = channels // groups
                ref = firsts[(b * groups + c // each) * cols + s]
                lines[put, pl.ds(base + b * lon, lon)] = ref[c % each, half * height : (half + 1) * height]
            lines[put, pl.ds(base + wide - lon, lon)] = lasts[s][c]
    for j in range(steps):
        if j + 1 < steps:
            fetch(j + 1).start()
        fetch(j).wait()
        if j >= 2:
            for k in range(strips):
                flush(j - 2, k).wait()
        acc = lax.dot_general(lines[...], buffer[j % 2], NT, preferred_element_type=F32)
        for c in range(channels):
            for k in range(strips):
                at = slice(k * LANES, (k + 1) * LANES)
                stage[j % 2, k, pl.ds(c, height, stride=channels), :] = acc[c * height : (c + 1) * height, at]
        for k in range(strips):
            flush(j, k).start()
    for j in (steps - 2, steps - 1):
        for k in range(strips):
            flush(j, k).wait()


def swap(value, axis, mask):
    count = lax.axis_size(axis)
    return lax.ppermute(value, axis, [(i, i ^ mask) for i in range(count)])


def neighbours(value, axis, parity):
    count = lax.axis_size(axis)
    pairs = []
    for i in range(parity, count - 1, 2):
        pairs += [(i, i + 1), (i + 1, i)]
    return lax.ppermute(value, axis, pairs)


def shape_of(shape, dtype=F32):
    return jax.ShapeDtypeStruct(shape, dtype)


def whole(shape):
    return pl.BlockSpec(shape, lambda *_: (0,) * len(shape))


VMEM_SPEC = pl.BlockSpec(memory_space=pltpu.VMEM)
SMEM_SPEC = pl.BlockSpec(memory_space=pltpu.SMEM)
ANY_SPEC = pl.BlockSpec(memory_space=pl.ANY)


def shards(final_sens, courant, limiter, directions, nest_sens, box_lon, box_lat, eof, lat_filter, lon_filter):
    channels, lon_block, lat_block = final_sens.shape
    fields, levels = limiter.shape[1], courant.shape[2]
    rows_count, cols_count = lax.axis_size("row"), lax.axis_size("col")
    me_row, me_col = lax.axis_index("row"), lax.axis_index("col")
    ids = jnp.stack(
        [
            me_row,
            me_col,
            me_row % 2,
            me_col % 2,
            me_row * 0,
            me_row * 0 + lon_block,
            box_lon[0] - me_col * lon_block,
            box_lat[0] - me_row * lat_block,
            me_col % 2,
        ]
    ).astype(jnp.int32)
    lat_part = lat_filter.shape[0] // cols_count
    share = channels // rows_count
    tall = min(BAND, lon_block)
    n_bands = lon_block // tall

    nest = jnp.transpose(nest_sens, (0, 2, 1))
    fine_lat, fine_lon = nest.shape[1:]
    coarse = pl.pallas_call(
        coarse_sums,
        out_shape=shape_of((fine_lon // RATIO, channels * fine_lat // RATIO)),
        in_specs=[SMEM_SPEC, VMEM_SPEC],
        out_specs=VMEM_SPEC,
        scratch_shapes=[pltpu.VMEM((channels * fine_lat, fine_lon), F32)],
        name="coarse",
    )(ids, nest)
    masks = [(0, 0)]
    stages = [("col", m) for m in (2**k for k in range(1, 10)) if m < cols_count]
    stages += [("row", m) for m in (2**k for k in range(10)) if m < rows_count]
    stages += [("col", 1)]

    def spread(held, count, last=False):
        nonlocal stages, masks
        for axis, mask in stages[:count]:
            other = swap(held, axis, mask)
            held = (held, other) if last else jnp.concatenate([held, other], axis=0)
            masks = masks + [(r ^ mask, c) if axis == "row" else (r, c ^ mask) for r, c in masks]
        stages = stages[count:]
        return held

    def after(value, *others):
        return lax.optimization_barrier((value, *others))[0]

    held = spread(coarse[None], 1)

    mu = final_sens.reshape(fields, levels, lon_block, lat_block)
    mu1, ef, em, ew, xr, xm, xw = pl.pallas_call(
        first_step,
        grid=(levels,),
        out_shape=(
            shape_of(mu.shape),
            shape_of((tall, LANES)),
            shape_of((tall, LANES)),
            shape_of((tall, LANES)),
            shape_of((levels + 1, 2 * fields, lat_block)),
            shape_of((levels, 2 * fields, lat_block)),
            shape_of((levels, 2 * fields, lat_block)),
        ),
        in_specs=[
            pl.BlockSpec((fields, 1, lon_block, lat_block), lambda l: (0, l, 0, 0)),
            pl.BlockSpec((2, 2, 1, lon_block, lat_block), lambda l: (0, 0, l, 0, 0)),
            whole(limiter.shape),
            whole(directions.shape),
        ],
        out_specs=(
            pl.BlockSpec((fields, 1, lon_block, lat_block), lambda l: (0, l, 0, 0)),
            whole((tall, LANES)),
            whole((tall, LANES)),
            whole((tall, LANES)),
            whole((levels + 1, 2 * fields, lat_block)),
            whole((levels, 2 * fields, lat_block)),
            whole((levels, 2 * fields, lat_block)),
        ),
        scratch_shapes=[
            pltpu.VMEM((fields, lon_block, lat_block), F32),
            pltpu.VMEM((lon_block, lat_block), F32),
            pltpu.VMEM((lon_block, lat_block), F32),
            pltpu.VMEM((fields, lon_block, LANES), F32),
        ],
        name="first_step",
    )(mu, courant, limiter, directions)
    held = spread(after(held, ef), 1)
    efa, efb = neighbours(ef, "row", 0), neighbours(ef, "row", 1)
    xra, xrb = neighbours(xr, "col", 0), neighbours(xr, "col", 1)
    held = spread(after(held, efb, xrb), 1)
    size = channels * SUB
    e2, x2, m1, x1, kh, kl = pl.pallas_call(
        functools.partial(rims, lon_block, rows_count),
        out_shape=(
            shape_of(ef.shape),
            shape_of(xm.shape),
            shape_of(ef.shape),
            shape_of(xm.shape),
            shape_of((size, size), BF16),
            shape_of((size, size), BF16),
        ),
        in_specs=[SMEM_SPEC] + [VMEM_SPEC] * 9,
        out_specs=(VMEM_SPEC,) * 6,
        name="rims",
    )(ids, efa, efb, xra, xrb, em, ew, xm, xw, eof)
    e2a, e2b = neighbours(e2, "row", 0), neighbours(e2, "row", 1)
    x2a, x2b = neighbours(x2, "col", 0), neighbours(x2, "col", 1)
    held = spread(after(held, e2), len(stages) - 1)
    held = spread(held, 1, True)
    box = pl.pallas_call(
        functools.partial(arrange, masks),
        out_shape=shape_of((lon_block, rows_count * coarse.shape[1])),
        in_specs=[SMEM_SPEC, VMEM_SPEC, VMEM_SPEC],
        out_specs=VMEM_SPEC,
        scratch_shapes=[pltpu.VMEM((cols_count * coarse.shape[0], rows_count * coarse.shape[1]), F32)],
        name="arrange",
    )(ids, *held)

    groups = tall // GROUP
    fine = GROUP // SUB
    top = lon_block // SUB - 1

    def control(band, halves, kl):
        def at(g):
            return band * groups + g

        def low(g):
            return jnp.maximum((band * groups + g) * fine - 1, 0)

        def high(g):
            return jnp.minimum((band * groups + g) * fine + fine, top)

        depth = share // halves
        return pl.pallas_call(
            functools.partial(second_step, band, rows_count),
            grid=(groups,),
            out_shape=(shape_of((depth, tall, lat_block), BF16),) * (rows_count * halves),
            in_specs=[
                SMEM_SPEC,
                pl.BlockSpec((fields, levels, GROUP, lat_block), lambda g: (0, 0, at(g), 0)),
                pl.BlockSpec((fields, levels, SUB, lat_block), lambda g: (0, 0, low(g), 0)),
                pl.BlockSpec((fields, levels, SUB, lat_block), lambda g: (0, 0, high(g), 0)),
                pl.BlockSpec((1, 2, levels, GROUP, lat_block), lambda g: (0, 0, 0, at(g), 0)),
                pl.BlockSpec((1, 1, levels, SUB, lat_block), lambda g: (0, 0, 0, low(g), 0)),
                pl.BlockSpec((1, 1, levels, SUB, lat_block), lambda g: (0, 0, 0, high(g), 0)),
                pl.BlockSpec((1, fields, GROUP, lat_block), lambda g: (0, 0, at(g), 0)),
                pl.BlockSpec((1, fields, SUB, lat_block), lambda g: (0, 0, low(g), 0)),
                pl.BlockSpec((1, fields, SUB, lat_block), lambda g: (0, 0, high(g), 0)),
                pl.BlockSpec((1, 2, GROUP, lat_block), lambda g: (0, 0, at(g), 0)),
                pl.BlockSpec((1, 1, SUB, lat_block), lambda g: (0, 0, low(g), 0)),
                pl.BlockSpec((1, 1, SUB, lat_block), lambda g: (0, 0, high(g), 0)),
                whole(m1.shape),
                whole(x1.shape),
                whole(e2.shape),
                whole(e2.shape),
                whole(x2.shape),
                whole(x2.shape),
                pl.BlockSpec((GROUP, box.shape[1]), lambda g: (at(g), 0)),
                whole(kh.shape),
                whole(kl.shape),
            ],
            out_specs=(pl.BlockSpec((depth, GROUP, lat_block), lambda g: (0, g, 0)),) * (rows_count * halves),
            scratch_shapes=[
                pltpu.VMEM((fields, GROUP + 2 * SUB, lat_block), F32),
                pltpu.VMEM((GROUP + 2 * SUB, lat_block), F32),
                pltpu.VMEM((GROUP, lat_block), F32),
                pltpu.VMEM((tall, LANES), F32),
                pltpu.VMEM((fine, channels * SUB, lat_block), F32),
            ],
            name="second_step",
        )(ids, mu1, mu1, mu1, courant, courant, courant, limiter, limiter, limiter, directions, directions, directions,
          m1, x1, e2a, e2b, x2a, x2b, box, kh, kl)

    def to_rows(pieces):
        return [pieces[0]] + [swap(pieces[s], "row", s) for s in range(1, rows_count)]

    def smooth(pieces, start, height, token):
        count = pieces[0].shape[0]
        filt = lat_filter if token is None else after(lat_filter, token)
        call = pl.pallas_call(
            functools.partial(lat_filter_part, start, height, count, rows_count, cols_count),
            out_shape=(shape_of((count, height, tall), BF16),) * cols_count,
            in_specs=[SMEM_SPEC] + [VMEM_SPEC] * (rows_count + 1),
            out_specs=(VMEM_SPEC,) * cols_count,
            name="lat_filter",
        )
        outs = call(ids, *pieces, filt)
        moved = {s: swap(outs[s], "col", s) for s in range(cols_count - 1, 0, -1)}
        return [outs[0]] + [moved[s] for s in range(1, cols_count)], outs[-1]

    firsts = []
    sent = []
    order = None
    for band in range(n_bands):
        final = band == n_bands - 1
        halves = 1 if final else 2
        kl = kl if order is None else after(kl, order)
        outs = control(band, halves, kl)
        order = outs[-1]
        for h in range(halves):
            sent.append(to_rows([outs[s * halves + h] for s in range(rows_count)]))

    height = lon_filter.shape[0] // 2
    own = lax.dynamic_slice_in_dim(lon_filter, (me_col % 2) * height, height, 0)
    own = after(own, order)
    gathered = [own] + [swap(own, "row", s) for s in range(1, rows_count)]

    token = None
    for pieces in sent[:-1]:
        moved, token = smooth(pieces, 0, lat_part, token)
        firsts += moved
    half_height = lat_part // 2
    lasts = []
    for h in range(2):
        moved, token = smooth(sent[-1], h * half_height, half_height, token)
        lasts.append(moved)
    filters = []
    for piece in gathered:
        filters += [piece, swap(after(piece, token), "col", 1)]

    n_lon = cols_count * lon_block
    rows = share * half_height
    if lon_block % LANES:
        stacked = jnp.stack([jnp.concatenate([lasts[0][s], lasts[1][s]], axis=1) for s in range(cols_count)])
        lines = jnp.take(stacked, me_col ^ jnp.arange(cols_count), axis=0)
        lines = jnp.transpose(lines, (2, 1, 0, 3)).reshape(lat_part, share, n_lon)
        whole_filter = jnp.stack(filters).reshape(rows_count, 2, height, n_lon)
        whole_filter = jnp.take(whole_filter, me_row ^ jnp.arange(rows_count), axis=0)
        whole_filter = jnp.take(whole_filter, me_col % 2 ^ jnp.arange(2), axis=1).reshape(n_lon, n_lon)
        return jnp.einsum("lci,oi->lco", lines, whole_filter, preferred_element_type=F32)
    out = None
    for h in range(2):
        aliased = out is not None
        operands = (ids, *firsts, *lasts[h], *filters) + ((out,) if aliased else ())
        call = pl.pallas_call(
            functools.partial(lon_filter_part, h, half_height, cols_count, rows_count, len(firsts), aliased),
            out_shape=shape_of((2 * rows, n_lon)),
            in_specs=[SMEM_SPEC] + [VMEM_SPEC] * (len(firsts) + cols_count) + [ANY_SPEC] * (2 * rows_count + aliased),
            out_specs=ANY_SPEC,
            scratch_shapes=[
                pltpu.VMEM((rows, n_lon), BF16),
                pltpu.VMEM((2, height, n_lon), BF16),
                pltpu.VMEM((2, height // LANES, rows, LANES), F32),
                pltpu.SemaphoreType.DMA((2,)),
                pltpu.SemaphoreType.DMA((2, height // LANES)),
            ],
            input_output_aliases={len(operands) - 1: 0} if aliased else {},
            name="lon_filter",
        )
        out = call(*operands)
    return out.reshape(lat_part, share, n_lon)


def solution(mesh):
    placed = (
        P(None, "col", "row"),
        P(None, None, None, "col", "row"),
        P(None, None, "col", "row"),
        P(None, None, "col", "row"),
        P(None, "col", "row"),
        P(),
        P(),
        P(),
        P(),
        P("row", None),
    )
    return jax.shard_map(shards, mesh=mesh, in_specs=placed, out_specs=P("col", "row", None), check_vma=False)
```

```python
import functools

import jax
import jax.numpy as jnp
from jax import lax
from jax.experimental import pallas as pl
from jax.experimental.pallas import tpu as pltpu
from jax.sharding import PartitionSpec as P


RATIO = 3
BOXX = 256
BOXY = 32
LANES = 128
SUB = 8
BAND = 128
GROUP = 32
F32 = jnp.float32
BF16 = jnp.bfloat16
NT = (((1,), (1,)), ((), ()))
HIGHEST = lax.Precision.HIGHEST


def lanes_of(shape):
    return lax.broadcasted_iota(jnp.int32, shape, len(shape) - 1)


def sublanes_of(shape):
    return lax.broadcasted_iota(jnp.int32, shape, len(shape) - 2)


def split(value):
    return [value[:, k * LANES : (k + 1) * LANES] for k in range(value.shape[1] // LANES)]


def rows_at(start):
    return pl.ds(pl.multiple_of(start, SUB), SUB)


def x_fluxes(mu, coef, damp, east):
    flux = coef * damp * mu
    part = east * flux
    return part, flux - part


def stencil(mu, px, qx, up_x, down_x, coef, damp, north, halo_up, halo_down):
    flux = coef * damp * mu
    py = north * flux
    qy = flux - py
    base = mu - px + qx - py + qy + up_x - down_x
    lane = lanes_of((SUB, LANES))
    last, first = lane == LANES - 1, lane == 0
    py, qy, base = split(py), split(qy), split(base)
    rolled_up = [pltpu.roll(v, LANES - 1, 1) for v in py]
    rolled_down = [pltpu.roll(v, 1, 1) for v in qy]
    count = len(base)
    out = []
    for k in range(count):
        above = rolled_up[k + 1] if k + 1 < count else halo_up
        below = rolled_down[k - 1] if k > 0 else halo_down
        out.append(base[k] + jnp.where(last, above, rolled_up[k]) - jnp.where(first, below, rolled_down[k]))
    return out, py, qy


def shifted(px_here, px_next, qx_prev, qx_here):
    sub = sublanes_of(px_here.shape)
    up = jnp.where(sub == SUB - 1, pltpu.roll(px_next, SUB - 1, 0), pltpu.roll(px_here, SUB - 1, 0))
    down = jnp.where(sub == 0, pltpu.roll(qx_prev, 1, 0), pltpu.roll(qx_here, 1, 0))
    return up, down


def first_step(mu_ref, cour_ref, lim_ref, dir_ref, out_ref, ef_ref, em_ref, ew_ref, xr_ref, xm_ref, xw_ref, damp, east, north, rim):
    level = pl.program_id(0)
    fields, _, rows, width = mu_ref.shape
    tiles = width // LANES
    groups = rows // GROUP
    tall = ef_ref.shape[0]
    lane = lanes_of((SUB, LANES))
    last = lane == LANES - 1
    edge = slice((tiles - 1) * LANES, tiles * LANES)

    @pl.when(level == 0)
    def _():
        for ref in (ef_ref, em_ref, ew_ref, xr_ref):
            ref[...] = jnp.zeros_like(ref)

        def prepare(tile, carry):
            at = rows_at(tile * SUB)
            east[at] = dir_ref[1, 0, at].astype(F32)
            north[at] = dir_ref[1, 1, at].astype(F32)
            side = jnp.where(last, 1 - dir_ref[0, 1, at, edge], dir_ref[0, 1, at, :LANES]).astype(F32)
            for f in range(fields):
                damp[f, at] = 0.5 + 0.5 * lim_ref[1, f, at].astype(F32)
                flag = jnp.where(last, lim_ref[0, f, at, edge], lim_ref[0, f, at, :LANES]).astype(F32)
                rim[f, at] = side * (0.5 + 0.5 * flag)
            return carry

        lax.fori_loop(0, rows // SUB, prepare, 0)

    def group(g, carry):
        base = g * GROUP
        inside = GROUP // SUB
        starts = [jnp.maximum(base - SUB, 0)] + [base + SUB * t for t in range(inside)] + [jnp.minimum(base + GROUP, rows - SUB)]
        keep_low = jnp.where(g > 0, 1.0, 0.0).astype(F32)
        keep_high = jnp.where(g < groups - 1, 1.0, 0.0).astype(F32)
        band = base // tall
        held = [[ref[rows_at(lax.rem(base, tall) + SUB * t)] for t in range(inside)] for ref in (ef_ref, em_ref, ew_ref)]
        for f in range(fields):
            slot = level * fields + f
            turn = lax.rem(2 * slot + 1 + band * 64, LANES)
            mine = (lane // 2) == slot + 32 * band
            mus = [mu_ref[f, 0, rows_at(s)] for s in starts]
            pq = [
                x_fluxes(m, cour_ref[1, 0, 0, rows_at(s)], damp[f, rows_at(s)], east[rows_at(s)])
                for m, s in zip(mus, starts)
            ]
            px = [v[0] for v in pq]
            qx = [v[1] for v in pq]
            qx[0] = qx[0] * keep_low
            px[-1] = px[-1] * keep_high
            for t in range(inside):
                at = rows_at(starts[t + 1])
                up, down = shifted(px[t + 1], px[t + 2], qx[t], qx[t + 1])
                new, py, qy = stencil(
                    mus[t + 1], px[t + 1], qx[t + 1], up, down, cour_ref[1, 1, 0, at], damp[f, at], north[at],
                    jnp.zeros((SUB, LANES), F32), jnp.zeros((SUB, LANES), F32),
                )
                for k in range(tiles):
                    out_ref[f, 0, at, k * LANES : (k + 1) * LANES] = new[k]
                weight = jnp.where(last, cour_ref[0, 1, 0, at, edge], cour_ref[0, 1, 0, at, :LANES]) * rim[f, at]
                for which, value in enumerate((jnp.where(last, qy[-1], py[0]), jnp.where(last, new[-1], new[0]), weight)):
                    held[which][t] = jnp.where(mine, pltpu.roll(value, turn, 1), held[which][t])
        for which, ref in enumerate((ef_ref, em_ref, ew_ref)):
            for t in range(inside):
                ref[rows_at(lax.rem(base, tall) + SUB * t)] = held[which][t]
        return carry

    lax.fori_loop(0, groups, group, 0)

    low, high = slice(0, SUB), slice(rows - SUB, rows)
    for f in range(fields):
        slot = level * fields + f
        turn = 2 * slot + 1
        mine = (lane // 2) == slot
        px, _ = x_fluxes(mu_ref[f, 0, low], cour_ref[1, 0, 0, low], damp[f, low], east[low])
        _, qx = x_fluxes(mu_ref[f, 0, high], cour_ref[1, 0, 0, high], damp[f, high], east[high])
        xr_ref[level, f : f + 1] = px[:1]
        xr_ref[level, fields + f : fields + f + 1] = qx[SUB - 1 :]
        px_edge = pltpu.roll(jnp.where(last, px[:, edge], px[:, :LANES]), turn, 1)
        qx_edge = pltpu.roll(jnp.where(last, qx[:, edge], qx[:, :LANES]), turn, 1)
        corner = xr_ref.shape[0] - 1
        xr_ref[corner, 0:1, :LANES] = jnp.where(mine, px_edge, jnp.broadcast_to(xr_ref[corner, 0:1, :LANES], (SUB, LANES)))[:1]
        xr_ref[corner, 4:5, :LANES] = jnp.where(mine, qx_edge, jnp.broadcast_to(xr_ref[corner, 4:5, :LANES], (SUB, LANES)))[SUB - 1 :]
        xm_ref[level, f : f + 1] = out_ref[f, 0, low][:1]
        xm_ref[level, fields + f : fields + f + 1] = out_ref[f, 0, high][SUB - 1 :]
        for at, part, row in ((low, 0, 0), (high, 1, SUB - 1)):
            way = dir_ref[0, 0, at].astype(F32)
            way = 1.0 - way if part else way
            value = way * (0.5 + 0.5 * lim_ref[0, f, at].astype(F32)) * cour_ref[0, 0, 0, at]
            xw_ref[level, part * fields + f : part * fields + f + 1] = value[row : row + 1]


def pick(first, a, b):
    return jnp.where(first, a, b)


def rims(rows, parts, ids, efa_ref, efb_ref, xra_ref, xrb_ref, em_ref, ew_ref, xm_ref, xw_ref, eof_ref, e2_ref, x2_ref, m1_ref, x1_ref, kh_ref, kl_ref):
    me_row = ids[0]
    even_row, even_col = ids[2] == 0, ids[3] == 0
    levels, twice, width = xm_ref.shape
    fields = twice // 2
    tiles = width // LANES
    tall = em_ref.shape[0]
    top_band = (rows - 1) // tall
    lane = lanes_of((tall, LANES))
    sub = sublanes_of((tall, LANES))
    up = pick(even_row, efa_ref[...], efb_ref[...])
    down = pick(even_row, efb_ref[...], efa_ref[...])
    merged = jnp.where(lane % 2 == 1, up, -pltpu.roll(down, 2, 1))
    m1_ref[...] = merged
    fixed = em_ref[...] + jnp.where(lane % 2 == 0, pltpu.roll(up, LANES - 1, 1), -pltpu.roll(down, 1, 1))
    corner = xra_ref.shape[0] - 1
    ca, cb = xra_ref[corner, :, :LANES], xrb_ref[corner, :, :LANES]
    corner_up = pick(even_col, ca, cb)[0:1]
    corner_down = pick(even_col, cb, ca)[4:5]
    if top_band:
        corner_up = pltpu.roll(jnp.broadcast_to(corner_up, (SUB, LANES)), 64 * top_band, 1)[:1]
    fixed = fixed + jnp.where(sub == tall - 1, corner_up, 0.0) - jnp.where(sub == 0, corner_down, 0.0)
    e2_ref[...] = ew_ref[...] * fixed

    lane8 = lanes_of((twice, LANES))
    sub8 = sublanes_of((twice, LANES))
    ends = jnp.where(sub8 < fields, jnp.broadcast_to(merged[0:1], (twice, LANES)), jnp.broadcast_to(merged[tall - 1 :], (twice, LANES)))
    wide = sublanes_of((twice, width))
    for level in range(levels):
        a, b = xra_ref[level], xrb_ref[level]
        halo = jnp.where(wide < fields, pick(even_col, a, b), -pick(even_col, b, a))
        x1_ref[level] = halo
        target = 2 * (level * fields + sub8 % fields) + 1 + jnp.where(sub8 >= fields, 64 * top_band, 0)
        at_last = jnp.sum(jnp.where(lane8 == target, ends, 0.0), axis=1, keepdims=True)
        at_first = jnp.sum(jnp.where(lane8 == (target + 1) % LANES, ends, 0.0), axis=1, keepdims=True)
        here = split(xm_ref[level] + pltpu.roll(halo, fields, 0))
        here[-1] = here[-1] + jnp.where(lane8 == LANES - 1, at_last, 0.0)
        here[0] = here[0] + jnp.where(lane8 == 0, at_first, 0.0)
        for k in range(tiles):
            at = slice(k * LANES, (k + 1) * LANES)
            x2_ref[level, :, at] = xw_ref[level, :, at] * here[k]

    channels = eof_ref.shape[0]
    size = kh_ref.shape[0]
    share = channels // parts
    i = lax.broadcasted_iota(jnp.int32, (size, channels), 0) // SUB
    chosen = ((i // share) ^ me_row) * share + i % share
    left = (lax.broadcasted_iota(jnp.int32, (size, channels), 1) == chosen).astype(F32)
    j = lax.broadcasted_iota(jnp.int32, (channels, size), 1) // SUB
    right = (lax.broadcasted_iota(jnp.int32, (channels, size), 0) == j).astype(F32)
    mixed = jnp.dot(left, eof_ref[...], precision=HIGHEST, preferred_element_type=F32)
    spread = jnp.dot(mixed, right, precision=HIGHEST, preferred_element_type=F32)
    same = (lax.broadcasted_iota(jnp.int32, (size, size), 0) - lax.broadcasted_iota(jnp.int32, (size, size), 1)) % SUB == 0
    spread = jnp.where(same, spread, 0.0)
    high = spread.astype(BF16)
    kh_ref[...] = high
    kl_ref[...] = (spread - high.astype(F32)).astype(BF16)


def second_step(
    band, parts, ids, mu_ref, mu_low, mu_high, cour_ref, cx_low, cx_high, lim_ref, lim_low, lim_high, dir_ref, dir_low, dir_high,
    m1_ref, x1_ref, e2a_ref, e2b_ref, x2a_ref, x2b_ref, box_ref, kh_ref, kl_ref, *rest,
):
    outs, (damp, east, north, m2_ref, mixed) = rest[:-5], rest[-5:]
    g = pl.program_id(0)
    fields, levels, _, width = mu_ref.shape
    rows = ids[5]
    tall = m1_ref.shape[0]
    even_row, even_col = ids[2] == 0, ids[3] == 0
    tiles = width // LANES
    inside = GROUP // SUB
    lane = lanes_of((SUB, LANES))
    sub = sublanes_of((SUB, width))
    last, first = lane == LANES - 1, lane == 0

    @pl.when(g == 0)
    def _():
        wide = lanes_of((tall, LANES))
        up = pick(even_row, e2a_ref[...], e2b_ref[...])
        down = pick(even_row, e2b_ref[...], e2a_ref[...])
        m2_ref[...] = jnp.where(wide % 2 == 1, up, -pltpu.roll(down, 2, 1))

    lims = [(lim_low, 0)] + [(lim_ref, SUB * t) for t in range(inside)] + [(lim_high, 0)]
    dirs = [(dir_low, 0)] + [(dir_ref, SUB * t) for t in range(inside)] + [(dir_high, 0)]
    mus = [(mu_low, 0)] + [(mu_ref, SUB * t) for t in range(inside)] + [(mu_high, 0)]
    cxs = [(cx_low, 0)] + [(cour_ref, SUB * t) for t in range(inside)] + [(cx_high, 0)]
    for t in range(inside + 2):
        put = slice(SUB * t, SUB * (t + 1))
        ref, r = dirs[t]
        east[put] = ref[0, 0, r : r + SUB].astype(F32)
        if 0 < t <= inside:
            north[SUB * (t - 1) : SUB * t] = ref[0, 1, r : r + SUB].astype(F32)
        ref, r = lims[t]
        for f in range(fields):
            damp[f, put] = 0.5 + 0.5 * ref[0, f, r : r + SUB].astype(F32)

    base = band * tall + g * GROUP
    starts = [jnp.maximum(base - SUB, 0)] + [base + SUB * t for t in range(inside)] + [jnp.minimum(base + GROUP, rows - SUB)]
    bands = [s // tall for s in starts]
    places = [lax.rem(s, tall) for s in starts]
    at_start = base == 0
    at_end = base + GROUP == rows
    lat_at = ids[7]
    box_lats = box_ref.shape[1] // (fields * levels * parts)
    away = (lane - lat_at) & (LANES - 1)
    piece = away // box_lats
    total = parts * box_lats
    span = fields * levels * box_lats // LANES
    inner = [((lane + LANES * k - lat_at) >= 0) & ((lane + LANES * k - lat_at) < total) for k in range(tiles)]

    def channel_group(level, carry):
        for f in range(fields):
            slot = level * fields + f
            vals, px, qx = [], [], []
            for t in range(inside + 2):
                ref, r = mus[t]
                value = ref[f, level, r : r + SUB]
                fix = pltpu.roll(m1_ref[rows_at(places[t])], (126 - 2 * slot - 64 * bands[t]) & (LANES - 1), 1)
                pieces = split(value)
                pieces[-1] = pieces[-1] + jnp.where(last, fix, 0.0)
                pieces[0] = pieces[0] + jnp.where(first, fix, 0.0)
                value = jnp.concatenate(pieces, axis=1)
                if t == 1:
                    value = value + jnp.where((sub == 0) & at_start, x1_ref[level, fields + f : fields + f + 1], 0.0)
                if t == inside:
                    value = value + jnp.where((sub == SUB - 1) & at_end, x1_ref[level, f : f + 1], 0.0)
                ref, r = cxs[t]
                p, q = x_fluxes(value, ref[0, 0, level, r : r + SUB], damp[f, SUB * t : SUB * (t + 1)], east[SUB * t : SUB * (t + 1)])
                vals.append(value)
                px.append(p)
                qx.append(q)
            halo_low = pick(even_col, x2b_ref[level, fields + f : fields + f + 1], x2a_ref[level, fields + f : fields + f + 1])
            halo_high = pick(even_col, x2a_ref[level, f : f + 1], x2b_ref[level, f : f + 1])
            qx[0] = jnp.where(at_start, jnp.broadcast_to(halo_low, (SUB, width)), qx[0])
            px[-1] = jnp.where(at_end, jnp.broadcast_to(halo_high, (SUB, width)), px[-1])
            for t in range(inside):
                here = slice(SUB * (t + 1), SUB * (t + 2))
                mine = slice(SUB * t, SUB * (t + 1))
                up, down = shifted(px[t + 1], px[t + 2], qx[t], qx[t + 1])
                halo = pltpu.roll(m2_ref[rows_at(places[t + 1])], (126 - 2 * slot - 64 * bands[t + 1]) & (LANES - 1), 1)
                new, _, _ = stencil(
                    vals[t + 1], px[t + 1], qx[t + 1], up, down, cour_ref[0, 1, level, mine], damp[f, here], north[mine], halo, -halo
                )
                gathered = jnp.zeros((SUB, LANES), F32)
                for r in range(parts):
                    block = r * span + f * levels * box_lats // LANES
                    begin = (f * levels * box_lats) % LANES + level * box_lats
                    source = box_ref[mine, block * LANES : (block + 1) * LANES]
                    moved = pltpu.roll(source, (lat_at + box_lats * r - begin) & (LANES - 1), 1)
                    gathered = jnp.where(piece == r, moved, gathered)
                put = rows_at((f * levels + level) * SUB)
                for k in range(tiles):
                    mixed[t, put, k * LANES : (k + 1) * LANES] = new[k] + jnp.where(inner[k], gathered, 0.0)
        return carry

    lax.fori_loop(0, levels, channel_group, 0)

    channels = fields * levels
    share = channels // parts
    per = len(outs) // parts
    depth = share // per
    for v in range(inside // 2):
        both = []
        for t in (2 * v, 2 * v + 1):
            full = mixed[t]
            high = full.astype(BF16)
            low = (full - high.astype(F32)).astype(BF16)
            result = jnp.dot(kh_ref[...], high, preferred_element_type=F32)
            result += jnp.dot(kl_ref[...], high, preferred_element_type=F32)
            result += jnp.dot(kh_ref[...], low, preferred_element_type=F32)
            both.append(result)
        for c in range(channels):
            at = slice(c * SUB, (c + 1) * SUB)
            pair = jnp.concatenate([both[0][at], both[1][at]], axis=0).astype(BF16)
            outs[(c // share) * per + (c % share) // depth][c % depth, 2 * SUB * v : 2 * SUB * (v + 1)] = pair


def coarse_sums(ids, nest_ref, out_ref, held):
    channels, fine_lat, fine_lon = nest_ref.shape
    lon = ids[1] * fine_lon + lax.broadcasted_iota(jnp.int32, (fine_lat, fine_lon), 1)
    lat = ids[0] * fine_lat + lax.broadcasted_iota(jnp.int32, (fine_lat, fine_lon), 0)
    edge = (lon < RATIO) | (lon >= RATIO * BOXX - RATIO) | (lat < RATIO) | (lat >= RATIO * BOXY - RATIO)
    weight = jnp.where(edge, 1.0, 1.0 / (RATIO * RATIO)).astype(F32)
    for c in range(channels):
        held[c * fine_lat : (c + 1) * fine_lat] = nest_ref[c] * weight
    count = channels * fine_lat // RATIO
    sums = held[pl.ds(0, count, stride=RATIO)]
    for a in range(1, RATIO):
        sums = sums + held[pl.ds(a, count, stride=RATIO)]
    shape = (fine_lon // RATIO, fine_lon)
    select = (lax.broadcasted_iota(jnp.int32, shape, 1) // RATIO == lax.broadcasted_iota(jnp.int32, shape, 0)).astype(F32)
    out_ref[...] = lax.dot_general(select, sums, NT, precision=HIGHEST, preferred_element_type=F32)


def arrange(masks, ids, near_ref, far_ref, out_ref, box):
    half, slab, wide = near_ref.shape
    rows = out_ref.shape[0]
    for p, (row_mask, col_mask) in enumerate(masks):
        at = pl.multiple_of((ids[1] ^ col_mask) * slab, SUB)
        to = pl.multiple_of((ids[0] ^ row_mask) * wide, LANES)
        box[pl.ds(at, slab), pl.ds(to, wide)] = near_ref[p] if p < half else far_ref[p - half]
    height = box.shape[0]
    away = ids[6]
    row = lax.broadcasted_iota(jnp.int32, (rows, LANES), 0) - away
    inside = (row >= 0) & (row < height)
    turn = lax.rem(lax.rem(away, height) + height, height)
    for k in range(box.shape[1] // LANES):
        at = slice(k * LANES, (k + 1) * LANES)
        out_ref[:, at] = jnp.where(inside, pltpu.roll(box[:, at], turn, 0)[:rows], 0.0)


def lat_filter_part(start, height, count, parts, cols, ids, *refs):
    pieces, filt, outs = refs[:parts], refs[parts], refs[parts + 1 :]
    lat_block = pieces[0].shape[2]
    lon = pieces[0].shape[1]
    lat_part = filt.shape[0] // cols
    step = 2
    for p in range(count // step):
        right = [ref[step * p : step * (p + 1)].reshape(step * lon, lat_block) for ref in pieces]
        for s0 in range(0, cols, 4):
            acc = None
            for r in range(parts):
                at = pl.ds(pl.multiple_of((ids[0] ^ r) * lat_block, LANES), lat_block)
                left = jnp.concatenate(
                    [
                        filt[pl.ds(pl.multiple_of((ids[1] ^ s) * lat_part + start, 16), height), at]
                        for s in range(s0, min(s0 + 4, cols))
                    ],
                    axis=0,
                )
                term = lax.dot_general(left, right[r], NT, preferred_element_type=F32)
                acc = term if acc is None else acc + term
            for s in range(s0, min(s0 + 4, cols)):
                for c in range(step):
                    value = acc[(s - s0) * height : (s - s0 + 1) * height, c * lon : (c + 1) * lon]
                    outs[s][step * p + c] = value.astype(BF16)


def lon_filter_part(half, height, cols, parts, n_first, aliased, owners, ids, *refs):
    firsts = refs[:n_first]
    lasts = refs[n_first : n_first + cols]
    filters = refs[n_first + cols : n_first + cols + 2 * parts]
    rest = refs[n_first + cols + 2 * parts + (1 if aliased else 0) :]
    out, lines, buffer, stage, in_sem, out_sem = rest
    channels, _, lon = lasts[0].shape
    wide = lines.shape[1] // cols
    rows = channels * height
    block = filters[0].shape[0]
    steps = 2 * parts
    strips = block // LANES

    def fetch(j):
        return pltpu.make_async_copy(filters[j], buffer.at[j % 2], in_sem.at[j % 2])

    def owner(j):
        side = ids[8] if j % 2 == 0 else 1 - ids[8]
        even, odd = owners[j // 2]
        return (ids[0] ^ jnp.where(side == 0, even, odd)) * 2 + side

    def flush(j, k):
        at = pl.ds(pl.multiple_of(owner(j) * block + k * LANES, LANES), LANES)
        return pltpu.make_async_copy(stage.at[j % 2, k], out.at[pl.ds(half * rows, rows), at], out_sem.at[j % 2, k])

    fetch(0).start()
    for s in range(cols):
        base = pl.multiple_of((ids[1] ^ s) * wide, LANES)
        for c in range(channels):
            put = slice(c * height, (c + 1) * height)
            for b in range(wide // lon - 1):
                groups = n_first // cols // (wide // lon - 1)
                each = channels // groups
                ref = firsts[(b * groups + c // each) * cols + s]
                lines[put, pl.ds(base + b * lon, lon)] = ref[c % each, half * height : (half + 1) * height]
            lines[put, pl.ds(base + wide - lon, lon)] = lasts[s][c]
    for j in range(steps):
        if j + 1 < steps:
            fetch(j + 1).start()
        fetch(j).wait()
        if j >= 2:
            for k in range(strips):
                flush(j - 2, k).wait()
        acc = lax.dot_general(lines[...], buffer[j % 2], NT, preferred_element_type=F32)
        for c in range(channels):
            for k in range(strips):
                at = slice(k * LANES, (k + 1) * LANES)
                stage[j % 2, k, pl.ds(c, height, stride=channels), :] = acc[c * height : (c + 1) * height, at]
        for k in range(strips):
            flush(j, k).start()
    for j in (steps - 2, steps - 1):
        for k in range(strips):
            flush(j, k).wait()


def swap(value, axis, mask):
    count = lax.axis_size(axis)
    return lax.ppermute(value, axis, [(i, i ^ mask) for i in range(count)])


def neighbours(value, axis, parity):
    count = lax.axis_size(axis)
    pairs = []
    for i in range(parity, count - 1, 2):
        pairs += [(i, i + 1), (i + 1, i)]
    return lax.ppermute(value, axis, pairs)


def shape_of(shape, dtype=F32):
    return jax.ShapeDtypeStruct(shape, dtype)


def whole(shape):
    return pl.BlockSpec(shape, lambda *_: (0,) * len(shape))


VMEM_SPEC = pl.BlockSpec(memory_space=pltpu.VMEM)
SMEM_SPEC = pl.BlockSpec(memory_space=pltpu.SMEM)
ANY_SPEC = pl.BlockSpec(memory_space=pl.ANY)


def shards(final_sens, courant, limiter, directions, nest_sens, box_lon, box_lat, eof, lat_filter, lon_filter):
    channels, lon_block, lat_block = final_sens.shape
    fields, levels = limiter.shape[1], courant.shape[2]
    rows_count, cols_count = lax.axis_size("row"), lax.axis_size("col")
    me_row, me_col = lax.axis_index("row"), lax.axis_index("col")
    ids = jnp.stack(
        [
            me_row,
            me_col,
            me_row % 2,
            me_col % 2,
            me_row * 0,
            me_row * 0 + lon_block,
            box_lon[0] - me_col * lon_block,
            box_lat[0] - me_row * lat_block,
            me_col % 2,
        ]
    ).astype(jnp.int32)
    lat_part = lat_filter.shape[0] // cols_count
    share = channels // rows_count
    tall = min(BAND, lon_block)
    n_bands = lon_block // tall

    height = lon_filter.shape[0] // 2
    gathered = [lax.dynamic_slice_in_dim(lon_filter, (me_col % 2) * height, height, 0)]
    orders = [2**k for k in range(10) if 2**k < rows_count]
    turns = (orders, orders[::-1])
    owners = [(0, 0)]

    def gather(stage, pieces):
        pairs = []
        for i in range(rows_count * cols_count):
            row, col = divmod(i, cols_count)
            pairs.append((i, (row ^ turns[col % 2][stage]) * cols_count + col))
        return [lax.ppermute(piece, ("row", "col"), pairs) for piece in pieces]

    gathered += gather(0, gathered)
    owners += [(turns[0][0], turns[1][0])]

    nest = jnp.transpose(nest_sens, (0, 2, 1))
    fine_lat, fine_lon = nest.shape[1:]
    coarse = pl.pallas_call(
        coarse_sums,
        out_shape=shape_of((fine_lon // RATIO, channels * fine_lat // RATIO)),
        in_specs=[SMEM_SPEC, VMEM_SPEC],
        out_specs=VMEM_SPEC,
        scratch_shapes=[pltpu.VMEM((channels * fine_lat, fine_lon), F32)],
        name="coarse",
    )(ids, nest)
    masks = [(0, 0)]
    stages = [("col", m) for m in (2**k for k in range(1, 10)) if m < cols_count]
    stages += [("row", m) for m in (2**k for k in range(10)) if m < rows_count]
    stages += [("col", 1)]

    def spread(held, count, last=False):
        nonlocal stages, masks
        for axis, mask in stages[:count]:
            other = swap(held, axis, mask)
            held = (held, other) if last else jnp.concatenate([held, other], axis=0)
            masks = masks + [(r ^ mask, c) if axis == "row" else (r, c ^ mask) for r, c in masks]
        stages = stages[count:]
        return held

    def after(value, *others):
        return lax.optimization_barrier((value, *others))[0]

    held = spread(coarse[None], 2)

    mu = final_sens.reshape(fields, levels, lon_block, lat_block)
    call = pl.pallas_call(
        first_step,
        grid=(levels,),
        out_shape=(
            shape_of(mu.shape),
            shape_of((tall, LANES)),
            shape_of((tall, LANES)),
            shape_of((tall, LANES)),
            shape_of((levels + 1, 2 * fields, lat_block)),
            shape_of((levels, 2 * fields, lat_block)),
            shape_of((levels, 2 * fields, lat_block)),
        ),
        in_specs=[
            pl.BlockSpec((fields, 1, lon_block, lat_block), lambda l: (0, l, 0, 0)),
            pl.BlockSpec((2, 2, 1, lon_block, lat_block), lambda l: (0, 0, l, 0, 0)),
            whole(limiter.shape),
            whole(directions.shape),
        ],
        out_specs=(
            pl.BlockSpec((fields, 1, lon_block, lat_block), lambda l: (0, l, 0, 0)),
            whole((tall, LANES)),
            whole((tall, LANES)),
            whole((tall, LANES)),
            whole((levels + 1, 2 * fields, lat_block)),
            whole((levels, 2 * fields, lat_block)),
            whole((levels, 2 * fields, lat_block)),
        ),
        scratch_shapes=[
            pltpu.VMEM((fields, lon_block, lat_block), F32),
            pltpu.VMEM((lon_block, lat_block), F32),
            pltpu.VMEM((lon_block, lat_block), F32),
            pltpu.VMEM((fields, lon_block, LANES), F32),
        ],
        name="first_step",
    )
    mu1, ef, em, ew, xr, xm, xw = call(mu, courant, limiter, directions)
    held = spread(after(held, ef), 1)
    efa, efb = neighbours(ef, "row", 0), neighbours(ef, "row", 1)
    xra, xrb = neighbours(xr, "col", 0), neighbours(xr, "col", 1)
    held = spread(after(held, efa, efb, xra, xrb), len(stages) - 1)
    size = channels * SUB
    call = pl.pallas_call(
        functools.partial(rims, lon_block, rows_count),
        out_shape=(
            shape_of(ef.shape),
            shape_of(xm.shape),
            shape_of(ef.shape),
            shape_of(xm.shape),
            shape_of((size, size), BF16),
            shape_of((size, size), BF16),
        ),
        in_specs=[SMEM_SPEC] + [VMEM_SPEC] * 9,
        out_specs=(VMEM_SPEC,) * 6,
        name="rims",
    )
    e2, x2, m1, x1, kh, kl = call(ids, efa, efb, xra, xrb, em, ew, xm, xw, eof)
    e2a, e2b = neighbours(e2, "row", 0), neighbours(e2, "row", 1)
    x2a, x2b = neighbours(x2, "col", 0), neighbours(x2, "col", 1)
    held = spread(held, 1, True)
    box = pl.pallas_call(
        functools.partial(arrange, masks),
        out_shape=shape_of((lon_block, rows_count * coarse.shape[1])),
        in_specs=[SMEM_SPEC, VMEM_SPEC, VMEM_SPEC],
        out_specs=VMEM_SPEC,
        scratch_shapes=[pltpu.VMEM((cols_count * coarse.shape[0], rows_count * coarse.shape[1]), F32)],
        name="arrange",
    )(ids, *held)

    groups = tall // GROUP
    fine = GROUP // SUB
    top = lon_block // SUB - 1

    def control(band, halves, kl):
        def at(g):
            return band * groups + g

        def low(g):
            return jnp.maximum((band * groups + g) * fine - 1, 0)

        def high(g):
            return jnp.minimum((band * groups + g) * fine + fine, top)

        depth = share // halves
        return pl.pallas_call(
            functools.partial(second_step, band, rows_count),
            grid=(groups,),
            out_shape=(shape_of((depth, tall, lat_block), BF16),) * (rows_count * halves),
            in_specs=[
                SMEM_SPEC,
                pl.BlockSpec((fields, levels, GROUP, lat_block), lambda g: (0, 0, at(g), 0)),
                pl.BlockSpec((fields, levels, SUB, lat_block), lambda g: (0, 0, low(g), 0)),
                pl.BlockSpec((fields, levels, SUB, lat_block), lambda g: (0, 0, high(g), 0)),
                pl.BlockSpec((1, 2, levels, GROUP, lat_block), lambda g: (0, 0, 0, at(g), 0)),
                pl.BlockSpec((1, 1, levels, SUB, lat_block), lambda g: (0, 0, 0, low(g), 0)),
                pl.BlockSpec((1, 1, levels, SUB, lat_block), lambda g: (0, 0, 0, high(g), 0)),
                pl.BlockSpec((1, fields, GROUP, lat_block), lambda g: (0, 0, at(g), 0)),
                pl.BlockSpec((1, fields, SUB, lat_block), lambda g: (0, 0, low(g), 0)),
                pl.BlockSpec((1, fields, SUB, lat_block), lambda g: (0, 0, high(g), 0)),
                pl.BlockSpec((1, 2, GROUP, lat_block), lambda g: (0, 0, at(g), 0)),
                pl.BlockSpec((1, 1, SUB, lat_block), lambda g: (0, 0, low(g), 0)),
                pl.BlockSpec((1, 1, SUB, lat_block), lambda g: (0, 0, high(g), 0)),
                whole(m1.shape),
                whole(x1.shape),
                whole(e2.shape),
                whole(e2.shape),
                whole(x2.shape),
                whole(x2.shape),
                pl.BlockSpec((GROUP, box.shape[1]), lambda g: (at(g), 0)),
                whole(kh.shape),
                whole(kl.shape),
            ],
            out_specs=(pl.BlockSpec((depth, GROUP, lat_block), lambda g: (0, g, 0)),) * (rows_count * halves),
            scratch_shapes=[
                pltpu.VMEM((fields, GROUP + 2 * SUB, lat_block), F32),
                pltpu.VMEM((GROUP + 2 * SUB, lat_block), F32),
                pltpu.VMEM((GROUP, lat_block), F32),
                pltpu.VMEM((tall, LANES), F32),
                pltpu.VMEM((fine, channels * SUB, lat_block), F32),
            ],
            name="second_step",
        )(ids, mu1, mu1, mu1, courant, courant, courant, limiter, limiter, limiter, directions, directions, directions,
          m1, x1, e2a, e2b, x2a, x2b, box, kh, kl)

    def to_rows(pieces):
        return [pieces[0]] + [swap(pieces[s], "row", s) for s in range(1, rows_count)]

    def smooth(pieces, start, height, token):
        count = pieces[0].shape[0]
        filt = lat_filter if token is None else after(lat_filter, token)
        call = pl.pallas_call(
            functools.partial(lat_filter_part, start, height, count, rows_count, cols_count),
            out_shape=(shape_of((count, height, tall), BF16),) * cols_count,
            in_specs=[SMEM_SPEC] + [VMEM_SPEC] * (rows_count + 1),
            out_specs=(VMEM_SPEC,) * cols_count,
            name="lat_filter",
        )
        outs = call(ids, *pieces, filt)
        moved = {s: swap(outs[s], "col", s) for s in range(cols_count - 1, 0, -1)}
        return [outs[0]] + [moved[s] for s in range(1, cols_count)], outs[-1]

    firsts = []
    sent = []
    order = None
    for band in range(n_bands):
        final = band == n_bands - 1
        halves = 1 if final else 2
        kl = kl if order is None else after(kl, order)
        outs = control(band, halves, kl)
        order = outs[-1]
        for h in range(halves):
            sent.append(to_rows([outs[s * halves + h] for s in range(rows_count)]))

    token = None
    for pieces in sent[:-1]:
        moved, token = smooth(pieces, 0, lat_part, token)
        firsts += moved
    half_height = lat_part // 2
    lasts = []
    for h in range(2):
        early = token
        moved, token = smooth(sent[-1], h * half_height, half_height, token)
        lasts.append(moved)
    for stage in range(1, len(orders)):
        gathered += gather(stage, [after(piece, early) for piece in gathered])
        owners += [(a ^ turns[0][stage], b ^ turns[1][stage]) for a, b in owners]
    filters = []
    for piece in gathered:
        filters += [piece, swap(after(piece, token), "col", 1)]

    n_lon = cols_count * lon_block
    rows = share * half_height
    if lon_block % LANES:
        stacked = jnp.stack([jnp.concatenate([lasts[0][s], lasts[1][s]], axis=1) for s in range(cols_count)])
        lines = jnp.take(stacked, me_col ^ jnp.arange(cols_count), axis=0)
        lines = jnp.transpose(lines, (2, 1, 0, 3)).reshape(lat_part, share, n_lon)
        whole_filter = jnp.zeros((n_lon, n_lon), BF16)
        for j, piece in enumerate(filters):
            side = me_col % 2 if j % 2 == 0 else 1 - me_col % 2
            owner = (me_row ^ jnp.where(side == 0, *owners[j // 2])) * 2 + side
            whole_filter = lax.dynamic_update_slice_in_dim(whole_filter, piece, owner * height, 0)
        return jnp.einsum("lci,oi->lco", lines, whole_filter, preferred_element_type=F32)
    out = None
    for h in range(2):
        aliased = out is not None
        operands = (ids, *firsts, *lasts[h], *filters) + ((out,) if aliased else ())
        call = pl.pallas_call(
            functools.partial(lon_filter_part, h, half_height, cols_count, rows_count, len(firsts), aliased, owners),
            out_shape=shape_of((2 * rows, n_lon)),
            in_specs=[SMEM_SPEC] + [VMEM_SPEC] * (len(firsts) + cols_count) + [ANY_SPEC] * (2 * rows_count + aliased),
            out_specs=ANY_SPEC,
            scratch_shapes=[
                pltpu.VMEM((rows, n_lon), BF16),
                pltpu.VMEM((2, height, n_lon), BF16),
                pltpu.VMEM((2, height // LANES, rows, LANES), F32),
                pltpu.SemaphoreType.DMA((2,)),
                pltpu.SemaphoreType.DMA((2, height // LANES)),
            ],
            input_output_aliases={len(operands) - 1: 0} if aliased else {},
            name="lon_filter",
        )
        out = call(*operands)
    return out.reshape(lat_part, share, n_lon)


def solution(mesh):
    placed = (
        P(None, "col", "row"),
        P(None, None, None, "col", "row"),
        P(None, None, "col", "row"),
        P(None, None, "col", "row"),
        P(None, "col", "row"),
        P(),
        P(),
        P(),
        P(),
        P("row", None),
    )
    return jax.shard_map(shards, mesh=mesh, in_specs=placed, out_specs=P("col", "row", None), check_vma=False)
```

```python
import functools

import jax
import jax.numpy as jnp
from jax import lax
from jax.experimental import pallas as pl
from jax.experimental.pallas import tpu as pltpu
from jax.sharding import PartitionSpec as P


RATIO = 3
BOXX = 256
BOXY = 32
LANES = 128
SUB = 8
BAND = 128
GROUP = 32
F32 = jnp.float32
BF16 = jnp.bfloat16
NT = (((1,), (1,)), ((), ()))
HIGHEST = lax.Precision.HIGHEST


def lanes_of(shape):
    return lax.broadcasted_iota(jnp.int32, shape, len(shape) - 1)


def sublanes_of(shape):
    return lax.broadcasted_iota(jnp.int32, shape, len(shape) - 2)


def split(value):
    return [value[:, k * LANES : (k + 1) * LANES] for k in range(value.shape[1] // LANES)]


def rows_at(start):
    return pl.ds(pl.multiple_of(start, SUB), SUB)


def x_fluxes(damped, coef, east):
    flux = coef * damped
    part = east * flux
    return part, flux - part


def stencil(mu, px, qx, up_x, down_x, damped, coef, north, halo_up, halo_down):
    flux = coef * damped
    py = north * flux
    qy = flux - py
    base = mu - px + qx - py + qy + up_x - down_x
    lane = lanes_of((SUB, LANES))
    last, first = lane == LANES - 1, lane == 0
    py, qy, base = split(py), split(qy), split(base)
    rolled_up = [pltpu.roll(v, LANES - 1, 1) for v in py]
    rolled_down = [pltpu.roll(v, 1, 1) for v in qy]
    count = len(base)
    out = []
    for k in range(count):
        above = rolled_up[k + 1] if k + 1 < count else halo_up
        below = rolled_down[k - 1] if k > 0 else halo_down
        out.append(base[k] + jnp.where(last, above, rolled_up[k]) - jnp.where(first, below, rolled_down[k]))
    return out, py, qy


def shifted(px_here, px_next, qx_prev, qx_here):
    sub = sublanes_of(px_here.shape)
    up = jnp.where(sub == SUB - 1, pltpu.roll(px_next, SUB - 1, 0), pltpu.roll(px_here, SUB - 1, 0))
    down = jnp.where(sub == 0, pltpu.roll(qx_prev, 1, 0), pltpu.roll(qx_here, 1, 0))
    return up, down


def first_step(mu_ref, cour_ref, lim_ref, dir_ref, out_ref, ef_ref, em_ref, ew_ref, xr_ref, xm_ref, xw_ref, damp, east, north, rim):
    level = pl.program_id(0)
    fields, _, rows, width = mu_ref.shape
    tiles = width // LANES
    groups = rows // GROUP
    tall = ef_ref.shape[0]
    lane = lanes_of((SUB, LANES))
    last = lane == LANES - 1
    edge = slice((tiles - 1) * LANES, tiles * LANES)

    @pl.when(level == 0)
    def _():
        for ref in (ef_ref, em_ref, ew_ref, xr_ref):
            ref[...] = jnp.zeros_like(ref)

        def prepare(tile, carry):
            at = rows_at(tile * SUB)
            east[at] = dir_ref[1, 0, at].astype(F32)
            north[at] = dir_ref[1, 1, at].astype(F32)
            side = jnp.where(last, 1 - dir_ref[0, 1, at, edge], dir_ref[0, 1, at, :LANES]).astype(F32)
            for f in range(fields):
                damp[f, at] = 0.5 + 0.5 * lim_ref[1, f, at].astype(F32)
                flag = jnp.where(last, lim_ref[0, f, at, edge], lim_ref[0, f, at, :LANES]).astype(F32)
                rim[f, at] = side * (0.5 + 0.5 * flag)
            return carry

        lax.fori_loop(0, rows // SUB, prepare, 0)

    def group(g, carry):
        base = g * GROUP
        inside = GROUP // SUB
        starts = [jnp.maximum(base - SUB, 0)] + [base + SUB * t for t in range(inside)] + [jnp.minimum(base + GROUP, rows - SUB)]
        keep_low = jnp.where(g > 0, 1.0, 0.0).astype(F32)
        keep_high = jnp.where(g < groups - 1, 1.0, 0.0).astype(F32)
        band = base // tall
        held = [[ref[rows_at(lax.rem(base, tall) + SUB * t)] for t in range(inside)] for ref in (ef_ref, em_ref, ew_ref)]
        for f in range(fields):
            slot = level * fields + f
            turn = lax.rem(2 * slot + 1 + band * 64, LANES)
            mine = (lane // 2) == slot + 32 * band
            mus = [mu_ref[f, 0, rows_at(s)] for s in starts]
            damped = [m * damp[f, rows_at(s)] for m, s in zip(mus, starts)]
            pq = [x_fluxes(m, cour_ref[1, 0, 0, rows_at(s)], east[rows_at(s)]) for m, s in zip(damped, starts)]
            px = [v[0] for v in pq]
            qx = [v[1] for v in pq]
            qx[0] = qx[0] * keep_low
            px[-1] = px[-1] * keep_high
            for t in range(inside):
                at = rows_at(starts[t + 1])
                up, down = shifted(px[t + 1], px[t + 2], qx[t], qx[t + 1])
                new, py, qy = stencil(
                    mus[t + 1], px[t + 1], qx[t + 1], up, down, damped[t + 1], cour_ref[1, 1, 0, at], north[at],
                    jnp.zeros((SUB, LANES), F32), jnp.zeros((SUB, LANES), F32),
                )
                for k in range(tiles):
                    out_ref[f, 0, at, k * LANES : (k + 1) * LANES] = new[k]
                weight = jnp.where(last, cour_ref[0, 1, 0, at, edge], cour_ref[0, 1, 0, at, :LANES]) * rim[f, at]
                for which, value in enumerate((jnp.where(last, qy[-1], py[0]), jnp.where(last, new[-1], new[0]), weight)):
                    held[which][t] = jnp.where(mine, pltpu.roll(value, turn, 1), held[which][t])
        for which, ref in enumerate((ef_ref, em_ref, ew_ref)):
            for t in range(inside):
                ref[rows_at(lax.rem(base, tall) + SUB * t)] = held[which][t]
        return carry

    lax.fori_loop(0, groups, group, 0)

    low, high = slice(0, SUB), slice(rows - SUB, rows)
    for f in range(fields):
        slot = level * fields + f
        turn = 2 * slot + 1
        mine = (lane // 2) == slot
        px, _ = x_fluxes(mu_ref[f, 0, low] * damp[f, low], cour_ref[1, 0, 0, low], east[low])
        _, qx = x_fluxes(mu_ref[f, 0, high] * damp[f, high], cour_ref[1, 0, 0, high], east[high])
        xr_ref[level, f : f + 1] = px[:1]
        xr_ref[level, fields + f : fields + f + 1] = qx[SUB - 1 :]
        px_edge = pltpu.roll(jnp.where(last, px[:, edge], px[:, :LANES]), turn, 1)
        qx_edge = pltpu.roll(jnp.where(last, qx[:, edge], qx[:, :LANES]), turn, 1)
        corner = xr_ref.shape[0] - 1
        xr_ref[corner, 0:1, :LANES] = jnp.where(mine, px_edge, jnp.broadcast_to(xr_ref[corner, 0:1, :LANES], (SUB, LANES)))[:1]
        xr_ref[corner, 4:5, :LANES] = jnp.where(mine, qx_edge, jnp.broadcast_to(xr_ref[corner, 4:5, :LANES], (SUB, LANES)))[SUB - 1 :]
        xm_ref[level, f : f + 1] = out_ref[f, 0, low][:1]
        xm_ref[level, fields + f : fields + f + 1] = out_ref[f, 0, high][SUB - 1 :]
        for at, part, row in ((low, 0, 0), (high, 1, SUB - 1)):
            way = dir_ref[0, 0, at].astype(F32)
            way = 1.0 - way if part else way
            value = way * (0.5 + 0.5 * lim_ref[0, f, at].astype(F32)) * cour_ref[0, 0, 0, at]
            xw_ref[level, part * fields + f : part * fields + f + 1] = value[row : row + 1]


def pick(first, a, b):
    return jnp.where(first, a, b)


def rims(rows, parts, ids, efa_ref, efb_ref, xra_ref, xrb_ref, em_ref, ew_ref, xm_ref, xw_ref, eof_ref, e2_ref, x2_ref, m1_ref, x1_ref, kh_ref, kl_ref):
    me_row = ids[0]
    even_row, even_col = ids[2] == 0, ids[3] == 0
    levels, twice, width = xm_ref.shape
    fields = twice // 2
    tiles = width // LANES
    tall = em_ref.shape[0]
    top_band = (rows - 1) // tall
    lane = lanes_of((tall, LANES))
    sub = sublanes_of((tall, LANES))
    up = pick(even_row, efa_ref[...], efb_ref[...])
    down = pick(even_row, efb_ref[...], efa_ref[...])
    merged = jnp.where(lane % 2 == 1, up, -pltpu.roll(down, 2, 1))
    m1_ref[...] = merged
    fixed = em_ref[...] + jnp.where(lane % 2 == 0, pltpu.roll(up, LANES - 1, 1), -pltpu.roll(down, 1, 1))
    corner = xra_ref.shape[0] - 1
    ca, cb = xra_ref[corner, :, :LANES], xrb_ref[corner, :, :LANES]
    corner_up = pick(even_col, ca, cb)[0:1]
    corner_down = pick(even_col, cb, ca)[4:5]
    if top_band:
        corner_up = pltpu.roll(jnp.broadcast_to(corner_up, (SUB, LANES)), 64 * top_band, 1)[:1]
    fixed = fixed + jnp.where(sub == tall - 1, corner_up, 0.0) - jnp.where(sub == 0, corner_down, 0.0)
    e2_ref[...] = ew_ref[...] * fixed

    lane8 = lanes_of((twice, LANES))
    sub8 = sublanes_of((twice, LANES))
    ends = jnp.where(sub8 < fields, jnp.broadcast_to(merged[0:1], (twice, LANES)), jnp.broadcast_to(merged[tall - 1 :], (twice, LANES)))
    wide = sublanes_of((twice, width))
    for level in range(levels):
        a, b = xra_ref[level], xrb_ref[level]
        halo = jnp.where(wide < fields, pick(even_col, a, b), -pick(even_col, b, a))
        x1_ref[level] = halo
        target = 2 * (level * fields + sub8 % fields) + 1 + jnp.where(sub8 >= fields, 64 * top_band, 0)
        at_last = jnp.sum(jnp.where(lane8 == target, ends, 0.0), axis=1, keepdims=True)
        at_first = jnp.sum(jnp.where(lane8 == (target + 1) % LANES, ends, 0.0), axis=1, keepdims=True)
        here = split(xm_ref[level] + pltpu.roll(halo, fields, 0))
        here[-1] = here[-1] + jnp.where(lane8 == LANES - 1, at_last, 0.0)
        here[0] = here[0] + jnp.where(lane8 == 0, at_first, 0.0)
        for k in range(tiles):
            at = slice(k * LANES, (k + 1) * LANES)
            x2_ref[level, :, at] = xw_ref[level, :, at] * here[k]

    channels = eof_ref.shape[0]
    size = kh_ref.shape[0]
    share = channels // parts
    i = lax.broadcasted_iota(jnp.int32, (size, channels), 0) // SUB
    chosen = ((i // share) ^ me_row) * share + i % share
    left = (lax.broadcasted_iota(jnp.int32, (size, channels), 1) == chosen).astype(F32)
    j = lax.broadcasted_iota(jnp.int32, (channels, size), 1) // SUB
    right = (lax.broadcasted_iota(jnp.int32, (channels, size), 0) == j).astype(F32)
    mixed = jnp.dot(left, eof_ref[...], precision=HIGHEST, preferred_element_type=F32)
    spread = jnp.dot(mixed, right, precision=HIGHEST, preferred_element_type=F32)
    same = (lax.broadcasted_iota(jnp.int32, (size, size), 0) - lax.broadcasted_iota(jnp.int32, (size, size), 1)) % SUB == 0
    spread = jnp.where(same, spread, 0.0)
    high = spread.astype(BF16)
    kh_ref[...] = high
    kl_ref[...] = (spread - high.astype(F32)).astype(BF16)


def second_step(
    band, parts, ids, mu_ref, mu_low, mu_high, cour_ref, cx_low, cx_high, lim_ref, lim_low, lim_high, dir_ref, dir_low, dir_high,
    m1_ref, x1_ref, e2a_ref, e2b_ref, x2a_ref, x2b_ref, box_ref, kh_ref, kl_ref, *rest,
):
    outs, (damp, east, north, m2_ref, mixed) = rest[:-5], rest[-5:]
    g = pl.program_id(0)
    fields, levels, _, width = mu_ref.shape
    rows = ids[5]
    tall = m1_ref.shape[0]
    even_row, even_col = ids[2] == 0, ids[3] == 0
    tiles = width // LANES
    inside = GROUP // SUB
    lane = lanes_of((SUB, LANES))
    sub = sublanes_of((SUB, width))
    last, first = lane == LANES - 1, lane == 0

    @pl.when(g == 0)
    def _():
        wide = lanes_of((tall, LANES))
        up = pick(even_row, e2a_ref[...], e2b_ref[...])
        down = pick(even_row, e2b_ref[...], e2a_ref[...])
        m2_ref[...] = jnp.where(wide % 2 == 1, up, -pltpu.roll(down, 2, 1))

    lims = [(lim_low, 0)] + [(lim_ref, SUB * t) for t in range(inside)] + [(lim_high, 0)]
    dirs = [(dir_low, 0)] + [(dir_ref, SUB * t) for t in range(inside)] + [(dir_high, 0)]
    mus = [(mu_low, 0)] + [(mu_ref, SUB * t) for t in range(inside)] + [(mu_high, 0)]
    cxs = [(cx_low, 0)] + [(cour_ref, SUB * t) for t in range(inside)] + [(cx_high, 0)]
    for t in range(inside + 2):
        put = slice(SUB * t, SUB * (t + 1))
        ref, r = dirs[t]
        east[put] = ref[0, 0, r : r + SUB].astype(F32)
        if 0 < t <= inside:
            north[SUB * (t - 1) : SUB * t] = ref[0, 1, r : r + SUB].astype(F32)
        ref, r = lims[t]
        for f in range(fields):
            damp[f, put] = 0.5 + 0.5 * ref[0, f, r : r + SUB].astype(F32)

    base = band * tall + g * GROUP
    starts = [jnp.maximum(base - SUB, 0)] + [base + SUB * t for t in range(inside)] + [jnp.minimum(base + GROUP, rows - SUB)]
    bands = [s // tall for s in starts]
    places = [lax.rem(s, tall) for s in starts]
    at_start = base == 0
    at_end = base + GROUP == rows
    lat_at = ids[7]
    box_lats = box_ref.shape[1] // (fields * levels * parts)
    away = (lane - lat_at) & (LANES - 1)
    piece = away // box_lats
    total = parts * box_lats
    span = fields * levels * box_lats // LANES
    inner = [((lane + LANES * k - lat_at) >= 0) & ((lane + LANES * k - lat_at) < total) for k in range(tiles)]

    def channel_group(level, carry):
        for f in range(fields):
            slot = level * fields + f
            vals, damped, px, qx = [], [], [], []
            for t in range(inside + 2):
                ref, r = mus[t]
                value = ref[f, level, r : r + SUB]
                fix = pltpu.roll(m1_ref[rows_at(places[t])], (126 - 2 * slot - 64 * bands[t]) & (LANES - 1), 1)
                pieces = split(value)
                pieces[-1] = pieces[-1] + jnp.where(last, fix, 0.0)
                pieces[0] = pieces[0] + jnp.where(first, fix, 0.0)
                value = jnp.concatenate(pieces, axis=1)
                if t == 1:
                    value = value + jnp.where((sub == 0) & at_start, x1_ref[level, fields + f : fields + f + 1], 0.0)
                if t == inside:
                    value = value + jnp.where((sub == SUB - 1) & at_end, x1_ref[level, f : f + 1], 0.0)
                ref, r = cxs[t]
                weighed = value * damp[f, SUB * t : SUB * (t + 1)]
                p, q = x_fluxes(weighed, ref[0, 0, level, r : r + SUB], east[SUB * t : SUB * (t + 1)])
                vals.append(value)
                damped.append(weighed)
                px.append(p)
                qx.append(q)
            halo_low = pick(even_col, x2b_ref[level, fields + f : fields + f + 1], x2a_ref[level, fields + f : fields + f + 1])
            halo_high = pick(even_col, x2a_ref[level, f : f + 1], x2b_ref[level, f : f + 1])
            qx[0] = jnp.where(at_start, jnp.broadcast_to(halo_low, (SUB, width)), qx[0])
            px[-1] = jnp.where(at_end, jnp.broadcast_to(halo_high, (SUB, width)), px[-1])
            for t in range(inside):
                mine = slice(SUB * t, SUB * (t + 1))
                up, down = shifted(px[t + 1], px[t + 2], qx[t], qx[t + 1])
                halo = pltpu.roll(m2_ref[rows_at(places[t + 1])], (126 - 2 * slot - 64 * bands[t + 1]) & (LANES - 1), 1)
                new, _, _ = stencil(
                    vals[t + 1], px[t + 1], qx[t + 1], up, down, damped[t + 1], cour_ref[0, 1, level, mine], north[mine], halo, -halo
                )
                gathered = jnp.zeros((SUB, LANES), F32)
                for r in range(parts):
                    block = r * span + f * levels * box_lats // LANES
                    begin = (f * levels * box_lats) % LANES + level * box_lats
                    source = box_ref[mine, block * LANES : (block + 1) * LANES]
                    moved = pltpu.roll(source, (lat_at + box_lats * r - begin) & (LANES - 1), 1)
                    gathered = jnp.where(piece == r, moved, gathered)
                put = rows_at((f * levels + level) * SUB)
                for k in range(tiles):
                    mixed[t, put, k * LANES : (k + 1) * LANES] = new[k] + jnp.where(inner[k], gathered, 0.0)
        return carry

    lax.fori_loop(0, levels, channel_group, 0)

    channels = fields * levels
    share = channels // parts
    per = len(outs) // parts
    depth = share // per
    for v in range(inside // 2):
        both = []
        for t in (2 * v, 2 * v + 1):
            full = mixed[t]
            high = full.astype(BF16)
            low = (full - high.astype(F32)).astype(BF16)
            result = jnp.dot(kh_ref[...], high, preferred_element_type=F32)
            result += jnp.dot(kl_ref[...], high, preferred_element_type=F32)
            result += jnp.dot(kh_ref[...], low, preferred_element_type=F32)
            both.append(result)
        for c in range(channels):
            at = slice(c * SUB, (c + 1) * SUB)
            pair = jnp.concatenate([both[0][at], both[1][at]], axis=0).astype(BF16)
            outs[(c // share) * per + (c % share) // depth][c % depth, 2 * SUB * v : 2 * SUB * (v + 1)] = pair


def coarse_sums(ids, nest_ref, out_ref, held):
    channels, fine_lat, fine_lon = nest_ref.shape
    lon = ids[1] * fine_lon + lax.broadcasted_iota(jnp.int32, (fine_lat, fine_lon), 1)
    lat = ids[0] * fine_lat + lax.broadcasted_iota(jnp.int32, (fine_lat, fine_lon), 0)
    edge = (lon < RATIO) | (lon >= RATIO * BOXX - RATIO) | (lat < RATIO) | (lat >= RATIO * BOXY - RATIO)
    weight = jnp.where(edge, 1.0, 1.0 / (RATIO * RATIO)).astype(F32)
    for c in range(channels):
        held[c * fine_lat : (c + 1) * fine_lat] = nest_ref[c] * weight
    count = channels * fine_lat // RATIO
    sums = held[pl.ds(0, count, stride=RATIO)]
    for a in range(1, RATIO):
        sums = sums + held[pl.ds(a, count, stride=RATIO)]
    shape = (fine_lon // RATIO, fine_lon)
    select = (lax.broadcasted_iota(jnp.int32, shape, 1) // RATIO == lax.broadcasted_iota(jnp.int32, shape, 0)).astype(F32)
    out_ref[...] = lax.dot_general(select, sums, NT, precision=HIGHEST, preferred_element_type=F32)


def arrange(masks, ids, near_ref, far_ref, out_ref, box):
    half, slab, wide = near_ref.shape
    rows = out_ref.shape[0]
    for p, (row_mask, col_mask) in enumerate(masks):
        at = pl.multiple_of((ids[1] ^ col_mask) * slab, SUB)
        to = pl.multiple_of((ids[0] ^ row_mask) * wide, LANES)
        box[pl.ds(at, slab), pl.ds(to, wide)] = near_ref[p] if p < half else far_ref[p - half]
    height = box.shape[0]
    away = ids[6]
    row = lax.broadcasted_iota(jnp.int32, (rows, LANES), 0) - away
    inside = (row >= 0) & (row < height)
    turn = lax.rem(lax.rem(away, height) + height, height)
    for k in range(box.shape[1] // LANES):
        at = slice(k * LANES, (k + 1) * LANES)
        out_ref[:, at] = jnp.where(inside, pltpu.roll(box[:, at], turn, 0)[:rows], 0.0)


def lat_filter_part(start, height, count, parts, cols, ids, *refs):
    pieces, filt, outs = refs[:parts], refs[parts], refs[parts + 1 :]
    lat_block = pieces[0].shape[2]
    lon = pieces[0].shape[1]
    lat_part = filt.shape[0] // cols
    step = 2
    for p in range(count // step):
        right = [ref[step * p : step * (p + 1)].reshape(step * lon, lat_block) for ref in pieces]
        for s0 in range(0, cols, 4):
            acc = None
            for r in range(parts):
                at = pl.ds(pl.multiple_of((ids[0] ^ r) * lat_block, LANES), lat_block)
                left = jnp.concatenate(
                    [
                        filt[pl.ds(pl.multiple_of((ids[1] ^ s) * lat_part + start, 16), height), at]
                        for s in range(s0, min(s0 + 4, cols))
                    ],
                    axis=0,
                )
                term = lax.dot_general(left, right[r], NT, preferred_element_type=F32)
                acc = term if acc is None else acc + term
            for s in range(s0, min(s0 + 4, cols)):
                for c in range(step):
                    value = acc[(s - s0) * height : (s - s0 + 1) * height, c * lon : (c + 1) * lon]
                    outs[s][step * p + c] = value.astype(BF16)


def lon_filter_part(half, height, cols, parts, n_first, aliased, owners, ids, *refs):
    firsts = refs[:n_first]
    lasts = refs[n_first : n_first + cols]
    filters = refs[n_first + cols : n_first + cols + 2 * parts]
    rest = refs[n_first + cols + 2 * parts + (1 if aliased else 0) :]
    out, lines, stage, sem = rest
    channels, _, lon = lasts[0].shape
    wide = lines.shape[1] // cols
    rows = channels * height
    block = filters[0].shape[0]
    strips = block // LANES

    def flush(j, k):
        side = ids[8] if j % 2 == 0 else 1 - ids[8]
        even, odd = owners[j // 2]
        owner = (ids[0] ^ jnp.where(side == 0, even, odd)) * 2 + side
        at = pl.ds(pl.multiple_of(owner * block + k * LANES, LANES), LANES)
        slot = j % 4
        return pltpu.make_async_copy(stage.at[slot, k], out.at[pl.ds(half * rows, rows), at], sem.at[slot, k])

    for s in range(cols):
        base = pl.multiple_of((ids[1] ^ s) * wide, LANES)
        for c in range(channels):
            put = slice(c * height, (c + 1) * height)
            for b in range(wide // lon - 1):
                groups = n_first // cols // (wide // lon - 1)
                each = channels // groups
                ref = firsts[(b * groups + c // each) * cols + s]
                lines[put, pl.ds(base + b * lon, lon)] = ref[c % each, half * height : (half + 1) * height]
            lines[put, pl.ds(base + wide - lon, lon)] = lasts[s][c]
    for p in range(parts):
        right = jnp.concatenate([filters[2 * p][...], filters[2 * p + 1][...]], axis=0)
        acc = lax.dot_general(lines[...], right, NT, preferred_element_type=F32)
        for j in (2 * p, 2 * p + 1):
            for k in range(strips):
                if j >= 4:
                    flush(j - 4, k).wait()
                begin = (j % 2) * block + k * LANES
                for c in range(channels):
                    stage[j % 4, k, pl.ds(c, height, stride=channels), :] = acc[c * height : (c + 1) * height, begin : begin + LANES]
                flush(j, k).start()
    for j in range(max(0, 2 * parts - 4), 2 * parts):
        for k in range(strips):
            flush(j, k).wait()


def swap(value, axis, mask):
    count = lax.axis_size(axis)
    return lax.ppermute(value, axis, [(i, i ^ mask) for i in range(count)])


def neighbours(value, axis, parity):
    count = lax.axis_size(axis)
    pairs = []
    for i in range(parity, count - 1, 2):
        pairs += [(i, i + 1), (i + 1, i)]
    return lax.ppermute(value, axis, pairs)


def shape_of(shape, dtype=F32):
    return jax.ShapeDtypeStruct(shape, dtype)


def whole(shape):
    return pl.BlockSpec(shape, lambda *_: (0,) * len(shape))


VMEM_SPEC = pl.BlockSpec(memory_space=pltpu.VMEM)
SMEM_SPEC = pl.BlockSpec(memory_space=pltpu.SMEM)
ANY_SPEC = pl.BlockSpec(memory_space=pl.ANY)


def shards(final_sens, courant, limiter, directions, nest_sens, box_lon, box_lat, eof, lat_filter, lon_filter):
    channels, lon_block, lat_block = final_sens.shape
    fields, levels = limiter.shape[1], courant.shape[2]
    rows_count, cols_count = lax.axis_size("row"), lax.axis_size("col")
    me_row, me_col = lax.axis_index("row"), lax.axis_index("col")
    ids = jnp.stack(
        [
            me_row,
            me_col,
            me_row % 2,
            me_col % 2,
            me_row * 0,
            me_row * 0 + lon_block,
            box_lon[0] - me_col * lon_block,
            box_lat[0] - me_row * lat_block,
            me_col % 2,
        ]
    ).astype(jnp.int32)
    lat_part = lat_filter.shape[0] // cols_count
    share = channels // rows_count
    tall = min(BAND, lon_block)
    n_bands = lon_block // tall

    height = lon_filter.shape[0] // 2
    gathered = [lax.dynamic_slice_in_dim(lon_filter, (me_col % 2) * height, height, 0)]
    orders = [2**k for k in range(10) if 2**k < rows_count]
    turns = (orders, orders[::-1])
    owners = [(0, 0)]

    def gather(stage, pieces):
        pairs = []
        for i in range(rows_count * cols_count):
            row, col = divmod(i, cols_count)
            pairs.append((i, (row ^ turns[col % 2][stage]) * cols_count + col))
        return [lax.ppermute(piece, ("row", "col"), pairs) for piece in pieces]

    direct = []
    for stage in range(len(orders)):
        direct += gather(stage, gathered[:1])

    nest = jnp.transpose(nest_sens, (0, 2, 1))
    fine_lat, fine_lon = nest.shape[1:]
    coarse = pl.pallas_call(
        coarse_sums,
        out_shape=shape_of((fine_lon // RATIO, channels * fine_lat // RATIO)),
        in_specs=[SMEM_SPEC, VMEM_SPEC],
        out_specs=VMEM_SPEC,
        scratch_shapes=[pltpu.VMEM((channels * fine_lat, fine_lon), F32)],
        name="coarse",
    )(ids, nest)
    masks = [(0, 0)]
    stages = [("col", m) for m in (2**k for k in range(1, 10)) if m < cols_count]
    stages += [("row", m) for m in (2**k for k in range(10)) if m < rows_count]
    stages += [("col", 1)]

    def spread(held, count, last=False):
        nonlocal stages, masks
        for axis, mask in stages[:count]:
            other = swap(held, axis, mask)
            held = (held, other) if last else jnp.concatenate([held, other], axis=0)
            masks = masks + [(r ^ mask, c) if axis == "row" else (r, c ^ mask) for r, c in masks]
        stages = stages[count:]
        return held

    def after(value, *others):
        return lax.optimization_barrier((value, *others))[0]

    held = spread(coarse[None], 2)

    mu = final_sens.reshape(fields, levels, lon_block, lat_block)
    call = pl.pallas_call(
        first_step,
        grid=(levels,),
        out_shape=(
            shape_of(mu.shape),
            shape_of((tall, LANES)),
            shape_of((tall, LANES)),
            shape_of((tall, LANES)),
            shape_of((levels + 1, 2 * fields, lat_block)),
            shape_of((levels, 2 * fields, lat_block)),
            shape_of((levels, 2 * fields, lat_block)),
        ),
        in_specs=[
            pl.BlockSpec((fields, 1, lon_block, lat_block), lambda l: (0, l, 0, 0)),
            pl.BlockSpec((2, 2, 1, lon_block, lat_block), lambda l: (0, 0, l, 0, 0)),
            whole(limiter.shape),
            whole(directions.shape),
        ],
        out_specs=(
            pl.BlockSpec((fields, 1, lon_block, lat_block), lambda l: (0, l, 0, 0)),
            whole((tall, LANES)),
            whole((tall, LANES)),
            whole((tall, LANES)),
            whole((levels + 1, 2 * fields, lat_block)),
            whole((levels, 2 * fields, lat_block)),
            whole((levels, 2 * fields, lat_block)),
        ),
        scratch_shapes=[
            pltpu.VMEM((fields, lon_block, lat_block), F32),
            pltpu.VMEM((lon_block, lat_block), F32),
            pltpu.VMEM((lon_block, lat_block), F32),
            pltpu.VMEM((fields, lon_block, LANES), F32),
        ],
        name="first_step",
    )
    mu1, ef, em, ew, xr, xm, xw = call(mu, courant, limiter, directions)
    held = spread(after(held, ef), 1)
    efa, efb = neighbours(ef, "row", 0), neighbours(ef, "row", 1)
    xra, xrb = neighbours(xr, "col", 0), neighbours(xr, "col", 1)
    held = spread(after(held, efa, efb, xra, xrb), len(stages) - 1)
    size = channels * SUB
    call = pl.pallas_call(
        functools.partial(rims, lon_block, rows_count),
        out_shape=(
            shape_of(ef.shape),
            shape_of(xm.shape),
            shape_of(ef.shape),
            shape_of(xm.shape),
            shape_of((size, size), BF16),
            shape_of((size, size), BF16),
        ),
        in_specs=[SMEM_SPEC] + [VMEM_SPEC] * 9,
        out_specs=(VMEM_SPEC,) * 6,
        name="rims",
    )
    e2, x2, m1, x1, kh, kl = call(ids, efa, efb, xra, xrb, em, ew, xm, xw, eof)
    e2a, e2b = neighbours(e2, "row", 0), neighbours(e2, "row", 1)
    x2a, x2b = neighbours(x2, "col", 0), neighbours(x2, "col", 1)
    held = spread(held, 1, True)
    box = pl.pallas_call(
        functools.partial(arrange, masks),
        out_shape=shape_of((lon_block, rows_count * coarse.shape[1])),
        in_specs=[SMEM_SPEC, VMEM_SPEC, VMEM_SPEC],
        out_specs=VMEM_SPEC,
        scratch_shapes=[pltpu.VMEM((cols_count * coarse.shape[0], rows_count * coarse.shape[1]), F32)],
        name="arrange",
    )(ids, *held)

    groups = tall // GROUP
    fine = GROUP // SUB
    top = lon_block // SUB - 1

    def control(band, halves, kl):
        def at(g):
            return band * groups + g

        def low(g):
            return jnp.maximum((band * groups + g) * fine - 1, 0)

        def high(g):
            return jnp.minimum((band * groups + g) * fine + fine, top)

        depth = share // halves
        return pl.pallas_call(
            functools.partial(second_step, band, rows_count),
            grid=(groups,),
            out_shape=(shape_of((depth, tall, lat_block), BF16),) * (rows_count * halves),
            in_specs=[
                SMEM_SPEC,
                pl.BlockSpec((fields, levels, GROUP, lat_block), lambda g: (0, 0, at(g), 0)),
                pl.BlockSpec((fields, levels, SUB, lat_block), lambda g: (0, 0, low(g), 0)),
                pl.BlockSpec((fields, levels, SUB, lat_block), lambda g: (0, 0, high(g), 0)),
                pl.BlockSpec((1, 2, levels, GROUP, lat_block), lambda g: (0, 0, 0, at(g), 0)),
                pl.BlockSpec((1, 1, levels, SUB, lat_block), lambda g: (0, 0, 0, low(g), 0)),
                pl.BlockSpec((1, 1, levels, SUB, lat_block), lambda g: (0, 0, 0, high(g), 0)),
                pl.BlockSpec((1, fields, GROUP, lat_block), lambda g: (0, 0, at(g), 0)),
                pl.BlockSpec((1, fields, SUB, lat_block), lambda g: (0, 0, low(g), 0)),
                pl.BlockSpec((1, fields, SUB, lat_block), lambda g: (0, 0, high(g), 0)),
                pl.BlockSpec((1, 2, GROUP, lat_block), lambda g: (0, 0, at(g), 0)),
                pl.BlockSpec((1, 1, SUB, lat_block), lambda g: (0, 0, low(g), 0)),
                pl.BlockSpec((1, 1, SUB, lat_block), lambda g: (0, 0, high(g), 0)),
                whole(m1.shape),
                whole(x1.shape),
                whole(e2.shape),
                whole(e2.shape),
                whole(x2.shape),
                whole(x2.shape),
                pl.BlockSpec((GROUP, box.shape[1]), lambda g: (at(g), 0)),
                whole(kh.shape),
                whole(kl.shape),
            ],
            out_specs=(pl.BlockSpec((depth, GROUP, lat_block), lambda g: (0, g, 0)),) * (rows_count * halves),
            scratch_shapes=[
                pltpu.VMEM((fields, GROUP + 2 * SUB, lat_block), F32),
                pltpu.VMEM((GROUP + 2 * SUB, lat_block), F32),
                pltpu.VMEM((GROUP, lat_block), F32),
                pltpu.VMEM((tall, LANES), F32),
                pltpu.VMEM((fine, channels * SUB, lat_block), F32),
            ],
            name="second_step",
        )(ids, mu1, mu1, mu1, courant, courant, courant, limiter, limiter, limiter, directions, directions, directions,
          m1, x1, e2a, e2b, x2a, x2b, box, kh, kl)

    def to_rows(pieces):
        return [pieces[0]] + [swap(pieces[s], "row", s) for s in range(1, rows_count)]

    def smooth(pieces, start, height, token):
        count = pieces[0].shape[0]
        filt = lat_filter if token is None else after(lat_filter, token)
        call = pl.pallas_call(
            functools.partial(lat_filter_part, start, height, count, rows_count, cols_count),
            out_shape=(shape_of((count, height, tall), BF16),) * cols_count,
            in_specs=[SMEM_SPEC] + [VMEM_SPEC] * (rows_count + 1),
            out_specs=(VMEM_SPEC,) * cols_count,
            name="lat_filter",
        )
        outs = call(ids, *pieces, filt)
        moved = {s: swap(outs[s], "col", s) for s in range(cols_count - 1, 0, -1)}
        return [outs[0]] + [moved[s] for s in range(1, cols_count)], outs[-1]

    firsts = []
    sent = []
    order = None
    for band in range(n_bands):
        final = band == n_bands - 1
        halves = 1 if final else 2
        kl = kl if order is None else after(kl, order)
        outs = control(band, halves, kl)
        order = outs[-1]
        for h in range(halves):
            sent.append(to_rows([outs[s * halves + h] for s in range(rows_count)]))

    token = None
    for pieces in sent[:-1]:
        moved, token = smooth(pieces, 0, lat_part, token)
        firsts += moved
    half_height = lat_part // 2
    lasts = []
    for h in range(2):
        early = token
        moved, token = smooth(sent[-1], h * half_height, half_height, token)
        lasts.append(moved)
    for stage in range(len(orders)):
        gathered += [direct[stage]] + gather(stage, [after(piece, early) for piece in gathered[1:]])
        owners += [(a ^ turns[0][stage], b ^ turns[1][stage]) for a, b in owners]
    filters = []
    for piece in gathered:
        filters += [piece, swap(after(piece, token), "col", 1)]

    n_lon = cols_count * lon_block
    rows = share * half_height
    if lon_block % LANES:
        stacked = jnp.stack([jnp.concatenate([lasts[0][s], lasts[1][s]], axis=1) for s in range(cols_count)])
        lines = jnp.take(stacked, me_col ^ jnp.arange(cols_count), axis=0)
        lines = jnp.transpose(lines, (2, 1, 0, 3)).reshape(lat_part, share, n_lon)
        whole_filter = jnp.zeros((n_lon, n_lon), BF16)
        for j, piece in enumerate(filters):
            side = me_col % 2 if j % 2 == 0 else 1 - me_col % 2
            owner = (me_row ^ jnp.where(side == 0, *owners[j // 2])) * 2 + side
            whole_filter = lax.dynamic_update_slice_in_dim(whole_filter, piece, owner * height, 0)
        return jnp.einsum("lci,oi->lco", lines, whole_filter, preferred_element_type=F32)
    out = None
    for h in range(2):
        aliased = out is not None
        operands = (ids, *firsts, *lasts[h], *filters) + ((out,) if aliased else ())
        call = pl.pallas_call(
            functools.partial(lon_filter_part, h, half_height, cols_count, rows_count, len(firsts), aliased, owners),
            out_shape=shape_of((2 * rows, n_lon)),
            in_specs=[SMEM_SPEC] + [VMEM_SPEC] * (len(firsts) + cols_count + 2 * rows_count) + [ANY_SPEC] * aliased,
            out_specs=ANY_SPEC,
            scratch_shapes=[
                pltpu.VMEM((rows, n_lon), BF16),
                pltpu.VMEM((4, height // LANES, rows, LANES), F32),
                pltpu.SemaphoreType.DMA((4, height // LANES)),
            ],
            input_output_aliases={len(operands) - 1: 0} if aliased else {},
            name="lon_filter",
        )
        out = call(*operands)
    return out.reshape(lat_part, share, n_lon)


def solution(mesh):
    placed = (
        P(None, "col", "row"),
        P(None, None, None, "col", "row"),
        P(None, None, "col", "row"),
        P(None, None, "col", "row"),
        P(None, "col", "row"),
        P(),
        P(),
        P(),
        P(),
        P("row", None),
    )
    return jax.shard_map(shards, mesh=mesh, in_specs=placed, out_specs=P("col", "row", None), check_vma=False)
```

```python
import functools

import jax
import jax.numpy as jnp
from jax import lax
from jax.experimental import pallas as pl
from jax.experimental.pallas import tpu as pltpu
from jax.sharding import PartitionSpec as P


RATIO = 3
BOXX = 256
BOXY = 32
LANES = 128
SUB = 8
BAND = 128
GROUP = 128
GROUP_ONE = 128
UNROLL_ONE = 2
UNROLL_TWO = 2
F32 = jnp.float32
BF16 = jnp.bfloat16
NT = (((1,), (1,)), ((), ()))
HIGHEST = lax.Precision.HIGHEST


def lanes_of(shape):
    return lax.broadcasted_iota(jnp.int32, shape, len(shape) - 1)


def sublanes_of(shape):
    return lax.broadcasted_iota(jnp.int32, shape, len(shape) - 2)


def split(value):
    return [value[:, k * LANES : (k + 1) * LANES] for k in range(value.shape[1] // LANES)]


def rows_at(start):
    return pl.ds(pl.multiple_of(start, SUB), SUB)


def x_fluxes(damped, coef, east):
    flux = coef * damped
    part = east * flux
    return part, flux - part


def stencil(mu, px, qx, up_x, down_x, damped, coef, north, halo_up, halo_down):
    flux = coef * damped
    py = north * flux
    qy = flux - py
    base = mu - px + qx - py + qy + up_x - down_x
    lane = lanes_of((SUB, LANES))
    last, first = lane == LANES - 1, lane == 0
    py, qy, base = split(py), split(qy), split(base)
    rolled_up = [pltpu.roll(v, LANES - 1, 1) for v in py]
    rolled_down = [pltpu.roll(v, 1, 1) for v in qy]
    count = len(base)
    out = []
    for k in range(count):
        above = rolled_up[k + 1] if k + 1 < count else halo_up
        below = rolled_down[k - 1] if k > 0 else halo_down
        out.append(base[k] + jnp.where(last, above, rolled_up[k]) - jnp.where(first, below, rolled_down[k]))
    return out, py, qy


def shifted(px_here, px_next, qx_prev, qx_here):
    sub = sublanes_of(px_here.shape)
    up = jnp.where(sub == SUB - 1, pltpu.roll(px_next, SUB - 1, 0), pltpu.roll(px_here, SUB - 1, 0))
    down = jnp.where(sub == 0, pltpu.roll(qx_prev, 1, 0), pltpu.roll(qx_here, 1, 0))
    return up, down


def first_step(mu_ref, cour_ref, lim_ref, dir_ref, out_ref, ef_ref, em_ref, ew_ref, xr_ref, xm_ref, xw_ref, damp, east, north, rim):
    level = pl.program_id(0)
    fields, _, rows, width = mu_ref.shape
    tiles = width // LANES
    size = min(GROUP_ONE, rows)
    groups = rows // size
    tall = ef_ref.shape[0]
    lane = lanes_of((SUB, LANES))
    last = lane == LANES - 1
    edge = slice((tiles - 1) * LANES, tiles * LANES)

    @pl.when(level == 0)
    def _():
        for ref in (ef_ref, em_ref, ew_ref, xr_ref):
            ref[...] = jnp.zeros_like(ref)

        def prepare(tile, carry):
            at = rows_at(tile * SUB)
            east[at] = dir_ref[1, 0, at].astype(F32)
            north[at] = dir_ref[1, 1, at].astype(F32)
            side = jnp.where(last, 1 - dir_ref[0, 1, at, edge], dir_ref[0, 1, at, :LANES]).astype(F32)
            for f in range(fields):
                damp[f, at] = 0.5 + 0.5 * lim_ref[1, f, at].astype(F32)
                flag = jnp.where(last, lim_ref[0, f, at, edge], lim_ref[0, f, at, :LANES]).astype(F32)
                rim[f, at] = side * (0.5 + 0.5 * flag)
            return carry

        lax.fori_loop(0, rows // SUB, prepare, 0)

    def group(index, carry):
        f, g = index // groups, lax.rem(index, groups)
        base = g * size
        inside = size // SUB
        starts = [jnp.maximum(base - SUB, 0)] + [base + SUB * t for t in range(inside)] + [jnp.minimum(base + size, rows - SUB)]
        keep_low = jnp.where(g > 0, 1.0, 0.0).astype(F32)
        keep_high = jnp.where(g < groups - 1, 1.0, 0.0).astype(F32)
        slot = level * fields + f
        none = jnp.zeros((SUB, LANES), F32)
        mus = [mu_ref[f, 0, rows_at(s)] for s in starts]
        damped = [m * damp[f, rows_at(s)] for m, s in zip(mus, starts)]
        pq = [x_fluxes(m, cour_ref[1, 0, 0, rows_at(s)], east[rows_at(s)]) for m, s in zip(damped, starts)]
        px = [v[0] for v in pq]
        qx = [v[1] for v in pq]
        qx[0] = qx[0] * keep_low
        px[-1] = px[-1] * keep_high
        for t in range(inside):
            at = rows_at(starts[t + 1])
            up, down = shifted(px[t + 1], px[t + 2], qx[t], qx[t + 1])
            new, py, qy = stencil(
                mus[t + 1], px[t + 1], qx[t + 1], up, down, damped[t + 1], cour_ref[1, 1, 0, at], north[at], none, none
            )
            for k in range(tiles):
                out_ref[f, 0, at, k * LANES : (k + 1) * LANES] = new[k]
            band = starts[t + 1] // tall
            turn = (2 * slot + 1 + band * 64) & (LANES - 1)
            mine = (lane // 2) == slot + 32 * band
            weight = jnp.where(last, cour_ref[0, 1, 0, at, edge], cour_ref[0, 1, 0, at, :LANES]) * rim[f, at]
            place = rows_at(lax.rem(starts[t + 1], tall))
            values = (jnp.where(last, qy[-1], py[0]), jnp.where(last, new[-1], new[0]), weight)
            for ref, value in zip((ef_ref, em_ref, ew_ref), values):
                ref[place] = jnp.where(mine, pltpu.roll(value, turn, 1), ref[place])
        return carry

    def groups_at(index, carry):
        for u in range(UNROLL_ONE):
            group(index + u * (fields // UNROLL_ONE) * groups, carry)
        return carry

    lax.fori_loop(0, fields * groups // UNROLL_ONE, groups_at, 0)

    low, high = slice(0, SUB), slice(rows - SUB, rows)
    for f in range(fields):
        slot = level * fields + f
        turn = 2 * slot + 1
        mine = (lane // 2) == slot
        px, _ = x_fluxes(mu_ref[f, 0, low] * damp[f, low], cour_ref[1, 0, 0, low], east[low])
        _, qx = x_fluxes(mu_ref[f, 0, high] * damp[f, high], cour_ref[1, 0, 0, high], east[high])
        xr_ref[level, f : f + 1] = px[:1]
        xr_ref[level, fields + f : fields + f + 1] = qx[SUB - 1 :]
        px_edge = pltpu.roll(jnp.where(last, px[:, edge], px[:, :LANES]), turn, 1)
        qx_edge = pltpu.roll(jnp.where(last, qx[:, edge], qx[:, :LANES]), turn, 1)
        corner = xr_ref.shape[0] - 1
        xr_ref[corner, 0:1, :LANES] = jnp.where(mine, px_edge, jnp.broadcast_to(xr_ref[corner, 0:1, :LANES], (SUB, LANES)))[:1]
        xr_ref[corner, 4:5, :LANES] = jnp.where(mine, qx_edge, jnp.broadcast_to(xr_ref[corner, 4:5, :LANES], (SUB, LANES)))[SUB - 1 :]
        xm_ref[level, f : f + 1] = out_ref[f, 0, low][:1]
        xm_ref[level, fields + f : fields + f + 1] = out_ref[f, 0, high][SUB - 1 :]
        for at, part, row in ((low, 0, 0), (high, 1, SUB - 1)):
            way = dir_ref[0, 0, at].astype(F32)
            way = 1.0 - way if part else way
            value = way * (0.5 + 0.5 * lim_ref[0, f, at].astype(F32)) * cour_ref[0, 0, 0, at]
            xw_ref[level, part * fields + f : part * fields + f + 1] = value[row : row + 1]


def pick(first, a, b):
    return jnp.where(first, a, b)


def rims(rows, parts, ids, efa_ref, efb_ref, xra_ref, xrb_ref, em_ref, ew_ref, xm_ref, xw_ref, eof_ref, e2_ref, x2_ref, m1_ref, x1_ref, kh_ref, kl_ref):
    me_row = ids[0]
    even_row, even_col = ids[2] == 0, ids[3] == 0
    levels, twice, width = xm_ref.shape
    fields = twice // 2
    tiles = width // LANES
    tall = em_ref.shape[0]
    top_band = (rows - 1) // tall
    lane = lanes_of((tall, LANES))
    sub = sublanes_of((tall, LANES))
    up = pick(even_row, efa_ref[...], efb_ref[...])
    down = pick(even_row, efb_ref[...], efa_ref[...])
    merged = jnp.where(lane % 2 == 1, up, -pltpu.roll(down, 2, 1))
    m1_ref[...] = merged
    fixed = em_ref[...] + jnp.where(lane % 2 == 0, pltpu.roll(up, LANES - 1, 1), -pltpu.roll(down, 1, 1))
    corner = xra_ref.shape[0] - 1
    ca, cb = xra_ref[corner, :, :LANES], xrb_ref[corner, :, :LANES]
    corner_up = pick(even_col, ca, cb)[0:1]
    corner_down = pick(even_col, cb, ca)[4:5]
    if top_band:
        corner_up = pltpu.roll(jnp.broadcast_to(corner_up, (SUB, LANES)), 64 * top_band, 1)[:1]
    fixed = fixed + jnp.where(sub == tall - 1, corner_up, 0.0) - jnp.where(sub == 0, corner_down, 0.0)
    e2_ref[...] = ew_ref[...] * fixed

    lane8 = lanes_of((twice, LANES))
    sub8 = sublanes_of((twice, LANES))
    ends = jnp.where(sub8 < fields, jnp.broadcast_to(merged[0:1], (twice, LANES)), jnp.broadcast_to(merged[tall - 1 :], (twice, LANES)))
    wide = sublanes_of((twice, width))
    for level in range(levels):
        a, b = xra_ref[level], xrb_ref[level]
        halo = jnp.where(wide < fields, pick(even_col, a, b), -pick(even_col, b, a))
        x1_ref[level] = halo
        target = 2 * (level * fields + sub8 % fields) + 1 + jnp.where(sub8 >= fields, 64 * top_band, 0)
        at_last = jnp.sum(jnp.where(lane8 == target, ends, 0.0), axis=1, keepdims=True)
        at_first = jnp.sum(jnp.where(lane8 == (target + 1) % LANES, ends, 0.0), axis=1, keepdims=True)
        here = split(xm_ref[level] + pltpu.roll(halo, fields, 0))
        here[-1] = here[-1] + jnp.where(lane8 == LANES - 1, at_last, 0.0)
        here[0] = here[0] + jnp.where(lane8 == 0, at_first, 0.0)
        for k in range(tiles):
            at = slice(k * LANES, (k + 1) * LANES)
            x2_ref[level, :, at] = xw_ref[level, :, at] * here[k]

    channels = eof_ref.shape[0]
    size = kh_ref.shape[0]
    share = channels // parts
    i = lax.broadcasted_iota(jnp.int32, (size, channels), 0) // SUB
    chosen = ((i // share) ^ me_row) * share + i % share
    left = (lax.broadcasted_iota(jnp.int32, (size, channels), 1) == chosen).astype(F32)
    j = lax.broadcasted_iota(jnp.int32, (channels, size), 1) // SUB
    right = (lax.broadcasted_iota(jnp.int32, (channels, size), 0) == j).astype(F32)
    mixed = jnp.dot(left, eof_ref[...], precision=HIGHEST, preferred_element_type=F32)
    spread = jnp.dot(mixed, right, precision=HIGHEST, preferred_element_type=F32)
    same = (lax.broadcasted_iota(jnp.int32, (size, size), 0) - lax.broadcasted_iota(jnp.int32, (size, size), 1)) % SUB == 0
    spread = jnp.where(same, spread, 0.0)
    high = spread.astype(BF16)
    kh_ref[...] = high
    kl_ref[...] = (spread - high.astype(F32)).astype(BF16)


def second_step(
    band, parts, ids, mu_ref, mu_low, mu_high, cour_ref, cx_low, cx_high, lim_ref, lim_low, lim_high, dir_ref, dir_low, dir_high,
    m1_ref, x1_ref, e2a_ref, e2b_ref, x2a_ref, x2b_ref, box_ref, kh_ref, kl_ref, *rest,
):
    outs, (damp, east, north, m2_ref, mixed) = rest[:-5], rest[-5:]
    g = pl.program_id(0)
    fields, levels, _, width = mu_ref.shape
    rows = ids[5]
    tall = m1_ref.shape[0]
    even_row, even_col = ids[2] == 0, ids[3] == 0
    tiles = width // LANES
    size = mu_ref.shape[2]
    inside = size // SUB
    lane = lanes_of((SUB, LANES))
    sub = sublanes_of((SUB, width))
    last, first = lane == LANES - 1, lane == 0

    @pl.when(g == 0)
    def _():
        wide = lanes_of((tall, LANES))
        up = pick(even_row, e2a_ref[...], e2b_ref[...])
        down = pick(even_row, e2b_ref[...], e2a_ref[...])
        m2_ref[...] = jnp.where(wide % 2 == 1, up, -pltpu.roll(down, 2, 1))

    lims = [(lim_low, 0)] + [(lim_ref, SUB * t) for t in range(inside)] + [(lim_high, 0)]
    dirs = [(dir_low, 0)] + [(dir_ref, SUB * t) for t in range(inside)] + [(dir_high, 0)]
    mus = [(mu_low, 0)] + [(mu_ref, SUB * t) for t in range(inside)] + [(mu_high, 0)]
    cxs = [(cx_low, 0)] + [(cour_ref, SUB * t) for t in range(inside)] + [(cx_high, 0)]
    for t in range(inside + 2):
        put = slice(SUB * t, SUB * (t + 1))
        ref, r = dirs[t]
        east[put] = ref[0, 0, r : r + SUB].astype(F32)
        if 0 < t <= inside:
            north[SUB * (t - 1) : SUB * t] = ref[0, 1, r : r + SUB].astype(F32)
        ref, r = lims[t]
        for f in range(fields):
            damp[f, put] = 0.5 + 0.5 * ref[0, f, r : r + SUB].astype(F32)

    base = band * tall + g * size
    starts = [jnp.maximum(base - SUB, 0)] + [base + SUB * t for t in range(inside)] + [jnp.minimum(base + size, rows - SUB)]
    bands = [s // tall for s in starts]
    places = [lax.rem(s, tall) for s in starts]
    at_start = base == 0
    at_end = base + size == rows
    lat_at = ids[7]
    box_lats = box_ref.shape[1] // (fields * levels * parts)
    per_tile = LANES // box_lats
    total = parts * box_lats
    inner = [((lane + LANES * k - lat_at) >= 0) & ((lane + LANES * k - lat_at) < total) for k in range(tiles)]

    def channel(index, carry):
        f, level = index // levels, lax.rem(index, levels)
        slot = level * fields + f
        vals, damped, px, qx = [], [], [], []
        for t in range(inside + 2):
            ref, r = mus[t]
            value = ref[f, level, r : r + SUB]
            fix = pltpu.roll(m1_ref[rows_at(places[t])], (126 - 2 * slot - 64 * bands[t]) & (LANES - 1), 1)
            pieces = split(value)
            pieces[-1] = pieces[-1] + jnp.where(last, fix, 0.0)
            pieces[0] = pieces[0] + jnp.where(first, fix, 0.0)
            value = jnp.concatenate(pieces, axis=1)
            if t == 1:
                value = value + jnp.where((sub == 0) & at_start, x1_ref[level, pl.ds(fields + f, 1)], 0.0)
            if t == inside:
                value = value + jnp.where((sub == SUB - 1) & at_end, x1_ref[level, pl.ds(f, 1)], 0.0)
            ref, r = cxs[t]
            weighed = value * damp[f, SUB * t : SUB * (t + 1)]
            p, q = x_fluxes(weighed, ref[0, 0, level, r : r + SUB], east[SUB * t : SUB * (t + 1)])
            vals.append(value)
            damped.append(weighed)
            px.append(p)
            qx.append(q)
        halo_low = pick(even_col, x2b_ref[level, pl.ds(fields + f, 1)], x2a_ref[level, pl.ds(fields + f, 1)])
        halo_high = pick(even_col, x2a_ref[level, pl.ds(f, 1)], x2b_ref[level, pl.ds(f, 1)])
        qx[0] = jnp.where(at_start, jnp.broadcast_to(halo_low, (SUB, width)), qx[0])
        px[-1] = jnp.where(at_end, jnp.broadcast_to(halo_high, (SUB, width)), px[-1])
        box_tile = pl.multiple_of((index // per_tile * parts + lax.rem(index, parts)) * LANES, LANES)
        box_turn = (lat_at - lax.rem(index, per_tile) * box_lats) & (LANES - 1)
        put = rows_at(index * SUB)
        for t in range(inside):
            mine = slice(SUB * t, SUB * (t + 1))
            up, down = shifted(px[t + 1], px[t + 2], qx[t], qx[t + 1])
            halo = pltpu.roll(m2_ref[rows_at(places[t + 1])], (126 - 2 * slot - 64 * bands[t + 1]) & (LANES - 1), 1)
            new, _, _ = stencil(
                vals[t + 1], px[t + 1], qx[t + 1], up, down, damped[t + 1], cour_ref[0, 1, level, mine], north[mine], halo, -halo
            )
            moved = pltpu.roll(box_ref[mine, pl.ds(box_tile, LANES)], box_turn, 1)
            for k in range(tiles):
                mixed[t, put, k * LANES : (k + 1) * LANES] = new[k] + jnp.where(inner[k], moved, 0.0)
        return carry

    def channels_at(index, carry):
        for u in range(UNROLL_TWO):
            channel(index * UNROLL_TWO + u, carry)
        return carry

    lax.fori_loop(0, fields * levels // UNROLL_TWO, channels_at, 0)

    channels = fields * levels
    share = channels // parts
    per = len(outs) // parts
    depth = share // per
    for v in range(inside // 2):
        both = []
        for t in (2 * v, 2 * v + 1):
            full = mixed[t]
            high = full.astype(BF16)
            low = (full - high.astype(F32)).astype(BF16)
            result = jnp.dot(kh_ref[...], high, preferred_element_type=F32)
            result += jnp.dot(kl_ref[...], high, preferred_element_type=F32)
            result += jnp.dot(kh_ref[...], low, preferred_element_type=F32)
            both.append(result)
        for c in range(channels):
            at = slice(c * SUB, (c + 1) * SUB)
            pair = jnp.concatenate([both[0][at], both[1][at]], axis=0).astype(BF16)
            outs[(c // share) * per + (c % share) // depth][c % depth, 2 * SUB * v : 2 * SUB * (v + 1)] = pair


def coarse_sums(ids, nest_ref, out_ref, held):
    channels, fine_lat, fine_lon = nest_ref.shape
    lon = ids[1] * fine_lon + lax.broadcasted_iota(jnp.int32, (fine_lat, fine_lon), 1)
    lat = ids[0] * fine_lat + lax.broadcasted_iota(jnp.int32, (fine_lat, fine_lon), 0)
    edge = (lon < RATIO) | (lon >= RATIO * BOXX - RATIO) | (lat < RATIO) | (lat >= RATIO * BOXY - RATIO)
    weight = jnp.where(edge, 1.0, 1.0 / (RATIO * RATIO)).astype(F32)
    for c in range(channels):
        held[c * fine_lat : (c + 1) * fine_lat] = nest_ref[c] * weight
    count = channels * fine_lat // RATIO
    sums = held[pl.ds(0, count, stride=RATIO)]
    for a in range(1, RATIO):
        sums = sums + held[pl.ds(a, count, stride=RATIO)]
    shape = (fine_lon // RATIO, fine_lon)
    select = (lax.broadcasted_iota(jnp.int32, shape, 1) // RATIO == lax.broadcasted_iota(jnp.int32, shape, 0)).astype(F32)
    result = lax.dot_general(select, sums, NT, precision=HIGHEST, preferred_element_type=F32)
    for k, piece in enumerate(split(result)):
        out_ref[:, k * LANES : (k + 1) * LANES] = pltpu.roll(piece, (ids[0] * (fine_lat // RATIO)) & (LANES - 1), 1)


def arrange(masks, lats, ids, near_ref, far_ref, out_ref, box):
    half, slab, wide = near_ref.shape
    rows = out_ref.shape[0]
    for p, (row_mask, col_mask) in enumerate(masks):
        at = pl.multiple_of((ids[1] ^ col_mask) * slab, SUB)
        to = pl.multiple_of((ids[0] ^ row_mask) * wide, LANES)
        box[pl.ds(at, slab), pl.ds(to, wide)] = near_ref[p] if p < half else far_ref[p - half]
    height = box.shape[0]
    away = ids[6]
    row = lax.broadcasted_iota(jnp.int32, (rows, LANES), 0) - away
    inside = (row >= 0) & (row < height)
    turn = lax.rem(lax.rem(away, height) + height, height)
    parts = box.shape[1] // wide
    slot = lanes_of((height, LANES)) // lats
    for k in range(wide // LANES):
        pieces = [box[:, r * wide + k * LANES : r * wide + (k + 1) * LANES] for r in range(parts)]
        for m in range(parts):
            value = pieces[0]
            for r in range(1, parts):
                value = jnp.where((slot - m) % parts == r, pieces[r], value)
            at = (k * parts + m) * LANES
            out_ref[:, at : at + LANES] = jnp.where(inside, pltpu.roll(value, turn, 0)[:rows], 0.0)


def lat_filter_part(start, height, count, parts, cols, ids, *refs):
    pieces, filt, outs = refs[:parts], refs[parts], refs[parts + 1 :]
    lat_block = pieces[0].shape[2]
    lon = pieces[0].shape[1]
    lat_part = filt.shape[0] // cols
    step = 2
    for p in range(count // step):
        right = [ref[step * p : step * (p + 1)].reshape(step * lon, lat_block) for ref in pieces]
        for s0 in range(0, cols, 4):
            acc = None
            for r in range(parts):
                at = pl.ds(pl.multiple_of((ids[0] ^ r) * lat_block, LANES), lat_block)
                left = jnp.concatenate(
                    [
                        filt[pl.ds(pl.multiple_of((ids[1] ^ s) * lat_part + start, 16), height), at]
                        for s in range(s0, min(s0 + 4, cols))
                    ],
                    axis=0,
                )
                term = lax.dot_general(left, right[r], NT, preferred_element_type=F32)
                acc = term if acc is None else acc + term
            for s in range(s0, min(s0 + 4, cols)):
                for c in range(step):
                    value = acc[(s - s0) * height : (s - s0 + 1) * height, c * lon : (c + 1) * lon]
                    outs[s][step * p + c] = value.astype(BF16)


def lon_filter_part(half, height, cols, parts, n_first, aliased, owners, ids, *refs):
    firsts = refs[:n_first]
    lasts = refs[n_first : n_first + cols]
    filters = refs[n_first + cols : n_first + cols + 2 * parts]
    rest = refs[n_first + cols + 2 * parts + (1 if aliased else 0) :]
    out, lines, stage, sem = rest
    channels, _, lon = lasts[0].shape
    wide = lines.shape[1] // cols
    rows = channels * height
    block = filters[0].shape[0]
    strips = block // LANES

    def flush(j, k):
        side = ids[8] if j % 2 == 0 else 1 - ids[8]
        even, odd = owners[j // 2]
        owner = (ids[0] ^ jnp.where(side == 0, even, odd)) * 2 + side
        at = pl.ds(pl.multiple_of(owner * block + k * LANES, LANES), LANES)
        slot = j % 4
        return pltpu.make_async_copy(stage.at[slot, k], out.at[pl.ds(half * rows, rows), at], sem.at[slot, k])

    for s in range(cols):
        base = pl.multiple_of((ids[1] ^ s) * wide, LANES)
        for c in range(channels):
            put = slice(c * height, (c + 1) * height)
            for b in range(wide // lon - 1):
                groups = n_first // cols // (wide // lon - 1)
                each = channels // groups
                ref = firsts[(b * groups + c // each) * cols + s]
                lines[put, pl.ds(base + b * lon, lon)] = ref[c % each, half * height : (half + 1) * height]
            lines[put, pl.ds(base + wide - lon, lon)] = lasts[s][c]
    for p in range(parts):
        right = jnp.concatenate([filters[2 * p][...], filters[2 * p + 1][...]], axis=0)
        acc = lax.dot_general(lines[...], right, NT, preferred_element_type=F32)
        for j in (2 * p, 2 * p + 1):
            for k in range(strips):
                if j >= 4:
                    flush(j - 4, k).wait()
                begin = (j % 2) * block + k * LANES
                for c in range(channels):
                    stage[j % 4, k, pl.ds(c, height, stride=channels), :] = acc[c * height : (c + 1) * height, begin : begin + LANES]
                flush(j, k).start()
    for j in range(max(0, 2 * parts - 4), 2 * parts):
        for k in range(strips):
            flush(j, k).wait()


def swap(value, axis, mask):
    count = lax.axis_size(axis)
    return lax.ppermute(value, axis, [(i, i ^ mask) for i in range(count)])


def neighbours(value, axis, parity):
    count = lax.axis_size(axis)
    pairs = []
    for i in range(parity, count - 1, 2):
        pairs += [(i, i + 1), (i + 1, i)]
    return lax.ppermute(value, axis, pairs)


def shape_of(shape, dtype=F32):
    return jax.ShapeDtypeStruct(shape, dtype)


def whole(shape):
    return pl.BlockSpec(shape, lambda *_: (0,) * len(shape))


VMEM_SPEC = pl.BlockSpec(memory_space=pltpu.VMEM)
SMEM_SPEC = pl.BlockSpec(memory_space=pltpu.SMEM)
ANY_SPEC = pl.BlockSpec(memory_space=pl.ANY)


def shards(final_sens, courant, limiter, directions, nest_sens, box_lon, box_lat, eof, lat_filter, lon_filter):
    channels, lon_block, lat_block = final_sens.shape
    fields, levels = limiter.shape[1], courant.shape[2]
    rows_count, cols_count = lax.axis_size("row"), lax.axis_size("col")
    me_row, me_col = lax.axis_index("row"), lax.axis_index("col")
    ids = jnp.stack(
        [
            me_row,
            me_col,
            me_row % 2,
            me_col % 2,
            me_row * 0,
            me_row * 0 + lon_block,
            box_lon[0] - me_col * lon_block,
            box_lat[0] - me_row * lat_block,
            me_col % 2,
        ]
    ).astype(jnp.int32)
    lat_part = lat_filter.shape[0] // cols_count
    share = channels // rows_count
    tall = min(BAND, lon_block)
    n_bands = lon_block // tall

    height = lon_filter.shape[0] // 2
    gathered = [lax.dynamic_slice_in_dim(lon_filter, (me_col % 2) * height, height, 0)]
    orders = [2**k for k in range(10) if 2**k < rows_count]
    turns = (orders, orders[::-1])
    owners = [(0, 0)]

    def gather(stage, pieces):
        pairs = []
        for i in range(rows_count * cols_count):
            row, col = divmod(i, cols_count)
            pairs.append((i, (row ^ turns[col % 2][stage]) * cols_count + col))
        return [lax.ppermute(piece, ("row", "col"), pairs) for piece in pieces]

    direct = []
    for stage in range(len(orders)):
        direct += gather(stage, gathered[:1])

    nest = jnp.transpose(nest_sens, (0, 2, 1))
    fine_lat, fine_lon = nest.shape[1:]
    coarse = pl.pallas_call(
        coarse_sums,
        out_shape=shape_of((fine_lon // RATIO, channels * fine_lat // RATIO)),
        in_specs=[SMEM_SPEC, VMEM_SPEC],
        out_specs=VMEM_SPEC,
        scratch_shapes=[pltpu.VMEM((channels * fine_lat, fine_lon), F32)],
        name="coarse",
    )(ids, nest)
    masks = [(0, 0)]
    stages = [("col", m) for m in (2**k for k in range(1, 10)) if m < cols_count]
    stages += [("row", m) for m in (2**k for k in range(10)) if m < rows_count]
    stages += [("col", 1)]

    def spread(held, count, last=False):
        nonlocal stages, masks
        for axis, mask in stages[:count]:
            other = swap(held, axis, mask)
            held = (held, other) if last else jnp.concatenate([held, other], axis=0)
            masks = masks + [(r ^ mask, c) if axis == "row" else (r, c ^ mask) for r, c in masks]
        stages = stages[count:]
        return held

    def after(value, *others):
        return lax.optimization_barrier((value, *others))[0]

    held = spread(coarse[None], 2)

    mu = final_sens.reshape(fields, levels, lon_block, lat_block)
    call = pl.pallas_call(
        first_step,
        grid=(levels,),
        out_shape=(
            shape_of(mu.shape),
            shape_of((tall, LANES)),
            shape_of((tall, LANES)),
            shape_of((tall, LANES)),
            shape_of((levels + 1, 2 * fields, lat_block)),
            shape_of((levels, 2 * fields, lat_block)),
            shape_of((levels, 2 * fields, lat_block)),
        ),
        in_specs=[
            pl.BlockSpec((fields, 1, lon_block, lat_block), lambda l: (0, l, 0, 0)),
            pl.BlockSpec((2, 2, 1, lon_block, lat_block), lambda l: (0, 0, l, 0, 0)),
            whole(limiter.shape),
            whole(directions.shape),
        ],
        out_specs=(
            pl.BlockSpec((fields, 1, lon_block, lat_block), lambda l: (0, l, 0, 0)),
            whole((tall, LANES)),
            whole((tall, LANES)),
            whole((tall, LANES)),
            whole((levels + 1, 2 * fields, lat_block)),
            whole((levels, 2 * fields, lat_block)),
            whole((levels, 2 * fields, lat_block)),
        ),
        scratch_shapes=[
            pltpu.VMEM((fields, lon_block, lat_block), F32),
            pltpu.VMEM((lon_block, lat_block), F32),
            pltpu.VMEM((lon_block, lat_block), F32),
            pltpu.VMEM((fields, lon_block, LANES), F32),
        ],
        name="first_step",
    )
    mu1, ef, em, ew, xr, xm, xw = call(mu, courant, limiter, directions)
    held = spread(after(held, ef), 1)
    efa, efb = neighbours(ef, "row", 0), neighbours(ef, "row", 1)
    xra, xrb = neighbours(xr, "col", 0), neighbours(xr, "col", 1)
    held = spread(after(held, efa, efb, xra, xrb), len(stages) - 1)
    size = channels * SUB
    call = pl.pallas_call(
        functools.partial(rims, lon_block, rows_count),
        out_shape=(
            shape_of(ef.shape),
            shape_of(xm.shape),
            shape_of(ef.shape),
            shape_of(xm.shape),
            shape_of((size, size), BF16),
            shape_of((size, size), BF16),
        ),
        in_specs=[SMEM_SPEC] + [VMEM_SPEC] * 9,
        out_specs=(VMEM_SPEC,) * 6,
        name="rims",
    )
    e2, x2, m1, x1, kh, kl = call(ids, efa, efb, xra, xrb, em, ew, xm, xw, eof)
    e2a, e2b = neighbours(e2, "row", 0), neighbours(e2, "row", 1)
    x2a, x2b = neighbours(x2, "col", 0), neighbours(x2, "col", 1)
    held = spread(held, 1, True)
    box = pl.pallas_call(
        functools.partial(arrange, masks, fine_lat // RATIO),
        out_shape=shape_of((lon_block, rows_count * coarse.shape[1])),
        in_specs=[SMEM_SPEC, VMEM_SPEC, VMEM_SPEC],
        out_specs=VMEM_SPEC,
        scratch_shapes=[pltpu.VMEM((cols_count * coarse.shape[0], rows_count * coarse.shape[1]), F32)],
        name="arrange",
    )(ids, *held)

    size_two = min(GROUP, tall)
    groups = tall // size_two
    fine = size_two // SUB
    top = lon_block // SUB - 1

    def control(band, halves, kl):
        def at(g):
            return band * groups + g

        def low(g):
            return jnp.maximum((band * groups + g) * fine - 1, 0)

        def high(g):
            return jnp.minimum((band * groups + g) * fine + fine, top)

        depth = share // halves
        return pl.pallas_call(
            functools.partial(second_step, band, rows_count),
            grid=(groups,),
            out_shape=(shape_of((depth, tall, lat_block), BF16),) * (rows_count * halves),
            in_specs=[
                SMEM_SPEC,
                pl.BlockSpec((fields, levels, size_two, lat_block), lambda g: (0, 0, at(g), 0)),
                pl.BlockSpec((fields, levels, SUB, lat_block), lambda g: (0, 0, low(g), 0)),
                pl.BlockSpec((fields, levels, SUB, lat_block), lambda g: (0, 0, high(g), 0)),
                pl.BlockSpec((1, 2, levels, size_two, lat_block), lambda g: (0, 0, 0, at(g), 0)),
                pl.BlockSpec((1, 1, levels, SUB, lat_block), lambda g: (0, 0, 0, low(g), 0)),
                pl.BlockSpec((1, 1, levels, SUB, lat_block), lambda g: (0, 0, 0, high(g), 0)),
                pl.BlockSpec((1, fields, size_two, lat_block), lambda g: (0, 0, at(g), 0)),
                pl.BlockSpec((1, fields, SUB, lat_block), lambda g: (0, 0, low(g), 0)),
                pl.BlockSpec((1, fields, SUB, lat_block), lambda g: (0, 0, high(g), 0)),
                pl.BlockSpec((1, 2, size_two, lat_block), lambda g: (0, 0, at(g), 0)),
                pl.BlockSpec((1, 1, SUB, lat_block), lambda g: (0, 0, low(g), 0)),
                pl.BlockSpec((1, 1, SUB, lat_block), lambda g: (0, 0, high(g), 0)),
                whole(m1.shape),
                whole(x1.shape),
                whole(e2.shape),
                whole(e2.shape),
                whole(x2.shape),
                whole(x2.shape),
                pl.BlockSpec((size_two, box.shape[1]), lambda g: (at(g), 0)),
                whole(kh.shape),
                whole(kl.shape),
            ],
            out_specs=(pl.BlockSpec((depth, size_two, lat_block), lambda g: (0, g, 0)),) * (rows_count * halves),
            scratch_shapes=[
                pltpu.VMEM((fields, size_two + 2 * SUB, lat_block), F32),
                pltpu.VMEM((size_two + 2 * SUB, lat_block), F32),
                pltpu.VMEM((size_two, lat_block), F32),
                pltpu.VMEM((tall, LANES), F32),
                pltpu.VMEM((fine, channels * SUB, lat_block), F32),
            ],
            name="second_step",
        )(ids, mu1, mu1, mu1, courant, courant, courant, limiter, limiter, limiter, directions, directions, directions,
          m1, x1, e2a, e2b, x2a, x2b, box, kh, kl)

    def to_rows(pieces):
        return [pieces[0]] + [swap(pieces[s], "row", s) for s in range(1, rows_count)]

    def smooth(pieces, start, height, token):
        count = pieces[0].shape[0]
        filt = lat_filter if token is None else after(lat_filter, token)
        call = pl.pallas_call(
            functools.partial(lat_filter_part, start, height, count, rows_count, cols_count),
            out_shape=(shape_of((count, height, tall), BF16),) * cols_count,
            in_specs=[SMEM_SPEC] + [VMEM_SPEC] * (rows_count + 1),
            out_specs=(VMEM_SPEC,) * cols_count,
            name="lat_filter",
        )
        outs = call(ids, *pieces, filt)
        moved = {s: swap(outs[s], "col", s) for s in range(cols_count - 1, 0, -1)}
        return [outs[0]] + [moved[s] for s in range(1, cols_count)], outs[-1]

    firsts = []
    sent = []
    order = None
    for band in range(n_bands):
        final = band == n_bands - 1
        halves = 1 if final else 2
        kl = kl if order is None else after(kl, order)
        outs = control(band, halves, kl)
        order = outs[-1]
        for h in range(halves):
            sent.append(to_rows([outs[s * halves + h] for s in range(rows_count)]))

    token = None
    for pieces in sent[:-1]:
        moved, token = smooth(pieces, 0, lat_part, token)
        firsts += moved
    half_height = lat_part // 2
    lasts = []
    for h in range(2):
        early = token
        moved, token = smooth(sent[-1], h * half_height, half_height, token)
        lasts.append(moved)
    for stage in range(len(orders)):
        gathered += [direct[stage]] + gather(stage, [after(piece, early) for piece in gathered[1:]])
        owners += [(a ^ turns[0][stage], b ^ turns[1][stage]) for a, b in owners]
    filters = []
    for piece in gathered:
        filters += [piece, swap(after(piece, token), "col", 1)]

    n_lon = cols_count * lon_block
    rows = share * half_height
    if lon_block % LANES:
        stacked = jnp.stack([jnp.concatenate([lasts[0][s], lasts[1][s]], axis=1) for s in range(cols_count)])
        lines = jnp.take(stacked, me_col ^ jnp.arange(cols_count), axis=0)
        lines = jnp.transpose(lines, (2, 1, 0, 3)).reshape(lat_part, share, n_lon)
        whole_filter = jnp.zeros((n_lon, n_lon), BF16)
        for j, piece in enumerate(filters):
            side = me_col % 2 if j % 2 == 0 else 1 - me_col % 2
            owner = (me_row ^ jnp.where(side == 0, *owners[j // 2])) * 2 + side
            whole_filter = lax.dynamic_update_slice_in_dim(whole_filter, piece, owner * height, 0)
        return jnp.einsum("lci,oi->lco", lines, whole_filter, preferred_element_type=F32)
    out = None
    for h in range(2):
        aliased = out is not None
        operands = (ids, *firsts, *lasts[h], *filters) + ((out,) if aliased else ())
        call = pl.pallas_call(
            functools.partial(lon_filter_part, h, half_height, cols_count, rows_count, len(firsts), aliased, owners),
            out_shape=shape_of((2 * rows, n_lon)),
            in_specs=[SMEM_SPEC] + [VMEM_SPEC] * (len(firsts) + cols_count + 2 * rows_count) + [ANY_SPEC] * aliased,
            out_specs=ANY_SPEC,
            scratch_shapes=[
                pltpu.VMEM((rows, n_lon), BF16),
                pltpu.VMEM((4, height // LANES, rows, LANES), F32),
                pltpu.SemaphoreType.DMA((4, height // LANES)),
            ],
            input_output_aliases={len(operands) - 1: 0} if aliased else {},
            name="lon_filter",
        )
        out = call(*operands)
    return out.reshape(lat_part, share, n_lon)


def solution(mesh):
    placed = (
        P(None, "col", "row"),
        P(None, None, None, "col", "row"),
        P(None, None, "col", "row"),
        P(None, None, "col", "row"),
        P(None, "col", "row"),
        P(),
        P(),
        P(),
        P(),
        P("row", None),
    )
    return jax.shard_map(shards, mesh=mesh, in_specs=placed, out_specs=P("col", "row", None), check_vma=False)
```

```python
import functools

import jax
import jax.numpy as jnp
from jax import lax
from jax.experimental import pallas as pl
from jax.experimental.pallas import tpu as pltpu
from jax.sharding import PartitionSpec as P


RATIO = 3
BOXX = 256
BOXY = 32
LANES = 128
SUB = 8
BAND = 128
GROUP = 128
GROUP_ONE = 128
UNROLL_ONE = 2
UNROLL_TWO = 2
F32 = jnp.float32
BF16 = jnp.bfloat16
NT = (((1,), (1,)), ((), ()))
HIGHEST = lax.Precision.HIGHEST


def lanes_of(shape):
    return lax.broadcasted_iota(jnp.int32, shape, len(shape) - 1)


def sublanes_of(shape):
    return lax.broadcasted_iota(jnp.int32, shape, len(shape) - 2)


def split(value):
    return [value[:, k * LANES : (k + 1) * LANES] for k in range(value.shape[1] // LANES)]


def rows_at(start):
    return pl.ds(pl.multiple_of(start, SUB), SUB)


def x_fluxes(damped, coef, east):
    flux = coef * damped
    part = east * flux
    return part, flux - part


def stencil(mu, px, qx, up_x, down_x, damped, coef, north, halo_up, halo_down):
    flux = coef * damped
    py = north * flux
    qy = flux - py
    base = mu - px + qx - py + qy + up_x - down_x
    lane = lanes_of((SUB, LANES))
    last, first = lane == LANES - 1, lane == 0
    py, qy, base = split(py), split(qy), split(base)
    rolled_up = [pltpu.roll(v, LANES - 1, 1) for v in py]
    rolled_down = [pltpu.roll(v, 1, 1) for v in qy]
    count = len(base)
    out = []
    for k in range(count):
        above = rolled_up[k + 1] if k + 1 < count else halo_up
        below = rolled_down[k - 1] if k > 0 else halo_down
        out.append(base[k] + jnp.where(last, above, rolled_up[k]) - jnp.where(first, below, rolled_down[k]))
    return out, py, qy


def shifted(px_here, px_next, qx_prev, qx_here):
    sub = sublanes_of(px_here.shape)
    up = jnp.where(sub == SUB - 1, pltpu.roll(px_next, SUB - 1, 0), pltpu.roll(px_here, SUB - 1, 0))
    down = jnp.where(sub == 0, pltpu.roll(qx_prev, 1, 0), pltpu.roll(qx_here, 1, 0))
    return up, down


def first_step(mu_ref, cour_ref, lim_ref, dir_ref, out_ref, ef_ref, em_ref, ew_ref, xr_ref, xm_ref, xw_ref, damp, east, north, rim):
    level = pl.program_id(0)
    fields, _, rows, width = mu_ref.shape
    tiles = width // LANES
    size = min(GROUP_ONE, rows)
    groups = rows // size
    tall = ef_ref.shape[0]
    lane = lanes_of((SUB, LANES))
    last = lane == LANES - 1
    edge = slice((tiles - 1) * LANES, tiles * LANES)

    @pl.when(level == 0)
    def _():
        for ref in (ef_ref, em_ref, ew_ref, xr_ref):
            ref[...] = jnp.zeros_like(ref)

        def prepare(tile, carry):
            at = rows_at(tile * SUB)
            east[at] = dir_ref[1, 0, at].astype(F32)
            north[at] = dir_ref[1, 1, at].astype(F32)
            side = jnp.where(last, 1 - dir_ref[0, 1, at, edge], dir_ref[0, 1, at, :LANES]).astype(F32)
            for f in range(fields):
                damp[f, at] = 0.5 + 0.5 * lim_ref[1, f, at].astype(F32)
                flag = jnp.where(last, lim_ref[0, f, at, edge], lim_ref[0, f, at, :LANES]).astype(F32)
                rim[f, at] = side * (0.5 + 0.5 * flag)
            return carry

        lax.fori_loop(0, rows // SUB, prepare, 0)

    def group(index, carry):
        f, g = index // groups, lax.rem(index, groups)
        base = g * size
        inside = size // SUB
        starts = [jnp.maximum(base - SUB, 0)] + [base + SUB * t for t in range(inside)] + [jnp.minimum(base + size, rows - SUB)]
        keep_low = jnp.where(g > 0, 1.0, 0.0).astype(F32)
        keep_high = jnp.where(g < groups - 1, 1.0, 0.0).astype(F32)
        slot = level * fields + f
        none = jnp.zeros((SUB, LANES), F32)
        mus = [mu_ref[f, 0, rows_at(s)] for s in starts]
        damped = [m * damp[f, rows_at(s)] for m, s in zip(mus, starts)]
        pq = [x_fluxes(m, cour_ref[1, 0, 0, rows_at(s)], east[rows_at(s)]) for m, s in zip(damped, starts)]
        px = [v[0] for v in pq]
        qx = [v[1] for v in pq]
        qx[0] = qx[0] * keep_low
        px[-1] = px[-1] * keep_high
        for t in range(inside):
            at = rows_at(starts[t + 1])
            up, down = shifted(px[t + 1], px[t + 2], qx[t], qx[t + 1])
            new, py, qy = stencil(
                mus[t + 1], px[t + 1], qx[t + 1], up, down, damped[t + 1], cour_ref[1, 1, 0, at], north[at], none, none
            )
            for k in range(tiles):
                out_ref[f, 0, at, k * LANES : (k + 1) * LANES] = new[k]
            band = starts[t + 1] // tall
            turn = (2 * slot + 1 + band * 64) & (LANES - 1)
            mine = (lane // 2) == slot + 32 * band
            weight = jnp.where(last, cour_ref[0, 1, 0, at, edge], cour_ref[0, 1, 0, at, :LANES]) * rim[f, at]
            place = rows_at(lax.rem(starts[t + 1], tall))
            values = (jnp.where(last, qy[-1], py[0]), jnp.where(last, new[-1], new[0]), weight)
            for ref, value in zip((ef_ref, em_ref, ew_ref), values):
                ref[place] = jnp.where(mine, pltpu.roll(value, turn, 1), ref[place])
        return carry

    def groups_at(index, carry):
        for u in range(UNROLL_ONE):
            group(index + u * (fields // UNROLL_ONE) * groups, carry)
        return carry

    lax.fori_loop(0, fields * groups // UNROLL_ONE, groups_at, 0)

    low, high = slice(0, SUB), slice(rows - SUB, rows)
    for f in range(fields):
        slot = level * fields + f
        turn = 2 * slot + 1
        mine = (lane // 2) == slot
        px, _ = x_fluxes(mu_ref[f, 0, low] * damp[f, low], cour_ref[1, 0, 0, low], east[low])
        _, qx = x_fluxes(mu_ref[f, 0, high] * damp[f, high], cour_ref[1, 0, 0, high], east[high])
        xr_ref[level, f : f + 1] = px[:1]
        xr_ref[level, fields + f : fields + f + 1] = qx[SUB - 1 :]
        px_edge = pltpu.roll(jnp.where(last, px[:, edge], px[:, :LANES]), turn, 1)
        qx_edge = pltpu.roll(jnp.where(last, qx[:, edge], qx[:, :LANES]), turn, 1)
        corner = xr_ref.shape[0] - 1
        xr_ref[corner, 0:1, :LANES] = jnp.where(mine, px_edge, jnp.broadcast_to(xr_ref[corner, 0:1, :LANES], (SUB, LANES)))[:1]
        xr_ref[corner, 4:5, :LANES] = jnp.where(mine, qx_edge, jnp.broadcast_to(xr_ref[corner, 4:5, :LANES], (SUB, LANES)))[SUB - 1 :]
        xm_ref[level, f : f + 1] = out_ref[f, 0, low][:1]
        xm_ref[level, fields + f : fields + f + 1] = out_ref[f, 0, high][SUB - 1 :]
        for at, part, row in ((low, 0, 0), (high, 1, SUB - 1)):
            way = dir_ref[0, 0, at].astype(F32)
            way = 1.0 - way if part else way
            value = way * (0.5 + 0.5 * lim_ref[0, f, at].astype(F32)) * cour_ref[0, 0, 0, at]
            xw_ref[level, part * fields + f : part * fields + f + 1] = value[row : row + 1]


def pick(first, a, b):
    return jnp.where(first, a, b)


def rims(rows, parts, ids, efa_ref, efb_ref, xra_ref, xrb_ref, em_ref, ew_ref, xm_ref, xw_ref, eof_ref, e2_ref, x2_ref, m1_ref, x1_ref, kh_ref, kl_ref):
    me_row = ids[0]
    even_row, even_col = ids[2] == 0, ids[3] == 0
    levels, twice, width = xm_ref.shape
    fields = twice // 2
    tiles = width // LANES
    tall = em_ref.shape[0]
    top_band = (rows - 1) // tall
    lane = lanes_of((tall, LANES))
    sub = sublanes_of((tall, LANES))
    up = pick(even_row, efa_ref[...], efb_ref[...])
    down = pick(even_row, efb_ref[...], efa_ref[...])
    merged = jnp.where(lane % 2 == 1, up, -pltpu.roll(down, 2, 1))
    m1_ref[...] = merged
    fixed = em_ref[...] + jnp.where(lane % 2 == 0, pltpu.roll(up, LANES - 1, 1), -pltpu.roll(down, 1, 1))
    corner = xra_ref.shape[0] - 1
    ca, cb = xra_ref[corner, :, :LANES], xrb_ref[corner, :, :LANES]
    corner_up = pick(even_col, ca, cb)[0:1]
    corner_down = pick(even_col, cb, ca)[4:5]
    if top_band:
        corner_up = pltpu.roll(jnp.broadcast_to(corner_up, (SUB, LANES)), 64 * top_band, 1)[:1]
    fixed = fixed + jnp.where(sub == tall - 1, corner_up, 0.0) - jnp.where(sub == 0, corner_down, 0.0)
    e2_ref[...] = ew_ref[...] * fixed

    lane8 = lanes_of((twice, LANES))
    sub8 = sublanes_of((twice, LANES))
    ends = jnp.where(sub8 < fields, jnp.broadcast_to(merged[0:1], (twice, LANES)), jnp.broadcast_to(merged[tall - 1 :], (twice, LANES)))
    wide = sublanes_of((twice, width))
    for level in range(levels):
        a, b = xra_ref[level], xrb_ref[level]
        halo = jnp.where(wide < fields, pick(even_col, a, b), -pick(even_col, b, a))
        x1_ref[level] = halo
        target = 2 * (level * fields + sub8 % fields) + 1 + jnp.where(sub8 >= fields, 64 * top_band, 0)
        at_last = jnp.sum(jnp.where(lane8 == target, ends, 0.0), axis=1, keepdims=True)
        at_first = jnp.sum(jnp.where(lane8 == (target + 1) % LANES, ends, 0.0), axis=1, keepdims=True)
        here = split(xm_ref[level] + pltpu.roll(halo, fields, 0))
        here[-1] = here[-1] + jnp.where(lane8 == LANES - 1, at_last, 0.0)
        here[0] = here[0] + jnp.where(lane8 == 0, at_first, 0.0)
        for k in range(tiles):
            at = slice(k * LANES, (k + 1) * LANES)
            x2_ref[level, :, at] = xw_ref[level, :, at] * here[k]

    channels = eof_ref.shape[0]
    size = kh_ref.shape[0]
    share = channels // parts
    i = lax.broadcasted_iota(jnp.int32, (size, channels), 0) // SUB
    chosen = ((i // share) ^ me_row) * share + i % share
    left = (lax.broadcasted_iota(jnp.int32, (size, channels), 1) == chosen).astype(F32)
    j = lax.broadcasted_iota(jnp.int32, (channels, size), 1) // SUB
    right = (lax.broadcasted_iota(jnp.int32, (channels, size), 0) == j).astype(F32)
    mixed = jnp.dot(left, eof_ref[...], precision=HIGHEST, preferred_element_type=F32)
    spread = jnp.dot(mixed, right, precision=HIGHEST, preferred_element_type=F32)
    same = (lax.broadcasted_iota(jnp.int32, (size, size), 0) - lax.broadcasted_iota(jnp.int32, (size, size), 1)) % SUB == 0
    spread = jnp.where(same, spread, 0.0)
    high = spread.astype(BF16)
    kh_ref[...] = high
    kl_ref[...] = (spread - high.astype(F32)).astype(BF16)


def second_step(
    offset, parts, n_held, ids, mu_ref, mu_low, mu_high, cour_ref, cx_low, cx_high, lim_ref, lim_low, lim_high, dir_ref, dir_low, dir_high,
    m1_ref, x1_ref, e2a_ref, e2b_ref, x2a_ref, x2b_ref, box_ref, kh_ref, kl_ref, *rest,
):
    outs, (damp, east, north, m2_ref, mixed) = rest[n_held:-5], rest[-5:]
    g = pl.program_id(0)
    fields, levels, _, width = mu_ref.shape
    rows = ids[5]
    tall = m1_ref.shape[0]
    even_row, even_col = ids[2] == 0, ids[3] == 0
    tiles = width // LANES
    size = mu_ref.shape[2]
    inside = size // SUB
    lane = lanes_of((SUB, LANES))
    sub = sublanes_of((SUB, width))
    last, first = lane == LANES - 1, lane == 0

    @pl.when(g == 0)
    def _():
        wide = lanes_of((tall, LANES))
        up = pick(even_row, e2a_ref[...], e2b_ref[...])
        down = pick(even_row, e2b_ref[...], e2a_ref[...])
        m2_ref[...] = jnp.where(wide % 2 == 1, up, -pltpu.roll(down, 2, 1))

    lims = [(lim_low, 0)] + [(lim_ref, SUB * t) for t in range(inside)] + [(lim_high, 0)]
    dirs = [(dir_low, 0)] + [(dir_ref, SUB * t) for t in range(inside)] + [(dir_high, 0)]
    mus = [(mu_low, 0)] + [(mu_ref, SUB * t) for t in range(inside)] + [(mu_high, 0)]
    cxs = [(cx_low, 0)] + [(cour_ref, SUB * t) for t in range(inside)] + [(cx_high, 0)]
    for t in range(inside + 2):
        put = slice(SUB * t, SUB * (t + 1))
        ref, r = dirs[t]
        east[put] = ref[0, 0, r : r + SUB].astype(F32)
        if 0 < t <= inside:
            north[SUB * (t - 1) : SUB * t] = ref[0, 1, r : r + SUB].astype(F32)
        ref, r = lims[t]
        for f in range(fields):
            damp[f, put] = 0.5 + 0.5 * ref[0, f, r : r + SUB].astype(F32)

    base = offset + g * size
    starts = [jnp.maximum(base - SUB, 0)] + [base + SUB * t for t in range(inside)] + [jnp.minimum(base + size, rows - SUB)]
    bands = [s // tall for s in starts]
    places = [lax.rem(s, tall) for s in starts]
    at_start = base == 0
    at_end = base + size == rows
    lat_at = ids[7]
    box_lats = box_ref.shape[1] // (fields * levels * parts)
    per_tile = LANES // box_lats
    total = parts * box_lats
    inner = [((lane + LANES * k - lat_at) >= 0) & ((lane + LANES * k - lat_at) < total) for k in range(tiles)]

    def channel(index, carry):
        f, level = index // levels, lax.rem(index, levels)
        slot = level * fields + f
        vals, damped, px, qx = [], [], [], []
        for t in range(inside + 2):
            ref, r = mus[t]
            value = ref[f, level, r : r + SUB]
            fix = pltpu.roll(m1_ref[rows_at(places[t])], (126 - 2 * slot - 64 * bands[t]) & (LANES - 1), 1)
            pieces = split(value)
            pieces[-1] = pieces[-1] + jnp.where(last, fix, 0.0)
            pieces[0] = pieces[0] + jnp.where(first, fix, 0.0)
            value = jnp.concatenate(pieces, axis=1)
            if t == 1:
                value = value + jnp.where((sub == 0) & at_start, x1_ref[level, pl.ds(fields + f, 1)], 0.0)
            if t == inside:
                value = value + jnp.where((sub == SUB - 1) & at_end, x1_ref[level, pl.ds(f, 1)], 0.0)
            ref, r = cxs[t]
            weighed = value * damp[f, SUB * t : SUB * (t + 1)]
            p, q = x_fluxes(weighed, ref[0, 0, level, r : r + SUB], east[SUB * t : SUB * (t + 1)])
            vals.append(value)
            damped.append(weighed)
            px.append(p)
            qx.append(q)
        halo_low = pick(even_col, x2b_ref[level, pl.ds(fields + f, 1)], x2a_ref[level, pl.ds(fields + f, 1)])
        halo_high = pick(even_col, x2a_ref[level, pl.ds(f, 1)], x2b_ref[level, pl.ds(f, 1)])
        qx[0] = jnp.where(at_start, jnp.broadcast_to(halo_low, (SUB, width)), qx[0])
        px[-1] = jnp.where(at_end, jnp.broadcast_to(halo_high, (SUB, width)), px[-1])
        box_tile = pl.multiple_of((index // per_tile * parts + lax.rem(index, parts)) * LANES, LANES)
        box_turn = (lat_at - lax.rem(index, per_tile) * box_lats) & (LANES - 1)
        put = rows_at(index * SUB)
        for t in range(inside):
            mine = slice(SUB * t, SUB * (t + 1))
            up, down = shifted(px[t + 1], px[t + 2], qx[t], qx[t + 1])
            halo = pltpu.roll(m2_ref[rows_at(places[t + 1])], (126 - 2 * slot - 64 * bands[t + 1]) & (LANES - 1), 1)
            new, _, _ = stencil(
                vals[t + 1], px[t + 1], qx[t + 1], up, down, damped[t + 1], cour_ref[0, 1, level, mine], north[mine], halo, -halo
            )
            moved = pltpu.roll(box_ref[mine, pl.ds(box_tile, LANES)], box_turn, 1)
            for k in range(tiles):
                mixed[t, put, k * LANES : (k + 1) * LANES] = new[k] + jnp.where(inner[k], moved, 0.0)
        return carry

    def channels_at(index, carry):
        for u in range(UNROLL_TWO):
            channel(index * UNROLL_TWO + u, carry)
        return carry

    lax.fori_loop(0, fields * levels // UNROLL_TWO, channels_at, 0)

    channels = fields * levels
    share = channels // parts
    per = len(outs) // parts
    depth = share // per
    for v in range(inside // 2):
        both = []
        for t in (2 * v, 2 * v + 1):
            full = mixed[t]
            high = full.astype(BF16)
            low = (full - high.astype(F32)).astype(BF16)
            result = jnp.dot(kh_ref[...], high, preferred_element_type=F32)
            result += jnp.dot(kl_ref[...], high, preferred_element_type=F32)
            result += jnp.dot(kh_ref[...], low, preferred_element_type=F32)
            both.append(result)
        for c in range(channels):
            at = slice(c * SUB, (c + 1) * SUB)
            pair = jnp.concatenate([both[0][at], both[1][at]], axis=0).astype(BF16)
            outs[(c // share) * per + (c % share) // depth][c % depth, 2 * SUB * v : 2 * SUB * (v + 1)] = pair


def coarse_sums(ids, nest_ref, out_ref, held):
    channels, fine_lat, fine_lon = nest_ref.shape
    lon = ids[1] * fine_lon + lax.broadcasted_iota(jnp.int32, (fine_lat, fine_lon), 1)
    lat = ids[0] * fine_lat + lax.broadcasted_iota(jnp.int32, (fine_lat, fine_lon), 0)
    edge = (lon < RATIO) | (lon >= RATIO * BOXX - RATIO) | (lat < RATIO) | (lat >= RATIO * BOXY - RATIO)
    weight = jnp.where(edge, 1.0, 1.0 / (RATIO * RATIO)).astype(F32)
    for c in range(channels):
        held[c * fine_lat : (c + 1) * fine_lat] = nest_ref[c] * weight
    count = channels * fine_lat // RATIO
    sums = held[pl.ds(0, count, stride=RATIO)]
    for a in range(1, RATIO):
        sums = sums + held[pl.ds(a, count, stride=RATIO)]
    shape = (fine_lon // RATIO, fine_lon)
    select = (lax.broadcasted_iota(jnp.int32, shape, 1) // RATIO == lax.broadcasted_iota(jnp.int32, shape, 0)).astype(F32)
    result = lax.dot_general(select, sums, NT, precision=HIGHEST, preferred_element_type=F32)
    for k, piece in enumerate(split(result)):
        out_ref[:, k * LANES : (k + 1) * LANES] = pltpu.roll(piece, (ids[0] * (fine_lat // RATIO)) & (LANES - 1), 1)


def arrange(masks, lats, ids, near_ref, far_ref, out_ref, box):
    half, slab, wide = near_ref.shape
    rows = out_ref.shape[0]
    for p, (row_mask, col_mask) in enumerate(masks):
        at = pl.multiple_of((ids[1] ^ col_mask) * slab, SUB)
        to = pl.multiple_of((ids[0] ^ row_mask) * wide, LANES)
        box[pl.ds(at, slab), pl.ds(to, wide)] = near_ref[p] if p < half else far_ref[p - half]
    height = box.shape[0]
    away = ids[6]
    row = lax.broadcasted_iota(jnp.int32, (rows, LANES), 0) - away
    inside = (row >= 0) & (row < height)
    turn = lax.rem(lax.rem(away, height) + height, height)
    parts = box.shape[1] // wide
    slot = lanes_of((height, LANES)) // lats
    for k in range(wide // LANES):
        pieces = [box[:, r * wide + k * LANES : r * wide + (k + 1) * LANES] for r in range(parts)]
        for m in range(parts):
            value = pieces[0]
            for r in range(1, parts):
                value = jnp.where((slot - m) % parts == r, pieces[r], value)
            at = (k * parts + m) * LANES
            out_ref[:, at : at + LANES] = jnp.where(inside, pltpu.roll(value, turn, 0)[:rows], 0.0)


def lat_filter_part(start, height, count, parts, cols, ids, *refs):
    pieces, filt, outs = refs[:parts], refs[parts], refs[parts + 1 :]
    lat_block = pieces[0].shape[2]
    lon = pieces[0].shape[1]
    lat_part = filt.shape[0] // cols
    step = 2
    for p in range(count // step):
        right = [ref[step * p : step * (p + 1)].reshape(step * lon, lat_block) for ref in pieces]
        for s0 in range(0, cols, 4):
            acc = None
            for r in range(parts):
                at = pl.ds(pl.multiple_of((ids[0] ^ r) * lat_block, LANES), lat_block)
                left = jnp.concatenate(
                    [
                        filt[pl.ds(pl.multiple_of((ids[1] ^ s) * lat_part + start, 16), height), at]
                        for s in range(s0, min(s0 + 4, cols))
                    ],
                    axis=0,
                )
                term = lax.dot_general(left, right[r], NT, preferred_element_type=F32)
                acc = term if acc is None else acc + term
            for s in range(s0, min(s0 + 4, cols)):
                for c in range(step):
                    value = acc[(s - s0) * height : (s - s0 + 1) * height, c * lon : (c + 1) * lon]
                    outs[s][step * p + c] = value.astype(BF16)


def lon_filter_part(half, height, cols, parts, n_first, aliased, owners, ids, *refs):
    firsts = refs[:n_first]
    lasts = refs[n_first : n_first + cols]
    filters = refs[n_first + cols : n_first + cols + 2 * parts]
    rest = refs[n_first + cols + 2 * parts + (1 if aliased else 0) :]
    out, lines, stage, sem = rest
    channels, _, lon = lasts[0].shape
    wide = lines.shape[1] // cols
    rows = channels * height
    block = filters[0].shape[0]
    strips = block // LANES

    def flush(j, k):
        side = ids[8] if j % 2 == 0 else 1 - ids[8]
        even, odd = owners[j // 2]
        owner = (ids[0] ^ jnp.where(side == 0, even, odd)) * 2 + side
        at = pl.ds(pl.multiple_of(owner * block + k * LANES, LANES), LANES)
        slot = j % 4
        return pltpu.make_async_copy(stage.at[slot, k], out.at[pl.ds(half * rows, rows), at], sem.at[slot, k])

    for s in range(cols):
        base = pl.multiple_of((ids[1] ^ s) * wide, LANES)
        for c in range(channels):
            put = slice(c * height, (c + 1) * height)
            for b in range(wide // lon - 1):
                groups = n_first // cols // (wide // lon - 1)
                each = channels // groups
                ref = firsts[(b * groups + c // each) * cols + s]
                lines[put, pl.ds(base + b * lon, lon)] = ref[c % each, half * height : (half + 1) * height]
            lines[put, pl.ds(base + wide - lon, lon)] = lasts[s][c]
    for p in range(parts):
        right = jnp.concatenate([filters[2 * p][...], filters[2 * p + 1][...]], axis=0)
        acc = lax.dot_general(lines[...], right, NT, preferred_element_type=F32)
        for j in (2 * p, 2 * p + 1):
            for k in range(strips):
                if j >= 4:
                    flush(j - 4, k).wait()
                begin = (j % 2) * block + k * LANES
                for c in range(channels):
                    stage[j % 4, k, pl.ds(c, height, stride=channels), :] = acc[c * height : (c + 1) * height, begin : begin + LANES]
                flush(j, k).start()
    for j in range(max(0, 2 * parts - 4), 2 * parts):
        for k in range(strips):
            flush(j, k).wait()


def swap(value, axis, mask):
    count = lax.axis_size(axis)
    return lax.ppermute(value, axis, [(i, i ^ mask) for i in range(count)])


def neighbours(value, axis, parity):
    count = lax.axis_size(axis)
    pairs = []
    for i in range(parity, count - 1, 2):
        pairs += [(i, i + 1), (i + 1, i)]
    return lax.ppermute(value, axis, pairs)


def shape_of(shape, dtype=F32):
    return jax.ShapeDtypeStruct(shape, dtype)


def whole(shape):
    return pl.BlockSpec(shape, lambda *_: (0,) * len(shape))


VMEM_SPEC = pl.BlockSpec(memory_space=pltpu.VMEM)
SMEM_SPEC = pl.BlockSpec(memory_space=pltpu.SMEM)
ANY_SPEC = pl.BlockSpec(memory_space=pl.ANY)


def shards(final_sens, courant, limiter, directions, nest_sens, box_lon, box_lat, eof, lat_filter, lon_filter):
    channels, lon_block, lat_block = final_sens.shape
    fields, levels = limiter.shape[1], courant.shape[2]
    rows_count, cols_count = lax.axis_size("row"), lax.axis_size("col")
    me_row, me_col = lax.axis_index("row"), lax.axis_index("col")
    ids = jnp.stack(
        [
            me_row,
            me_col,
            me_row % 2,
            me_col % 2,
            me_row * 0,
            me_row * 0 + lon_block,
            box_lon[0] - me_col * lon_block,
            box_lat[0] - me_row * lat_block,
            me_col % 2,
        ]
    ).astype(jnp.int32)
    lat_part = lat_filter.shape[0] // cols_count
    share = channels // rows_count
    tall = min(BAND, lon_block)
    n_bands = lon_block // tall

    height = lon_filter.shape[0] // 2
    gathered = [lax.dynamic_slice_in_dim(lon_filter, (me_col % 2) * height, height, 0)]
    orders = [2**k for k in range(10) if 2**k < rows_count]
    turns = (orders, orders[::-1])
    owners = [(0, 0)]

    def gather(stage, pieces):
        pairs = []
        for i in range(rows_count * cols_count):
            row, col = divmod(i, cols_count)
            pairs.append((i, (row ^ turns[col % 2][stage]) * cols_count + col))
        return [lax.ppermute(piece, ("row", "col"), pairs) for piece in pieces]

    direct = []
    for stage in range(len(orders)):
        direct += gather(stage, gathered[:1])

    nest = jnp.transpose(nest_sens, (0, 2, 1))
    fine_lat, fine_lon = nest.shape[1:]
    coarse = pl.pallas_call(
        coarse_sums,
        out_shape=shape_of((fine_lon // RATIO, channels * fine_lat // RATIO)),
        in_specs=[SMEM_SPEC, VMEM_SPEC],
        out_specs=VMEM_SPEC,
        scratch_shapes=[pltpu.VMEM((channels * fine_lat, fine_lon), F32)],
        name="coarse",
    )(ids, nest)
    masks = [(0, 0)]
    stages = [("col", m) for m in (2**k for k in range(1, 10)) if m < cols_count]
    stages += [("row", m) for m in (2**k for k in range(10)) if m < rows_count]
    stages += [("col", 1)]

    def spread(held, count, last=False):
        nonlocal stages, masks
        for axis, mask in stages[:count]:
            other = swap(held, axis, mask)
            held = (held, other) if last else jnp.concatenate([held, other], axis=0)
            masks = masks + [(r ^ mask, c) if axis == "row" else (r, c ^ mask) for r, c in masks]
        stages = stages[count:]
        return held

    def after(value, *others):
        return lax.optimization_barrier((value, *others))[0]

    held = spread(coarse[None], 2)

    mu = final_sens.reshape(fields, levels, lon_block, lat_block)
    call = pl.pallas_call(
        first_step,
        grid=(levels,),
        out_shape=(
            shape_of(mu.shape),
            shape_of((tall, LANES)),
            shape_of((tall, LANES)),
            shape_of((tall, LANES)),
            shape_of((levels + 1, 2 * fields, lat_block)),
            shape_of((levels, 2 * fields, lat_block)),
            shape_of((levels, 2 * fields, lat_block)),
        ),
        in_specs=[
            pl.BlockSpec((fields, 1, lon_block, lat_block), lambda l: (0, l, 0, 0)),
            pl.BlockSpec((2, 2, 1, lon_block, lat_block), lambda l: (0, 0, l, 0, 0)),
            whole(limiter.shape),
            whole(directions.shape),
        ],
        out_specs=(
            pl.BlockSpec((fields, 1, lon_block, lat_block), lambda l: (0, l, 0, 0)),
            whole((tall, LANES)),
            whole((tall, LANES)),
            whole((tall, LANES)),
            whole((levels + 1, 2 * fields, lat_block)),
            whole((levels, 2 * fields, lat_block)),
            whole((levels, 2 * fields, lat_block)),
        ),
        scratch_shapes=[
            pltpu.VMEM((fields, lon_block, lat_block), F32),
            pltpu.VMEM((lon_block, lat_block), F32),
            pltpu.VMEM((lon_block, lat_block), F32),
            pltpu.VMEM((fields, lon_block, LANES), F32),
        ],
        name="first_step",
    )
    mu1, ef, em, ew, xr, xm, xw = call(mu, courant, limiter, directions)
    held = spread(after(held, ef), 1)
    efa, efb = neighbours(ef, "row", 0), neighbours(ef, "row", 1)
    xra, xrb = neighbours(xr, "col", 0), neighbours(xr, "col", 1)
    held = spread(after(held, efa, efb, xra, xrb), len(stages) - 1)
    size = channels * SUB
    call = pl.pallas_call(
        functools.partial(rims, lon_block, rows_count),
        out_shape=(
            shape_of(ef.shape),
            shape_of(xm.shape),
            shape_of(ef.shape),
            shape_of(xm.shape),
            shape_of((size, size), BF16),
            shape_of((size, size), BF16),
        ),
        in_specs=[SMEM_SPEC] + [VMEM_SPEC] * 9,
        out_specs=(VMEM_SPEC,) * 6,
        name="rims",
    )
    e2, x2, m1, x1, kh, kl = call(ids, efa, efb, xra, xrb, em, ew, xm, xw, eof)
    e2a, e2b = neighbours(e2, "row", 0), neighbours(e2, "row", 1)
    x2a, x2b = neighbours(x2, "col", 0), neighbours(x2, "col", 1)
    held = spread(held, 1, True)
    box = pl.pallas_call(
        functools.partial(arrange, masks, fine_lat // RATIO),
        out_shape=shape_of((lon_block, rows_count * coarse.shape[1])),
        in_specs=[SMEM_SPEC, VMEM_SPEC, VMEM_SPEC],
        out_specs=VMEM_SPEC,
        scratch_shapes=[pltpu.VMEM((cols_count * coarse.shape[0], rows_count * coarse.shape[1]), F32)],
        name="arrange",
    )(ids, *held)

    top = lon_block // SUB - 1

    def control(band, halves, kl, cut=1, part=0, held=()):
        size_two = min(GROUP, tall) // cut
        groups = tall // size_two // cut
        fine = size_two // SUB

        def at(g):
            return (band * cut + part) * groups + g

        def low(g):
            return jnp.maximum(at(g) * fine - 1, 0)

        def high(g):
            return jnp.minimum(at(g) * fine + fine, top)

        depth = share // halves
        return pl.pallas_call(
            functools.partial(second_step, band * tall + part * (tall // cut), rows_count, len(held)),
            grid=(groups,),
            out_shape=(shape_of((depth, tall, lat_block), BF16),) * (rows_count * halves),
            in_specs=[
                SMEM_SPEC,
                pl.BlockSpec((fields, levels, size_two, lat_block), lambda g: (0, 0, at(g), 0)),
                pl.BlockSpec((fields, levels, SUB, lat_block), lambda g: (0, 0, low(g), 0)),
                pl.BlockSpec((fields, levels, SUB, lat_block), lambda g: (0, 0, high(g), 0)),
                pl.BlockSpec((1, 2, levels, size_two, lat_block), lambda g: (0, 0, 0, at(g), 0)),
                pl.BlockSpec((1, 1, levels, SUB, lat_block), lambda g: (0, 0, 0, low(g), 0)),
                pl.BlockSpec((1, 1, levels, SUB, lat_block), lambda g: (0, 0, 0, high(g), 0)),
                pl.BlockSpec((1, fields, size_two, lat_block), lambda g: (0, 0, at(g), 0)),
                pl.BlockSpec((1, fields, SUB, lat_block), lambda g: (0, 0, low(g), 0)),
                pl.BlockSpec((1, fields, SUB, lat_block), lambda g: (0, 0, high(g), 0)),
                pl.BlockSpec((1, 2, size_two, lat_block), lambda g: (0, 0, at(g), 0)),
                pl.BlockSpec((1, 1, SUB, lat_block), lambda g: (0, 0, low(g), 0)),
                pl.BlockSpec((1, 1, SUB, lat_block), lambda g: (0, 0, high(g), 0)),
                whole(m1.shape),
                whole(x1.shape),
                whole(e2.shape),
                whole(e2.shape),
                whole(x2.shape),
                whole(x2.shape),
                pl.BlockSpec((size_two, box.shape[1]), lambda g: (at(g), 0)),
                whole(kh.shape),
                whole(kl.shape),
            ]
            + [ANY_SPEC] * len(held),
            out_specs=(pl.BlockSpec((depth, size_two, lat_block), lambda g: (0, part * groups + g, 0)),) * (rows_count * halves),
            input_output_aliases={22 + i: i for i in range(len(held))},
            scratch_shapes=[
                pltpu.VMEM((fields, size_two + 2 * SUB, lat_block), F32),
                pltpu.VMEM((size_two + 2 * SUB, lat_block), F32),
                pltpu.VMEM((size_two, lat_block), F32),
                pltpu.VMEM((tall, LANES), F32),
                pltpu.VMEM((fine, channels * SUB, lat_block), F32),
            ],
            name="second_step",
        )(ids, mu1, mu1, mu1, courant, courant, courant, limiter, limiter, limiter, directions, directions, directions,
          m1, x1, e2a, e2b, x2a, x2b, box, kh, kl, *held)

    def to_rows(pieces):
        moved = [pieces[0]]
        for s in range(1, rows_count):
            moved.append(swap(pieces[s], "row", s))
        return moved

    def smooth(pieces, start, height, token):
        count = pieces[0].shape[0]
        filt = lat_filter if token is None else after(lat_filter, token)
        call = pl.pallas_call(
            functools.partial(lat_filter_part, start, height, count, rows_count, cols_count),
            out_shape=(shape_of((count, height, tall), BF16),) * cols_count,
            in_specs=[SMEM_SPEC] + [VMEM_SPEC] * (rows_count + 1),
            out_specs=(VMEM_SPEC,) * cols_count,
            name="lat_filter",
        )
        outs = call(ids, *pieces, filt)
        moved = {}
        for s in range(cols_count - 1, 0, -1):
            moved[s] = swap(outs[s], "col", s)
        return [outs[0]] + [moved[s] for s in range(1, cols_count)], outs[-1]

    firsts = []
    sent = []
    order = None
    token = None
    for band in range(n_bands):
        final = band == n_bands - 1
        halves = 1 if final else 2
        if band:
            kl = after(kl, order)
            outs = control(band, halves, kl, 2)
            token = outs[0]
            outs = control(band, halves, kl, 2, 1, outs)
        else:
            outs = control(band, halves, kl)
        order = outs[-1]
        for h in range(halves):
            sent.append(to_rows([outs[s * halves + h] for s in range(rows_count)]))

    for pieces in sent[:-1]:
        moved, token = smooth(pieces, 0, lat_part, token)
        firsts += moved
    half_height = lat_part // 2
    lasts = []
    for h in range(2):
        early = token
        moved, token = smooth(sent[-1], h * half_height, half_height, token)
        lasts.append(moved)
    for stage in range(len(orders)):
        gathered += [direct[stage]] + gather(stage, [after(piece, early) for piece in gathered[1:]])
        owners += [(a ^ turns[0][stage], b ^ turns[1][stage]) for a, b in owners]
    filters = []
    for j, piece in enumerate(gathered):
        late = j and j == len(gathered) - 1
        filters += [piece, swap(after(piece, token if late else early), "col", 1)]

    n_lon = cols_count * lon_block
    rows = share * half_height
    if lon_block % LANES:
        stacked = jnp.stack([jnp.concatenate([lasts[0][s], lasts[1][s]], axis=1) for s in range(cols_count)])
        lines = jnp.take(stacked, me_col ^ jnp.arange(cols_count), axis=0)
        lines = jnp.transpose(lines, (2, 1, 0, 3)).reshape(lat_part, share, n_lon)
        whole_filter = jnp.zeros((n_lon, n_lon), BF16)
        for j, piece in enumerate(filters):
            side = me_col % 2 if j % 2 == 0 else 1 - me_col % 2
            owner = (me_row ^ jnp.where(side == 0, *owners[j // 2])) * 2 + side
            whole_filter = lax.dynamic_update_slice_in_dim(whole_filter, piece, owner * height, 0)
        return jnp.einsum("lci,oi->lco", lines, whole_filter, preferred_element_type=F32)
    out = None
    for h in range(2):
        aliased = out is not None
        operands = (ids, *firsts, *lasts[h], *filters) + ((out,) if aliased else ())
        call = pl.pallas_call(
            functools.partial(lon_filter_part, h, half_height, cols_count, rows_count, len(firsts), aliased, owners),
            out_shape=shape_of((2 * rows, n_lon)),
            in_specs=[SMEM_SPEC] + [VMEM_SPEC] * (len(firsts) + cols_count + 2 * rows_count) + [ANY_SPEC] * aliased,
            out_specs=ANY_SPEC,
            scratch_shapes=[
                pltpu.VMEM((rows, n_lon), BF16),
                pltpu.VMEM((4, height // LANES, rows, LANES), F32),
                pltpu.SemaphoreType.DMA((4, height // LANES)),
            ],
            input_output_aliases={len(operands) - 1: 0} if aliased else {},
            name="lon_filter",
        )
        out = call(*operands)
    return out.reshape(lat_part, share, n_lon)


def solution(mesh):
    placed = (
        P(None, "col", "row"),
        P(None, None, None, "col", "row"),
        P(None, None, "col", "row"),
        P(None, None, "col", "row"),
        P(None, "col", "row"),
        P(),
        P(),
        P(),
        P(),
        P("row", None),
    )
    return jax.shard_map(shards, mesh=mesh, in_specs=placed, out_specs=P("col", "row", None), check_vma=False)
```

```python
import functools

import jax
import jax.numpy as jnp
from jax import lax
from jax.experimental import pallas as pl
from jax.experimental.pallas import tpu as pltpu
from jax.sharding import PartitionSpec as P


RATIO = 3
BOXX = 256
BOXY = 32
LANES = 128
SUB = 8
BAND = 128
GROUP = 128
GROUP_ONE = 128
UNROLL_ONE = 2
UNROLL_TWO = 2
F32 = jnp.float32
BF16 = jnp.bfloat16
NT = (((1,), (1,)), ((), ()))
HIGHEST = lax.Precision.HIGHEST


def lanes_of(shape):
    return lax.broadcasted_iota(jnp.int32, shape, len(shape) - 1)


def sublanes_of(shape):
    return lax.broadcasted_iota(jnp.int32, shape, len(shape) - 2)


def split(value):
    return [value[:, k * LANES : (k + 1) * LANES] for k in range(value.shape[1] // LANES)]


def rows_at(start):
    return pl.ds(pl.multiple_of(start, SUB), SUB)


def x_fluxes(damped, coef, east):
    flux = coef * damped
    part = east * flux
    return part, flux - part


def stencil(mu, px, qx, up_x, down_x, damped, coef, north, halo_up, halo_down):
    flux = coef * damped
    py = north * flux
    qy = flux - py
    base = mu - px + qx - py + qy + up_x - down_x
    lane = lanes_of((SUB, LANES))
    last, first = lane == LANES - 1, lane == 0
    py, qy, base = split(py), split(qy), split(base)
    rolled_up = [pltpu.roll(v, LANES - 1, 1) for v in py]
    rolled_down = [pltpu.roll(v, 1, 1) for v in qy]
    count = len(base)
    out = []
    for k in range(count):
        above = rolled_up[k + 1] if k + 1 < count else halo_up
        below = rolled_down[k - 1] if k > 0 else halo_down
        out.append(base[k] + jnp.where(last, above, rolled_up[k]) - jnp.where(first, below, rolled_down[k]))
    return out, py, qy


def shifted(px_here, px_next, qx_prev, qx_here):
    sub = sublanes_of(px_here.shape)
    up = jnp.where(sub == SUB - 1, pltpu.roll(px_next, SUB - 1, 0), pltpu.roll(px_here, SUB - 1, 0))
    down = jnp.where(sub == 0, pltpu.roll(qx_prev, 1, 0), pltpu.roll(qx_here, 1, 0))
    return up, down


def first_step(mu_ref, cour_ref, lim_ref, dir_ref, out_ref, ef_ref, em_ref, ew_ref, xr_ref, xm_ref, xw_ref, damp, east, north, rim):
    level = pl.program_id(0)
    fields, _, rows, width = mu_ref.shape
    tiles = width // LANES
    size = min(GROUP_ONE, rows)
    groups = rows // size
    tall = ef_ref.shape[0]
    lane = lanes_of((SUB, LANES))
    last = lane == LANES - 1
    edge = slice((tiles - 1) * LANES, tiles * LANES)

    @pl.when(level == 0)
    def _():
        for ref in (ef_ref, em_ref, ew_ref, xr_ref):
            ref[...] = jnp.zeros_like(ref)

        def prepare(tile, carry):
            at = rows_at(tile * SUB)
            east[at] = dir_ref[1, 0, at].astype(F32)
            north[at] = dir_ref[1, 1, at].astype(F32)
            side = jnp.where(last, 1 - dir_ref[0, 1, at, edge], dir_ref[0, 1, at, :LANES]).astype(F32)
            for f in range(fields):
                damp[f, at] = 0.5 + 0.5 * lim_ref[1, f, at].astype(F32)
                flag = jnp.where(last, lim_ref[0, f, at, edge], lim_ref[0, f, at, :LANES]).astype(F32)
                rim[f, at] = side * (0.5 + 0.5 * flag)
            return carry

        lax.fori_loop(0, rows // SUB, prepare, 0)

    def group(index, carry):
        f, g = index // groups, lax.rem(index, groups)
        base = g * size
        inside = size // SUB
        starts = [jnp.maximum(base - SUB, 0)] + [base + SUB * t for t in range(inside)] + [jnp.minimum(base + size, rows - SUB)]
        keep_low = jnp.where(g > 0, 1.0, 0.0).astype(F32)
        keep_high = jnp.where(g < groups - 1, 1.0, 0.0).astype(F32)
        slot = level * fields + f
        none = jnp.zeros((SUB, LANES), F32)
        mus = [mu_ref[f, 0, rows_at(s)] for s in starts]
        damped = [m * damp[f, rows_at(s)] for m, s in zip(mus, starts)]
        pq = [x_fluxes(m, cour_ref[1, 0, 0, rows_at(s)], east[rows_at(s)]) for m, s in zip(damped, starts)]
        px = [v[0] for v in pq]
        qx = [v[1] for v in pq]
        qx[0] = qx[0] * keep_low
        px[-1] = px[-1] * keep_high
        for t in range(inside):
            at = rows_at(starts[t + 1])
            up, down = shifted(px[t + 1], px[t + 2], qx[t], qx[t + 1])
            new, py, qy = stencil(
                mus[t + 1], px[t + 1], qx[t + 1], up, down, damped[t + 1], cour_ref[1, 1, 0, at], north[at], none, none
            )
            for k in range(tiles):
                out_ref[f, 0, at, k * LANES : (k + 1) * LANES] = new[k]
            band = starts[t + 1] // tall
            turn = (2 * slot + 1 + band * 64) & (LANES - 1)
            mine = (lane // 2) == slot + 32 * band
            weight = jnp.where(last, cour_ref[0, 1, 0, at, edge], cour_ref[0, 1, 0, at, :LANES]) * rim[f, at]
            place = rows_at(lax.rem(starts[t + 1], tall))
            values = (jnp.where(last, qy[-1], py[0]), jnp.where(last, new[-1], new[0]), weight)
            for ref, value in zip((ef_ref, em_ref, ew_ref), values):
                ref[place] = jnp.where(mine, pltpu.roll(value, turn, 1), ref[place])
        return carry

    def groups_at(index, carry):
        for u in range(UNROLL_ONE):
            group(index + u * (fields // UNROLL_ONE) * groups, carry)
        return carry

    lax.fori_loop(0, fields * groups // UNROLL_ONE, groups_at, 0)

    low, high = slice(0, SUB), slice(rows - SUB, rows)
    for f in range(fields):
        slot = level * fields + f
        turn = 2 * slot + 1
        mine = (lane // 2) == slot
        px, _ = x_fluxes(mu_ref[f, 0, low] * damp[f, low], cour_ref[1, 0, 0, low], east[low])
        _, qx = x_fluxes(mu_ref[f, 0, high] * damp[f, high], cour_ref[1, 0, 0, high], east[high])
        xr_ref[level, f : f + 1] = px[:1]
        xr_ref[level, fields + f : fields + f + 1] = qx[SUB - 1 :]
        px_edge = pltpu.roll(jnp.where(last, px[:, edge], px[:, :LANES]), turn, 1)
        qx_edge = pltpu.roll(jnp.where(last, qx[:, edge], qx[:, :LANES]), turn, 1)
        corner = xr_ref.shape[0] - 1
        xr_ref[corner, 0:1, :LANES] = jnp.where(mine, px_edge, jnp.broadcast_to(xr_ref[corner, 0:1, :LANES], (SUB, LANES)))[:1]
        xr_ref[corner, 4:5, :LANES] = jnp.where(mine, qx_edge, jnp.broadcast_to(xr_ref[corner, 4:5, :LANES], (SUB, LANES)))[SUB - 1 :]
        xm_ref[level, f : f + 1] = out_ref[f, 0, low][:1]
        xm_ref[level, fields + f : fields + f + 1] = out_ref[f, 0, high][SUB - 1 :]
        for at, part, row in ((low, 0, 0), (high, 1, SUB - 1)):
            way = dir_ref[0, 0, at].astype(F32)
            way = 1.0 - way if part else way
            value = way * (0.5 + 0.5 * lim_ref[0, f, at].astype(F32)) * cour_ref[0, 0, 0, at]
            xw_ref[level, part * fields + f : part * fields + f + 1] = value[row : row + 1]


def pick(first, a, b):
    return jnp.where(first, a, b)


def rims(rows, parts, ids, efa_ref, efb_ref, xra_ref, xrb_ref, em_ref, ew_ref, xm_ref, xw_ref, eof_ref, e2_ref, x2_ref, m1_ref, x1_ref, kh_ref, kl_ref):
    me_row = ids[0]
    even_row, even_col = ids[2] == 0, ids[3] == 0
    levels, twice, width = xm_ref.shape
    fields = twice // 2
    tiles = width // LANES
    tall = em_ref.shape[0]
    top_band = (rows - 1) // tall
    lane = lanes_of((tall, LANES))
    sub = sublanes_of((tall, LANES))
    up = pick(even_row, efa_ref[...], efb_ref[...])
    down = pick(even_row, efb_ref[...], efa_ref[...])
    merged = jnp.where(lane % 2 == 1, up, -pltpu.roll(down, 2, 1))
    m1_ref[...] = merged
    fixed = em_ref[...] + jnp.where(lane % 2 == 0, pltpu.roll(up, LANES - 1, 1), -pltpu.roll(down, 1, 1))
    corner = xra_ref.shape[0] - 1
    ca, cb = xra_ref[corner, :, :LANES], xrb_ref[corner, :, :LANES]
    corner_up = pick(even_col, ca, cb)[0:1]
    corner_down = pick(even_col, cb, ca)[4:5]
    if top_band:
        corner_up = pltpu.roll(jnp.broadcast_to(corner_up, (SUB, LANES)), 64 * top_band, 1)[:1]
    fixed = fixed + jnp.where(sub == tall - 1, corner_up, 0.0) - jnp.where(sub == 0, corner_down, 0.0)
    e2_ref[...] = ew_ref[...] * fixed

    lane8 = lanes_of((twice, LANES))
    sub8 = sublanes_of((twice, LANES))
    ends = jnp.where(sub8 < fields, jnp.broadcast_to(merged[0:1], (twice, LANES)), jnp.broadcast_to(merged[tall - 1 :], (twice, LANES)))
    wide = sublanes_of((twice, width))
    for level in range(levels):
        a, b = xra_ref[level], xrb_ref[level]
        halo = jnp.where(wide < fields, pick(even_col, a, b), -pick(even_col, b, a))
        x1_ref[level] = halo
        target = 2 * (level * fields + sub8 % fields) + 1 + jnp.where(sub8 >= fields, 64 * top_band, 0)
        at_last = jnp.sum(jnp.where(lane8 == target, ends, 0.0), axis=1, keepdims=True)
        at_first = jnp.sum(jnp.where(lane8 == (target + 1) % LANES, ends, 0.0), axis=1, keepdims=True)
        here = split(xm_ref[level] + pltpu.roll(halo, fields, 0))
        here[-1] = here[-1] + jnp.where(lane8 == LANES - 1, at_last, 0.0)
        here[0] = here[0] + jnp.where(lane8 == 0, at_first, 0.0)
        for k in range(tiles):
            at = slice(k * LANES, (k + 1) * LANES)
            x2_ref[level, :, at] = xw_ref[level, :, at] * here[k]

    channels = eof_ref.shape[0]
    size = kh_ref.shape[0]
    share = channels // parts
    i = lax.broadcasted_iota(jnp.int32, (size, channels), 0) // SUB
    chosen = ((i // share) ^ me_row) * share + i % share
    left = (lax.broadcasted_iota(jnp.int32, (size, channels), 1) == chosen).astype(F32)
    j = lax.broadcasted_iota(jnp.int32, (channels, size), 1) // SUB
    right = (lax.broadcasted_iota(jnp.int32, (channels, size), 0) == j).astype(F32)
    mixed = jnp.dot(left, eof_ref[...], precision=HIGHEST, preferred_element_type=F32)
    spread = jnp.dot(mixed, right, precision=HIGHEST, preferred_element_type=F32)
    same = (lax.broadcasted_iota(jnp.int32, (size, size), 0) - lax.broadcasted_iota(jnp.int32, (size, size), 1)) % SUB == 0
    spread = jnp.where(same, spread, 0.0)
    high = spread.astype(BF16)
    kh_ref[...] = high
    kl_ref[...] = (spread - high.astype(F32)).astype(BF16)


def second_step(
    offset, parts, n_held, ids, mu_ref, mu_low, mu_high, cour_ref, cx_low, cx_high, lim_ref, lim_low, lim_high, dir_ref, dir_low, dir_high,
    m1_ref, x1_ref, e2a_ref, e2b_ref, x2a_ref, x2b_ref, box_ref, kh_ref, kl_ref, *rest,
):
    outs, (damp, east, north, m2_ref, mixed) = rest[n_held:-5], rest[-5:]
    g = pl.program_id(0)
    fields, levels, _, width = mu_ref.shape
    rows = ids[5]
    tall = m1_ref.shape[0]
    even_row, even_col = ids[2] == 0, ids[3] == 0
    tiles = width // LANES
    size = mu_ref.shape[2]
    inside = size // SUB
    lane = lanes_of((SUB, LANES))
    sub = sublanes_of((SUB, width))
    last, first = lane == LANES - 1, lane == 0

    @pl.when(g == 0)
    def _():
        wide = lanes_of((tall, LANES))
        up = pick(even_row, e2a_ref[...], e2b_ref[...])
        down = pick(even_row, e2b_ref[...], e2a_ref[...])
        m2_ref[...] = jnp.where(wide % 2 == 1, up, -pltpu.roll(down, 2, 1))

    lims = [(lim_low, 0)] + [(lim_ref, SUB * t) for t in range(inside)] + [(lim_high, 0)]
    dirs = [(dir_low, 0)] + [(dir_ref, SUB * t) for t in range(inside)] + [(dir_high, 0)]
    mus = [(mu_low, 0)] + [(mu_ref, SUB * t) for t in range(inside)] + [(mu_high, 0)]
    cxs = [(cx_low, 0)] + [(cour_ref, SUB * t) for t in range(inside)] + [(cx_high, 0)]
    for t in range(inside + 2):
        put = slice(SUB * t, SUB * (t + 1))
        ref, r = dirs[t]
        east[put] = ref[0, 0, r : r + SUB].astype(F32)
        if 0 < t <= inside:
            north[SUB * (t - 1) : SUB * t] = ref[0, 1, r : r + SUB].astype(F32)
        ref, r = lims[t]
        for f in range(fields):
            damp[f, put] = 0.5 + 0.5 * ref[0, f, r : r + SUB].astype(F32)

    base = offset + g * size
    starts = [jnp.maximum(base - SUB, 0)] + [base + SUB * t for t in range(inside)] + [jnp.minimum(base + size, rows - SUB)]
    bands = [s // tall for s in starts]
    places = [lax.rem(s, tall) for s in starts]
    at_start = base == 0
    at_end = base + size == rows
    lat_at = ids[7]
    box_lats = box_ref.shape[1] // (fields * levels * parts)
    per_tile = LANES // box_lats
    total = parts * box_lats
    inner = [((lane + LANES * k - lat_at) >= 0) & ((lane + LANES * k - lat_at) < total) for k in range(tiles)]

    def channel(index, carry):
        f, level = index // levels, lax.rem(index, levels)
        slot = level * fields + f
        vals, damped, px, qx = [], [], [], []
        for t in range(inside + 2):
            ref, r = mus[t]
            value = ref[f, level, r : r + SUB]
            fix = pltpu.roll(m1_ref[rows_at(places[t])], (126 - 2 * slot - 64 * bands[t]) & (LANES - 1), 1)
            pieces = split(value)
            pieces[-1] = pieces[-1] + jnp.where(last, fix, 0.0)
            pieces[0] = pieces[0] + jnp.where(first, fix, 0.0)
            value = jnp.concatenate(pieces, axis=1)
            if t == 1:
                value = value + jnp.where((sub == 0) & at_start, x1_ref[level, pl.ds(fields + f, 1)], 0.0)
            if t == inside:
                value = value + jnp.where((sub == SUB - 1) & at_end, x1_ref[level, pl.ds(f, 1)], 0.0)
            ref, r = cxs[t]
            weighed = value * damp[f, SUB * t : SUB * (t + 1)]
            p, q = x_fluxes(weighed, ref[0, 0, level, r : r + SUB], east[SUB * t : SUB * (t + 1)])
            vals.append(value)
            damped.append(weighed)
            px.append(p)
            qx.append(q)
        halo_low = pick(even_col, x2b_ref[level, pl.ds(fields + f, 1)], x2a_ref[level, pl.ds(fields + f, 1)])
        halo_high = pick(even_col, x2a_ref[level, pl.ds(f, 1)], x2b_ref[level, pl.ds(f, 1)])
        qx[0] = jnp.where(at_start, jnp.broadcast_to(halo_low, (SUB, width)), qx[0])
        px[-1] = jnp.where(at_end, jnp.broadcast_to(halo_high, (SUB, width)), px[-1])
        box_tile = pl.multiple_of((index // per_tile * parts + lax.rem(index, parts)) * LANES, LANES)
        box_turn = (lat_at - lax.rem(index, per_tile) * box_lats) & (LANES - 1)
        put = rows_at(index * SUB)
        for t in range(inside):
            mine = slice(SUB * t, SUB * (t + 1))
            up, down = shifted(px[t + 1], px[t + 2], qx[t], qx[t + 1])
            halo = pltpu.roll(m2_ref[rows_at(places[t + 1])], (126 - 2 * slot - 64 * bands[t + 1]) & (LANES - 1), 1)
            new, _, _ = stencil(
                vals[t + 1], px[t + 1], qx[t + 1], up, down, damped[t + 1], cour_ref[0, 1, level, mine], north[mine], halo, -halo
            )
            moved = pltpu.roll(box_ref[mine, pl.ds(box_tile, LANES)], box_turn, 1)
            for k in range(tiles):
                mixed[t, put, k * LANES : (k + 1) * LANES] = new[k] + jnp.where(inner[k], moved, 0.0)
        return carry

    def channels_at(index, carry):
        for u in range(UNROLL_TWO):
            channel(index * UNROLL_TWO + u, carry)
        return carry

    lax.fori_loop(0, fields * levels // UNROLL_TWO, channels_at, 0)

    channels = fields * levels
    share = channels // parts
    per = len(outs) // parts
    depth = share // per
    for v in range(inside // 2):
        both = []
        for t in (2 * v, 2 * v + 1):
            full = mixed[t]
            high = full.astype(BF16)
            low = (full - high.astype(F32)).astype(BF16)
            result = jnp.dot(kh_ref[...], high, preferred_element_type=F32)
            result += jnp.dot(kl_ref[...], high, preferred_element_type=F32)
            result += jnp.dot(kh_ref[...], low, preferred_element_type=F32)
            both.append(result)
        for c in range(channels):
            at = slice(c * SUB, (c + 1) * SUB)
            pair = jnp.concatenate([both[0][at], both[1][at]], axis=0).astype(BF16)
            outs[(c // share) * per + (c % share) // depth][c % depth, 2 * SUB * v : 2 * SUB * (v + 1)] = pair


def coarse_sums(ids, nest_ref, out_ref, held):
    channels, fine_lat, fine_lon = nest_ref.shape
    lon = ids[1] * fine_lon + lax.broadcasted_iota(jnp.int32, (fine_lat, fine_lon), 1)
    lat = ids[0] * fine_lat + lax.broadcasted_iota(jnp.int32, (fine_lat, fine_lon), 0)
    edge = (lon < RATIO) | (lon >= RATIO * BOXX - RATIO) | (lat < RATIO) | (lat >= RATIO * BOXY - RATIO)
    weight = jnp.where(edge, 1.0, 1.0 / (RATIO * RATIO)).astype(F32)
    for c in range(channels):
        held[c * fine_lat : (c + 1) * fine_lat] = nest_ref[c] * weight
    count = channels * fine_lat // RATIO
    sums = held[pl.ds(0, count, stride=RATIO)]
    for a in range(1, RATIO):
        sums = sums + held[pl.ds(a, count, stride=RATIO)]
    shape = (fine_lon // RATIO, fine_lon)
    select = (lax.broadcasted_iota(jnp.int32, shape, 1) // RATIO == lax.broadcasted_iota(jnp.int32, shape, 0)).astype(F32)
    result = lax.dot_general(select, sums, NT, precision=HIGHEST, preferred_element_type=F32)
    for k, piece in enumerate(split(result)):
        out_ref[:, k * LANES : (k + 1) * LANES] = pltpu.roll(piece, (ids[0] * (fine_lat // RATIO)) & (LANES - 1), 1)


def arrange(masks, lats, ids, near_ref, far_ref, out_ref, box):
    half, slab, wide = near_ref.shape
    rows = out_ref.shape[0]
    for p, (row_mask, col_mask) in enumerate(masks):
        at = pl.multiple_of((ids[1] ^ col_mask) * slab, SUB)
        to = pl.multiple_of((ids[0] ^ row_mask) * wide, LANES)
        box[pl.ds(at, slab), pl.ds(to, wide)] = near_ref[p] if p < half else far_ref[p - half]
    height = box.shape[0]
    away = ids[6]
    row = lax.broadcasted_iota(jnp.int32, (rows, LANES), 0) - away
    inside = (row >= 0) & (row < height)
    turn = lax.rem(lax.rem(away, height) + height, height)
    parts = box.shape[1] // wide
    slot = lanes_of((height, LANES)) // lats
    for k in range(wide // LANES):
        pieces = [box[:, r * wide + k * LANES : r * wide + (k + 1) * LANES] for r in range(parts)]
        for m in range(parts):
            value = pieces[0]
            for r in range(1, parts):
                value = jnp.where((slot - m) % parts == r, pieces[r], value)
            at = (k * parts + m) * LANES
            out_ref[:, at : at + LANES] = jnp.where(inside, pltpu.roll(value, turn, 0)[:rows], 0.0)


def lat_filter_part(start, height, count, parts, cols, ids, *refs):
    pieces, filt, outs = refs[:parts], refs[parts], refs[parts + 1 :]
    lat_block = pieces[0].shape[2]
    lon = pieces[0].shape[1]
    lat_part = filt.shape[0] // cols
    step = 2
    for p in range(count // step):
        right = [ref[step * p : step * (p + 1)].reshape(step * lon, lat_block) for ref in pieces]
        for s0 in range(0, cols, 4):
            acc = None
            for r in range(parts):
                at = pl.ds(pl.multiple_of((ids[0] ^ r) * lat_block, LANES), lat_block)
                left = jnp.concatenate(
                    [
                        filt[pl.ds(pl.multiple_of((ids[1] ^ s) * lat_part + start, 16), height), at]
                        for s in range(s0, min(s0 + 4, cols))
                    ],
                    axis=0,
                )
                term = lax.dot_general(left, right[r], NT, preferred_element_type=F32)
                acc = term if acc is None else acc + term
            for s in range(s0, min(s0 + 4, cols)):
                for c in range(step):
                    value = acc[(s - s0) * height : (s - s0 + 1) * height, c * lon : (c + 1) * lon]
                    outs[s][step * p + c] = value.astype(BF16)


def columns(ref, cols, wide, begin, end):
    return jnp.concatenate([ref[:, k * wide + begin : k * wide + end] for k in range(cols)], axis=1)


def lon_first_part(cols, parts, groups, ids, *refs):
    n_first = len(refs) - 2 * parts - 5
    firsts, filters = refs[:n_first], refs[n_first : n_first + 2 * parts]
    outs, (lines, stage, sem) = refs[n_first + 2 * parts : -3], refs[-3:]
    each, height, lon = firsts[0].shape
    half = height // 2
    bands = n_first // cols // groups
    rows = lines.shape[0] // 2
    wide = filters[0].shape[1] // cols

    def flush(p, h):
        return pltpu.make_async_copy(stage.at[p % 2, h], outs[h].at[p], sem.at[p % 2, h])

    for s in range(cols):
        for b in range(bands):
            at = pl.ds(pl.multiple_of(((ids[1] ^ s) * bands + b) * lon, LANES), lon)
            for c in range(each * groups):
                ref = firsts[(b * groups + c // each) * cols + s]
                for h in range(2):
                    put = h * rows + c * half
                    lines[put : put + half, at] = ref[c % each, h * half : (h + 1) * half]
    for p in range(parts):
        right = jnp.concatenate([columns(filters[2 * p + j], cols, wide, 0, bands * lon) for j in range(2)], axis=0)
        acc = lax.dot_general(lines[...], right, NT, preferred_element_type=F32)
        for h in range(2):
            if p >= 2:
                flush(p - 2, h).wait()
            stage[p % 2, h] = acc[h * rows : (h + 1) * rows]
            flush(p, h).start()
    for p in range(max(0, parts - 2), parts):
        for h in range(2):
            flush(p, h).wait()


def lon_filter_part(half, height, cols, parts, n_partial, aliased, owners, ids, *refs):
    partial = refs[:n_partial]
    lasts = refs[n_partial : n_partial + cols]
    filters = refs[n_partial + cols : n_partial + cols + 2 * parts]
    rest = refs[n_partial + cols + 2 * parts + (1 if aliased else 0) :]
    out, lines, stage, sem, earlier, in_sem = rest
    channels, _, lon = lasts[0].shape
    rows = channels * height
    block, total = filters[0].shape
    wide = total // cols
    strips = block // LANES

    def flush(j, k):
        side = ids[8] if j % 2 == 0 else 1 - ids[8]
        even, odd = owners[j // 2]
        owner = (ids[0] ^ jnp.where(side == 0, even, odd)) * 2 + side
        at = pl.ds(pl.multiple_of(owner * block + k * LANES, LANES), LANES)
        slot = j % 4
        return pltpu.make_async_copy(stage.at[slot, k], out.at[pl.ds(half * rows, rows), at], sem.at[slot, k])

    def fetch(p):
        return pltpu.make_async_copy(partial[0].at[p], earlier.at[p % 2], in_sem.at[p % 2])

    if n_partial:
        for p in range(min(2, parts)):
            fetch(p).start()
    for s in range(cols):
        at = pl.ds(pl.multiple_of((ids[1] ^ s) * lon, LANES), lon)
        for c in range(channels):
            lines[c * height : (c + 1) * height, at] = lasts[s][c]
    for p in range(parts):
        right = jnp.concatenate([columns(filters[2 * p + j], cols, wide, wide - lon, wide) for j in range(2)], axis=0)
        acc = lax.dot_general(lines[...], right, NT, preferred_element_type=F32)
        if n_partial:
            fetch(p).wait()
            acc = acc + earlier[p % 2]
        for j in (2 * p, 2 * p + 1):
            for k in range(strips):
                if j >= 4:
                    flush(j - 4, k).wait()
                begin = (j % 2) * block + k * LANES
                for c in range(channels):
                    stage[j % 4, k, pl.ds(c, height, stride=channels), :] = acc[c * height : (c + 1) * height, begin : begin + LANES]
                flush(j, k).start()
        if n_partial and p + 2 < parts:
            fetch(p + 2).start()
    for j in range(max(0, 2 * parts - 4), 2 * parts):
        for k in range(strips):
            flush(j, k).wait()


def swap(value, axis, mask):
    count = lax.axis_size(axis)
    return lax.ppermute(value, axis, [(i, i ^ mask) for i in range(count)])


def neighbours(value, axis, parity):
    count = lax.axis_size(axis)
    pairs = []
    for i in range(parity, count - 1, 2):
        pairs += [(i, i + 1), (i + 1, i)]
    return lax.ppermute(value, axis, pairs)


def shape_of(shape, dtype=F32):
    return jax.ShapeDtypeStruct(shape, dtype)


def whole(shape):
    return pl.BlockSpec(shape, lambda *_: (0,) * len(shape))


VMEM_SPEC = pl.BlockSpec(memory_space=pltpu.VMEM)
SMEM_SPEC = pl.BlockSpec(memory_space=pltpu.SMEM)
ANY_SPEC = pl.BlockSpec(memory_space=pl.ANY)


def shards(final_sens, courant, limiter, directions, nest_sens, box_lon, box_lat, eof, lat_filter, lon_filter):
    channels, lon_block, lat_block = final_sens.shape
    fields, levels = limiter.shape[1], courant.shape[2]
    rows_count, cols_count = lax.axis_size("row"), lax.axis_size("col")
    me_row, me_col = lax.axis_index("row"), lax.axis_index("col")
    ids = jnp.stack(
        [
            me_row,
            me_col,
            me_row % 2,
            me_col % 2,
            me_row * 0,
            me_row * 0 + lon_block,
            box_lon[0] - me_col * lon_block,
            box_lat[0] - me_row * lat_block,
            me_col % 2,
        ]
    ).astype(jnp.int32)
    lat_part = lat_filter.shape[0] // cols_count
    share = channels // rows_count
    tall = min(BAND, lon_block)
    n_bands = lon_block // tall

    height = lon_filter.shape[0] // 2
    gathered = [lax.dynamic_slice_in_dim(lon_filter, (me_col % 2) * height, height, 0)]
    orders = [2**k for k in range(10) if 2**k < rows_count]
    turns = (orders, orders[::-1])
    owners = [(0, 0)]

    def gather(stage, pieces):
        pairs = []
        for i in range(rows_count * cols_count):
            row, col = divmod(i, cols_count)
            pairs.append((i, (row ^ turns[col % 2][stage]) * cols_count + col))
        return [lax.ppermute(piece, ("row", "col"), pairs) for piece in pieces]

    direct = []
    for stage in range(len(orders)):
        direct += gather(stage, gathered[:1])

    nest = jnp.transpose(nest_sens, (0, 2, 1))
    fine_lat, fine_lon = nest.shape[1:]
    coarse = pl.pallas_call(
        coarse_sums,
        out_shape=shape_of((fine_lon // RATIO, channels * fine_lat // RATIO)),
        in_specs=[SMEM_SPEC, VMEM_SPEC],
        out_specs=VMEM_SPEC,
        scratch_shapes=[pltpu.VMEM((channels * fine_lat, fine_lon), F32)],
        name="coarse",
    )(ids, nest)
    masks = [(0, 0)]
    stages = [("col", m) for m in (2**k for k in range(1, 10)) if m < cols_count]
    stages += [("row", m) for m in (2**k for k in range(10)) if m < rows_count]
    stages += [("col", 1)]

    def spread(held, count, last=False):
        nonlocal stages, masks
        for axis, mask in stages[:count]:
            other = swap(held, axis, mask)
            held = (held, other) if last else jnp.concatenate([held, other], axis=0)
            masks = masks + [(r ^ mask, c) if axis == "row" else (r, c ^ mask) for r, c in masks]
        stages = stages[count:]
        return held

    def after(value, *others):
        return lax.optimization_barrier((value, *others))[0]

    held = spread(coarse[None], 2)

    mu = final_sens.reshape(fields, levels, lon_block, lat_block)
    call = pl.pallas_call(
        first_step,
        grid=(levels,),
        out_shape=(
            shape_of(mu.shape),
            shape_of((tall, LANES)),
            shape_of((tall, LANES)),
            shape_of((tall, LANES)),
            shape_of((levels + 1, 2 * fields, lat_block)),
            shape_of((levels, 2 * fields, lat_block)),
            shape_of((levels, 2 * fields, lat_block)),
        ),
        in_specs=[
            pl.BlockSpec((fields, 1, lon_block, lat_block), lambda l: (0, l, 0, 0)),
            pl.BlockSpec((2, 2, 1, lon_block, lat_block), lambda l: (0, 0, l, 0, 0)),
            whole(limiter.shape),
            whole(directions.shape),
        ],
        out_specs=(
            pl.BlockSpec((fields, 1, lon_block, lat_block), lambda l: (0, l, 0, 0)),
            whole((tall, LANES)),
            whole((tall, LANES)),
            whole((tall, LANES)),
            whole((levels + 1, 2 * fields, lat_block)),
            whole((levels, 2 * fields, lat_block)),
            whole((levels, 2 * fields, lat_block)),
        ),
        scratch_shapes=[
            pltpu.VMEM((fields, lon_block, lat_block), F32),
            pltpu.VMEM((lon_block, lat_block), F32),
            pltpu.VMEM((lon_block, lat_block), F32),
            pltpu.VMEM((fields, lon_block, LANES), F32),
        ],
        name="first_step",
    )
    mu1, ef, em, ew, xr, xm, xw = call(mu, courant, limiter, directions)
    held = spread(after(held, ef), 1)
    efa, efb = neighbours(ef, "row", 0), neighbours(ef, "row", 1)
    xra, xrb = neighbours(xr, "col", 0), neighbours(xr, "col", 1)
    held = spread(after(held, efa, efb, xra, xrb), len(stages) - 1)
    size = channels * SUB
    call = pl.pallas_call(
        functools.partial(rims, lon_block, rows_count),
        out_shape=(
            shape_of(ef.shape),
            shape_of(xm.shape),
            shape_of(ef.shape),
            shape_of(xm.shape),
            shape_of((size, size), BF16),
            shape_of((size, size), BF16),
        ),
        in_specs=[SMEM_SPEC] + [VMEM_SPEC] * 9,
        out_specs=(VMEM_SPEC,) * 6,
        name="rims",
    )
    e2, x2, m1, x1, kh, kl = call(ids, efa, efb, xra, xrb, em, ew, xm, xw, eof)
    e2a, e2b = neighbours(e2, "row", 0), neighbours(e2, "row", 1)
    x2a, x2b = neighbours(x2, "col", 0), neighbours(x2, "col", 1)
    held = spread(held, 1, True)
    box = pl.pallas_call(
        functools.partial(arrange, masks, fine_lat // RATIO),
        out_shape=shape_of((lon_block, rows_count * coarse.shape[1])),
        in_specs=[SMEM_SPEC, VMEM_SPEC, VMEM_SPEC],
        out_specs=VMEM_SPEC,
        scratch_shapes=[pltpu.VMEM((cols_count * coarse.shape[0], rows_count * coarse.shape[1]), F32)],
        name="arrange",
    )(ids, *held)

    top = lon_block // SUB - 1

    def control(band, halves, kl, cut=1, part=0, held=()):
        size_two = min(GROUP, tall) // cut
        groups = tall // size_two // cut
        fine = size_two // SUB

        def at(g):
            return (band * cut + part) * groups + g

        def low(g):
            return jnp.maximum(at(g) * fine - 1, 0)

        def high(g):
            return jnp.minimum(at(g) * fine + fine, top)

        depth = share // halves
        return pl.pallas_call(
            functools.partial(second_step, band * tall + part * (tall // cut), rows_count, len(held)),
            grid=(groups,),
            out_shape=(shape_of((depth, tall, lat_block), BF16),) * (rows_count * halves),
            in_specs=[
                SMEM_SPEC,
                pl.BlockSpec((fields, levels, size_two, lat_block), lambda g: (0, 0, at(g), 0)),
                pl.BlockSpec((fields, levels, SUB, lat_block), lambda g: (0, 0, low(g), 0)),
                pl.BlockSpec((fields, levels, SUB, lat_block), lambda g: (0, 0, high(g), 0)),
                pl.BlockSpec((1, 2, levels, size_two, lat_block), lambda g: (0, 0, 0, at(g), 0)),
                pl.BlockSpec((1, 1, levels, SUB, lat_block), lambda g: (0, 0, 0, low(g), 0)),
                pl.BlockSpec((1, 1, levels, SUB, lat_block), lambda g: (0, 0, 0, high(g), 0)),
                pl.BlockSpec((1, fields, size_two, lat_block), lambda g: (0, 0, at(g), 0)),
                pl.BlockSpec((1, fields, SUB, lat_block), lambda g: (0, 0, low(g), 0)),
                pl.BlockSpec((1, fields, SUB, lat_block), lambda g: (0, 0, high(g), 0)),
                pl.BlockSpec((1, 2, size_two, lat_block), lambda g: (0, 0, at(g), 0)),
                pl.BlockSpec((1, 1, SUB, lat_block), lambda g: (0, 0, low(g), 0)),
                pl.BlockSpec((1, 1, SUB, lat_block), lambda g: (0, 0, high(g), 0)),
                whole(m1.shape),
                whole(x1.shape),
                whole(e2.shape),
                whole(e2.shape),
                whole(x2.shape),
                whole(x2.shape),
                pl.BlockSpec((size_two, box.shape[1]), lambda g: (at(g), 0)),
                whole(kh.shape),
                whole(kl.shape),
            ]
            + [ANY_SPEC] * len(held),
            out_specs=(pl.BlockSpec((depth, size_two, lat_block), lambda g: (0, part * groups + g, 0)),) * (rows_count * halves),
            input_output_aliases={22 + i: i for i in range(len(held))},
            scratch_shapes=[
                pltpu.VMEM((fields, size_two + 2 * SUB, lat_block), F32),
                pltpu.VMEM((size_two + 2 * SUB, lat_block), F32),
                pltpu.VMEM((size_two, lat_block), F32),
                pltpu.VMEM((tall, LANES), F32),
                pltpu.VMEM((fine, channels * SUB, lat_block), F32),
            ],
            name="second_step",
        )(ids, mu1, mu1, mu1, courant, courant, courant, limiter, limiter, limiter, directions, directions, directions,
          m1, x1, e2a, e2b, x2a, x2b, box, kh, kl, *held)

    def to_rows(pieces):
        moved = [pieces[0]]
        for s in range(1, rows_count):
            moved.append(swap(pieces[s], "row", s))
        return moved

    def smooth(pieces, start, height, token):
        count = pieces[0].shape[0]
        filt = lat_filter if token is None else after(lat_filter, token)
        call = pl.pallas_call(
            functools.partial(lat_filter_part, start, height, count, rows_count, cols_count),
            out_shape=(shape_of((count, height, tall), BF16),) * cols_count,
            in_specs=[SMEM_SPEC] + [VMEM_SPEC] * (rows_count + 1),
            out_specs=(VMEM_SPEC,) * cols_count,
            name="lat_filter",
        )
        outs = call(ids, *pieces, filt)
        moved = {}
        for s in range(cols_count - 1, 0, -1):
            moved[s] = swap(outs[s], "col", s)
        return [outs[0]] + [moved[s] for s in range(1, cols_count)], outs[-1]

    firsts = []
    sent = []
    order = None
    token = None
    for band in range(n_bands):
        final = band == n_bands - 1
        halves = 1 if final else 2
        if band:
            kl = after(kl, order)
            outs = control(band, halves, kl, 2)
            token = outs[0]
            outs = control(band, halves, kl, 2, 1, outs)
        else:
            outs = control(band, halves, kl)
        order = outs[-1]
        for h in range(halves):
            sent.append(to_rows([outs[s * halves + h] for s in range(rows_count)]))

    for pieces in sent[:-1]:
        moved, token = smooth(pieces, 0, lat_part, token)
        firsts += moved
    half_height = lat_part // 2
    lasts = []
    for h in range(2):
        early = token
        moved, token = smooth(sent[-1], h * half_height, half_height, token)
        lasts.append(moved)
    for stage in range(len(orders)):
        gathered += [direct[stage]] + gather(stage, [after(piece, sent[-1][-1]) for piece in gathered[1:]])
        owners += [(a ^ turns[0][stage], b ^ turns[1][stage]) for a, b in owners]
    filters = []
    for piece in gathered:
        filters += [piece, swap(after(piece, early), "col", 1)]

    n_lon = cols_count * lon_block
    rows = share * half_height
    if lon_block % LANES:
        stacked = jnp.stack([jnp.concatenate([lasts[0][s], lasts[1][s]], axis=1) for s in range(cols_count)])
        lines = jnp.take(stacked, me_col ^ jnp.arange(cols_count), axis=0)
        lines = jnp.transpose(lines, (2, 1, 0, 3)).reshape(lat_part, share, n_lon)
        whole_filter = jnp.zeros((n_lon, n_lon), BF16)
        for j, piece in enumerate(filters):
            side = me_col % 2 if j % 2 == 0 else 1 - me_col % 2
            owner = (me_row ^ jnp.where(side == 0, *owners[j // 2])) * 2 + side
            whole_filter = lax.dynamic_update_slice_in_dim(whole_filter, piece, owner * height, 0)
        return jnp.einsum("lci,oi->lco", lines, whole_filter, preferred_element_type=F32)
    partial = ()
    if firsts:
        call = pl.pallas_call(
            functools.partial(lon_first_part, cols_count, rows_count, 2),
            out_shape=(shape_of((rows_count, rows, 2 * height)),) * 2,
            in_specs=[SMEM_SPEC] + [VMEM_SPEC] * (len(firsts) + 2 * rows_count),
            out_specs=(ANY_SPEC,) * 2,
            scratch_shapes=[
                pltpu.VMEM((2 * rows, n_lon - cols_count * tall), BF16),
                pltpu.VMEM((2, 2, rows, 2 * height), F32),
                pltpu.SemaphoreType.DMA((2, 2)),
            ],
            name="lon_first",
        )
        partial = call(ids, *firsts, *filters)
    out = None
    for h in range(2):
        aliased = out is not None
        held = partial[h : h + 1]
        operands = (ids, *held, *lasts[h], *filters) + ((out,) if aliased else ())
        call = pl.pallas_call(
            functools.partial(lon_filter_part, h, half_height, cols_count, rows_count, len(held), aliased, owners),
            out_shape=shape_of((2 * rows, n_lon)),
            in_specs=[SMEM_SPEC] + [ANY_SPEC] * len(held) + [VMEM_SPEC] * (cols_count + 2 * rows_count) + [ANY_SPEC] * aliased,
            out_specs=ANY_SPEC,
            scratch_shapes=[
                pltpu.VMEM((rows, cols_count * tall), BF16),
                pltpu.VMEM((4, height // LANES, rows, LANES), F32),
                pltpu.SemaphoreType.DMA((4, height // LANES)),
                pltpu.VMEM((2, rows, 2 * height), F32),
                pltpu.SemaphoreType.DMA((2,)),
            ],
            input_output_aliases={len(operands) - 1: 0} if aliased else {},
            name="lon_filter",
        )
        out = call(*operands)
    return out.reshape(lat_part, share, n_lon)


def solution(mesh):
    placed = (
        P(None, "col", "row"),
        P(None, None, None, "col", "row"),
        P(None, None, "col", "row"),
        P(None, None, "col", "row"),
        P(None, "col", "row"),
        P(),
        P(),
        P(),
        P(),
        P("row", None),
    )
    return jax.shard_map(shards, mesh=mesh, in_specs=placed, out_specs=P("col", "row", None), check_vma=False)
```

```python
import functools

import jax
import jax.numpy as jnp
from jax import lax
from jax.experimental import pallas as pl
from jax.experimental.pallas import tpu as pltpu
from jax.sharding import PartitionSpec as P


RATIO = 3
BOXX = 256
BOXY = 32
LANES = 128
SUB = 8
BAND = 128
GROUP = 128
GROUP_ONE = 128
UNROLL_ONE = 2
UNROLL_TWO = 2
F32 = jnp.float32
BF16 = jnp.bfloat16
NT = (((1,), (1,)), ((), ()))
HIGHEST = lax.Precision.HIGHEST


def lanes_of(shape):
    return lax.broadcasted_iota(jnp.int32, shape, len(shape) - 1)


def sublanes_of(shape):
    return lax.broadcasted_iota(jnp.int32, shape, len(shape) - 2)


def split(value):
    return [value[:, k * LANES : (k + 1) * LANES] for k in range(value.shape[1] // LANES)]


def rows_at(start):
    return pl.ds(pl.multiple_of(start, SUB), SUB)


def x_fluxes(damped, coef, east):
    flux = coef * damped
    part = east * flux
    return part, flux - part


def stencil(mu, px, qx, up_x, down_x, damped, coef, north, halo_up, halo_down):
    flux = coef * damped
    py = north * flux
    qy = flux - py
    base = mu - px + qx - py + qy + up_x - down_x
    lane = lanes_of((SUB, LANES))
    last, first = lane == LANES - 1, lane == 0
    py, qy, base = split(py), split(qy), split(base)
    rolled_up = [pltpu.roll(v, LANES - 1, 1) for v in py]
    rolled_down = [pltpu.roll(v, 1, 1) for v in qy]
    count = len(base)
    out = []
    for k in range(count):
        above = rolled_up[k + 1] if k + 1 < count else halo_up
        below = rolled_down[k - 1] if k > 0 else halo_down
        out.append(base[k] + jnp.where(last, above, rolled_up[k]) - jnp.where(first, below, rolled_down[k]))
    return out, py, qy


def shifted(px_here, px_next, qx_prev, qx_here):
    sub = sublanes_of(px_here.shape)
    up = jnp.where(sub == SUB - 1, pltpu.roll(px_next, SUB - 1, 0), pltpu.roll(px_here, SUB - 1, 0))
    down = jnp.where(sub == 0, pltpu.roll(qx_prev, 1, 0), pltpu.roll(qx_here, 1, 0))
    return up, down


def first_step(mu_ref, cour_ref, lim_ref, dir_ref, out_ref, ef_ref, em_ref, ew_ref, xr_ref, xm_ref, xw_ref, damp, east, north, rim):
    level = pl.program_id(0)
    fields, _, rows, width = mu_ref.shape
    tiles = width // LANES
    size = min(GROUP_ONE, rows)
    groups = rows // size
    tall = ef_ref.shape[0]
    lane = lanes_of((SUB, LANES))
    last = lane == LANES - 1
    edge = slice((tiles - 1) * LANES, tiles * LANES)

    @pl.when(level == 0)
    def _():
        for ref in (ef_ref, em_ref, ew_ref, xr_ref):
            ref[...] = jnp.zeros_like(ref)

        def prepare(tile, carry):
            at = rows_at(tile * SUB)
            east[at] = dir_ref[1, 0, at].astype(F32)
            north[at] = dir_ref[1, 1, at].astype(F32)
            side = jnp.where(last, 1 - dir_ref[0, 1, at, edge], dir_ref[0, 1, at, :LANES]).astype(F32)
            for f in range(fields):
                damp[f, at] = 0.5 + 0.5 * lim_ref[1, f, at].astype(F32)
                flag = jnp.where(last, lim_ref[0, f, at, edge], lim_ref[0, f, at, :LANES]).astype(F32)
                rim[f, at] = side * (0.5 + 0.5 * flag)
            return carry

        lax.fori_loop(0, rows // SUB, prepare, 0)

    def group(index, carry):
        f, g = index // groups, lax.rem(index, groups)
        base = g * size
        inside = size // SUB
        starts = [jnp.maximum(base - SUB, 0)] + [base + SUB * t for t in range(inside)] + [jnp.minimum(base + size, rows - SUB)]
        keep_low = jnp.where(g > 0, 1.0, 0.0).astype(F32)
        keep_high = jnp.where(g < groups - 1, 1.0, 0.0).astype(F32)
        slot = level * fields + f
        none = jnp.zeros((SUB, LANES), F32)
        mus = [mu_ref[f, 0, rows_at(s)] for s in starts]
        damped = [m * damp[f, rows_at(s)] for m, s in zip(mus, starts)]
        pq = [x_fluxes(m, cour_ref[1, 0, 0, rows_at(s)], east[rows_at(s)]) for m, s in zip(damped, starts)]
        px = [v[0] for v in pq]
        qx = [v[1] for v in pq]
        qx[0] = qx[0] * keep_low
        px[-1] = px[-1] * keep_high
        for t in range(inside):
            at = rows_at(starts[t + 1])
            up, down = shifted(px[t + 1], px[t + 2], qx[t], qx[t + 1])
            new, py, qy = stencil(
                mus[t + 1], px[t + 1], qx[t + 1], up, down, damped[t + 1], cour_ref[1, 1, 0, at], north[at], none, none
            )
            for k in range(tiles):
                out_ref[f, 0, at, k * LANES : (k + 1) * LANES] = new[k]
            band = starts[t + 1] // tall
            turn = (2 * slot + 1 + band * 64) & (LANES - 1)
            mine = (lane // 2) == slot + 32 * band
            weight = jnp.where(last, cour_ref[0, 1, 0, at, edge], cour_ref[0, 1, 0, at, :LANES]) * rim[f, at]
            place = rows_at(lax.rem(starts[t + 1], tall))
            values = (jnp.where(last, qy[-1], py[0]), jnp.where(last, new[-1], new[0]), weight)
            for ref, value in zip((ef_ref, em_ref, ew_ref), values):
                ref[place] = jnp.where(mine, pltpu.roll(value, turn, 1), ref[place])
        return carry

    def groups_at(index, carry):
        for u in range(UNROLL_ONE):
            group(index + u * (fields // UNROLL_ONE) * groups, carry)
        return carry

    lax.fori_loop(0, fields * groups // UNROLL_ONE, groups_at, 0)

    low, high = slice(0, SUB), slice(rows - SUB, rows)
    for f in range(fields):
        slot = level * fields + f
        turn = 2 * slot + 1
        mine = (lane // 2) == slot
        px, _ = x_fluxes(mu_ref[f, 0, low] * damp[f, low], cour_ref[1, 0, 0, low], east[low])
        _, qx = x_fluxes(mu_ref[f, 0, high] * damp[f, high], cour_ref[1, 0, 0, high], east[high])
        xr_ref[level, f : f + 1] = px[:1]
        xr_ref[level, fields + f : fields + f + 1] = qx[SUB - 1 :]
        px_edge = pltpu.roll(jnp.where(last, px[:, edge], px[:, :LANES]), turn, 1)
        qx_edge = pltpu.roll(jnp.where(last, qx[:, edge], qx[:, :LANES]), turn, 1)
        corner = xr_ref.shape[0] - 1
        xr_ref[corner, 0:1, :LANES] = jnp.where(mine, px_edge, jnp.broadcast_to(xr_ref[corner, 0:1, :LANES], (SUB, LANES)))[:1]
        xr_ref[corner, 4:5, :LANES] = jnp.where(mine, qx_edge, jnp.broadcast_to(xr_ref[corner, 4:5, :LANES], (SUB, LANES)))[SUB - 1 :]
        xm_ref[level, f : f + 1] = out_ref[f, 0, low][:1]
        xm_ref[level, fields + f : fields + f + 1] = out_ref[f, 0, high][SUB - 1 :]
        for at, part, row in ((low, 0, 0), (high, 1, SUB - 1)):
            way = dir_ref[0, 0, at].astype(F32)
            way = 1.0 - way if part else way
            value = way * (0.5 + 0.5 * lim_ref[0, f, at].astype(F32)) * cour_ref[0, 0, 0, at]
            xw_ref[level, part * fields + f : part * fields + f + 1] = value[row : row + 1]


def pick(first, a, b):
    return jnp.where(first, a, b)


def rims(rows, parts, ids, efa_ref, efb_ref, xra_ref, xrb_ref, em_ref, ew_ref, xm_ref, xw_ref, eof_ref, e2_ref, x2_ref, m1_ref, x1_ref, kh_ref, kl_ref):
    me_row = ids[0]
    even_row, even_col = ids[2] == 0, ids[3] == 0
    levels, twice, width = xm_ref.shape
    fields = twice // 2
    tiles = width // LANES
    tall = em_ref.shape[0]
    top_band = (rows - 1) // tall
    lane = lanes_of((tall, LANES))
    sub = sublanes_of((tall, LANES))
    up = pick(even_row, efa_ref[...], efb_ref[...])
    down = pick(even_row, efb_ref[...], efa_ref[...])
    merged = jnp.where(lane % 2 == 1, up, -pltpu.roll(down, 2, 1))
    m1_ref[...] = merged
    fixed = em_ref[...] + jnp.where(lane % 2 == 0, pltpu.roll(up, LANES - 1, 1), -pltpu.roll(down, 1, 1))
    corner = xra_ref.shape[0] - 1
    ca, cb = xra_ref[corner, :, :LANES], xrb_ref[corner, :, :LANES]
    corner_up = pick(even_col, ca, cb)[0:1]
    corner_down = pick(even_col, cb, ca)[4:5]
    if top_band:
        corner_up = pltpu.roll(jnp.broadcast_to(corner_up, (SUB, LANES)), 64 * top_band, 1)[:1]
    fixed = fixed + jnp.where(sub == tall - 1, corner_up, 0.0) - jnp.where(sub == 0, corner_down, 0.0)
    e2_ref[...] = ew_ref[...] * fixed

    lane8 = lanes_of((twice, LANES))
    sub8 = sublanes_of((twice, LANES))
    ends = jnp.where(sub8 < fields, jnp.broadcast_to(merged[0:1], (twice, LANES)), jnp.broadcast_to(merged[tall - 1 :], (twice, LANES)))
    wide = sublanes_of((twice, width))
    for level in range(levels):
        a, b = xra_ref[level], xrb_ref[level]
        halo = jnp.where(wide < fields, pick(even_col, a, b), -pick(even_col, b, a))
        x1_ref[level] = halo
        target = 2 * (level * fields + sub8 % fields) + 1 + jnp.where(sub8 >= fields, 64 * top_band, 0)
        at_last = jnp.sum(jnp.where(lane8 == target, ends, 0.0), axis=1, keepdims=True)
        at_first = jnp.sum(jnp.where(lane8 == (target + 1) % LANES, ends, 0.0), axis=1, keepdims=True)
        here = split(xm_ref[level] + pltpu.roll(halo, fields, 0))
        here[-1] = here[-1] + jnp.where(lane8 == LANES - 1, at_last, 0.0)
        here[0] = here[0] + jnp.where(lane8 == 0, at_first, 0.0)
        for k in range(tiles):
            at = slice(k * LANES, (k + 1) * LANES)
            x2_ref[level, :, at] = xw_ref[level, :, at] * here[k]

    channels = eof_ref.shape[0]
    size = kh_ref.shape[0]
    share = channels // parts
    i = lax.broadcasted_iota(jnp.int32, (size, channels), 0) // SUB
    chosen = ((i // share) ^ me_row) * share + i % share
    left = (lax.broadcasted_iota(jnp.int32, (size, channels), 1) == chosen).astype(F32)
    j = lax.broadcasted_iota(jnp.int32, (channels, size), 1) // SUB
    right = (lax.broadcasted_iota(jnp.int32, (channels, size), 0) == j).astype(F32)
    mixed = jnp.dot(left, eof_ref[...], precision=HIGHEST, preferred_element_type=F32)
    spread = jnp.dot(mixed, right, precision=HIGHEST, preferred_element_type=F32)
    same = (lax.broadcasted_iota(jnp.int32, (size, size), 0) - lax.broadcasted_iota(jnp.int32, (size, size), 1)) % SUB == 0
    spread = jnp.where(same, spread, 0.0)
    high = spread.astype(BF16)
    kh_ref[...] = high
    kl_ref[...] = (spread - high.astype(F32)).astype(BF16)


def second_step(
    offset, parts, n_held, ids, mu_ref, mu_low, mu_high, cour_ref, cx_low, cx_high, lim_ref, lim_low, lim_high, dir_ref, dir_low, dir_high,
    m1_ref, x1_ref, e2a_ref, e2b_ref, x2a_ref, x2b_ref, box_ref, kh_ref, kl_ref, *rest,
):
    outs, (damp, east, north, m2_ref, mixed) = rest[n_held:-5], rest[-5:]
    g = pl.program_id(0)
    fields, levels, _, width = mu_ref.shape
    rows = ids[5]
    tall = m1_ref.shape[0]
    even_row, even_col = ids[2] == 0, ids[3] == 0
    tiles = width // LANES
    size = mu_ref.shape[2]
    inside = size // SUB
    lane = lanes_of((SUB, LANES))
    sub = sublanes_of((SUB, width))
    last, first = lane == LANES - 1, lane == 0

    @pl.when(g == 0)
    def _():
        wide = lanes_of((tall, LANES))
        up = pick(even_row, e2a_ref[...], e2b_ref[...])
        down = pick(even_row, e2b_ref[...], e2a_ref[...])
        m2_ref[...] = jnp.where(wide % 2 == 1, up, -pltpu.roll(down, 2, 1))

    lims = [(lim_low, 0)] + [(lim_ref, SUB * t) for t in range(inside)] + [(lim_high, 0)]
    dirs = [(dir_low, 0)] + [(dir_ref, SUB * t) for t in range(inside)] + [(dir_high, 0)]
    mus = [(mu_low, 0)] + [(mu_ref, SUB * t) for t in range(inside)] + [(mu_high, 0)]
    cxs = [(cx_low, 0)] + [(cour_ref, SUB * t) for t in range(inside)] + [(cx_high, 0)]
    for t in range(inside + 2):
        put = slice(SUB * t, SUB * (t + 1))
        ref, r = dirs[t]
        east[put] = ref[0, 0, r : r + SUB].astype(F32)
        if 0 < t <= inside:
            north[SUB * (t - 1) : SUB * t] = ref[0, 1, r : r + SUB].astype(F32)
        ref, r = lims[t]
        for f in range(fields):
            damp[f, put] = 0.5 + 0.5 * ref[0, f, r : r + SUB].astype(F32)

    base = offset + g * size
    starts = [jnp.maximum(base - SUB, 0)] + [base + SUB * t for t in range(inside)] + [jnp.minimum(base + size, rows - SUB)]
    bands = [s // tall for s in starts]
    places = [lax.rem(s, tall) for s in starts]
    at_start = base == 0
    at_end = base + size == rows
    lat_at = ids[7]
    box_lats = box_ref.shape[1] // (fields * levels * parts)
    per_tile = LANES // box_lats
    total = parts * box_lats
    inner = [((lane + LANES * k - lat_at) >= 0) & ((lane + LANES * k - lat_at) < total) for k in range(tiles)]

    def channel(index, carry):
        f, level = index // levels, lax.rem(index, levels)
        slot = level * fields + f
        vals, damped, px, qx = [], [], [], []
        for t in range(inside + 2):
            ref, r = mus[t]
            value = ref[f, level, r : r + SUB]
            fix = pltpu.roll(m1_ref[rows_at(places[t])], (126 - 2 * slot - 64 * bands[t]) & (LANES - 1), 1)
            pieces = split(value)
            pieces[-1] = pieces[-1] + jnp.where(last, fix, 0.0)
            pieces[0] = pieces[0] + jnp.where(first, fix, 0.0)
            value = jnp.concatenate(pieces, axis=1)
            if t == 1:
                value = value + jnp.where((sub == 0) & at_start, x1_ref[level, pl.ds(fields + f, 1)], 0.0)
            if t == inside:
                value = value + jnp.where((sub == SUB - 1) & at_end, x1_ref[level, pl.ds(f, 1)], 0.0)
            ref, r = cxs[t]
            weighed = value * damp[f, SUB * t : SUB * (t + 1)]
            p, q = x_fluxes(weighed, ref[0, 0, level, r : r + SUB], east[SUB * t : SUB * (t + 1)])
            vals.append(value)
            damped.append(weighed)
            px.append(p)
            qx.append(q)
        halo_low = pick(even_col, x2b_ref[level, pl.ds(fields + f, 1)], x2a_ref[level, pl.ds(fields + f, 1)])
        halo_high = pick(even_col, x2a_ref[level, pl.ds(f, 1)], x2b_ref[level, pl.ds(f, 1)])
        qx[0] = jnp.where(at_start, jnp.broadcast_to(halo_low, (SUB, width)), qx[0])
        px[-1] = jnp.where(at_end, jnp.broadcast_to(halo_high, (SUB, width)), px[-1])
        box_tile = pl.multiple_of((index // per_tile * parts + lax.rem(index, parts)) * LANES, LANES)
        box_turn = (lat_at - lax.rem(index, per_tile) * box_lats) & (LANES - 1)
        put = rows_at(index * SUB)
        for t in range(inside):
            mine = slice(SUB * t, SUB * (t + 1))
            up, down = shifted(px[t + 1], px[t + 2], qx[t], qx[t + 1])
            halo = pltpu.roll(m2_ref[rows_at(places[t + 1])], (126 - 2 * slot - 64 * bands[t + 1]) & (LANES - 1), 1)
            new, _, _ = stencil(
                vals[t + 1], px[t + 1], qx[t + 1], up, down, damped[t + 1], cour_ref[0, 1, level, mine], north[mine], halo, -halo
            )
            moved = pltpu.roll(box_ref[mine, pl.ds(box_tile, LANES)], box_turn, 1)
            for k in range(tiles):
                mixed[t, put, k * LANES : (k + 1) * LANES] = new[k] + jnp.where(inner[k], moved, 0.0)
        return carry

    def channels_at(index, carry):
        for u in range(UNROLL_TWO):
            channel(index * UNROLL_TWO + u, carry)
        return carry

    lax.fori_loop(0, fields * levels // UNROLL_TWO, channels_at, 0)

    channels = fields * levels
    share = channels // parts
    per = len(outs) // parts
    depth = share // per
    for v in range(inside // 2):
        both = []
        for t in (2 * v, 2 * v + 1):
            full = mixed[t]
            high = full.astype(BF16)
            low = (full - high.astype(F32)).astype(BF16)
            result = jnp.dot(kh_ref[...], high, preferred_element_type=F32)
            result += jnp.dot(kl_ref[...], high, preferred_element_type=F32)
            result += jnp.dot(kh_ref[...], low, preferred_element_type=F32)
            both.append(result)
        for c in range(channels):
            at = slice(c * SUB, (c + 1) * SUB)
            pair = jnp.concatenate([both[0][at], both[1][at]], axis=0).astype(BF16)
            outs[(c // share) * per + (c % share) // depth][c % depth, 2 * SUB * v : 2 * SUB * (v + 1)] = pair


def coarse_sums(ids, nest_ref, out_ref, held):
    channels, fine_lat, fine_lon = nest_ref.shape
    lon = ids[1] * fine_lon + lax.broadcasted_iota(jnp.int32, (fine_lat, fine_lon), 1)
    lat = ids[0] * fine_lat + lax.broadcasted_iota(jnp.int32, (fine_lat, fine_lon), 0)
    edge = (lon < RATIO) | (lon >= RATIO * BOXX - RATIO) | (lat < RATIO) | (lat >= RATIO * BOXY - RATIO)
    weight = jnp.where(edge, 1.0, 1.0 / (RATIO * RATIO)).astype(F32)
    for c in range(channels):
        held[c * fine_lat : (c + 1) * fine_lat] = nest_ref[c] * weight
    count = channels * fine_lat // RATIO
    sums = held[pl.ds(0, count, stride=RATIO)]
    for a in range(1, RATIO):
        sums = sums + held[pl.ds(a, count, stride=RATIO)]
    shape = (fine_lon // RATIO, fine_lon)
    select = (lax.broadcasted_iota(jnp.int32, shape, 1) // RATIO == lax.broadcasted_iota(jnp.int32, shape, 0)).astype(F32)
    result = lax.dot_general(select, sums, NT, precision=HIGHEST, preferred_element_type=F32)
    for k, piece in enumerate(split(result)):
        out_ref[:, k * LANES : (k + 1) * LANES] = pltpu.roll(piece, (ids[0] * (fine_lat // RATIO)) & (LANES - 1), 1)


def arrange(masks, lats, ids, near_ref, far_ref, out_ref, box):
    half, slab, wide = near_ref.shape
    rows = out_ref.shape[0]
    for p, (row_mask, col_mask) in enumerate(masks):
        at = pl.multiple_of((ids[1] ^ col_mask) * slab, SUB)
        to = pl.multiple_of((ids[0] ^ row_mask) * wide, LANES)
        box[pl.ds(at, slab), pl.ds(to, wide)] = near_ref[p] if p < half else far_ref[p - half]
    height = box.shape[0]
    away = ids[6]
    row = lax.broadcasted_iota(jnp.int32, (rows, LANES), 0) - away
    inside = (row >= 0) & (row < height)
    turn = lax.rem(lax.rem(away, height) + height, height)
    parts = box.shape[1] // wide
    slot = lanes_of((height, LANES)) // lats
    for k in range(wide // LANES):
        pieces = [box[:, r * wide + k * LANES : r * wide + (k + 1) * LANES] for r in range(parts)]
        for m in range(parts):
            value = pieces[0]
            for r in range(1, parts):
                value = jnp.where((slot - m) % parts == r, pieces[r], value)
            at = (k * parts + m) * LANES
            out_ref[:, at : at + LANES] = jnp.where(inside, pltpu.roll(value, turn, 0)[:rows], 0.0)


def lat_filter_part(start, height, count, parts, cols, ids, *refs):
    pieces, filt, outs = refs[:parts], refs[parts], refs[parts + 1 :]
    lat_block = pieces[0].shape[2]
    lon = pieces[0].shape[1]
    lat_part = filt.shape[0] // cols
    step = 2
    for p in range(count // step):
        right = [ref[step * p : step * (p + 1)].reshape(step * lon, lat_block) for ref in pieces]
        for s0 in range(0, cols, 4):
            acc = None
            for r in range(parts):
                at = pl.ds(pl.multiple_of((ids[0] ^ r) * lat_block, LANES), lat_block)
                left = jnp.concatenate(
                    [
                        filt[pl.ds(pl.multiple_of((ids[1] ^ s) * lat_part + start, 16), height), at]
                        for s in range(s0, min(s0 + 4, cols))
                    ],
                    axis=0,
                )
                term = lax.dot_general(left, right[r], NT, preferred_element_type=F32)
                acc = term if acc is None else acc + term
            for s in range(s0, min(s0 + 4, cols)):
                for c in range(step):
                    value = acc[(s - s0) * height : (s - s0 + 1) * height, c * lon : (c + 1) * lon]
                    outs[s][step * p + c] = value.astype(BF16)


def lon_filter_part(half, height, cols, parts, n_first, aliased, owners, ids, *refs):
    firsts = refs[:n_first]
    lasts = refs[n_first : n_first + cols]
    filters = refs[n_first + cols : n_first + cols + 2 * parts]
    rest = refs[n_first + cols + 2 * parts + (1 if aliased else 0) :]
    out, lines, stage, sem, held, in_sem = rest
    channels, _, lon = lasts[0].shape
    wide = lines.shape[1] // cols
    rows = channels * height
    block = filters[0].shape[0]
    strips = block // LANES

    def flush(j, k):
        side = ids[8] if j % 2 == 0 else 1 - ids[8]
        even, odd = owners[j // 2]
        owner = (ids[0] ^ jnp.where(side == 0, even, odd)) * 2 + side
        at = pl.ds(pl.multiple_of(owner * block + k * LANES, LANES), LANES)
        slot = j % 4
        return pltpu.make_async_copy(stage.at[slot, k], out.at[pl.ds(half * rows, rows), at], sem.at[slot, k])

    def fetch(j):
        return pltpu.make_async_copy(filters[j], held.at[pl.ds(j * block, block)], in_sem.at[j])

    for j in range(2 * parts):
        fetch(j).start()
    for s in range(cols):
        base = pl.multiple_of((ids[1] ^ s) * wide, LANES)
        for c in range(channels):
            put = slice(c * height, (c + 1) * height)
            for b in range(wide // lon - 1):
                groups = n_first // cols // (wide // lon - 1)
                each = channels // groups
                ref = firsts[(b * groups + c // each) * cols + s]
                lines[put, pl.ds(base + b * lon, lon)] = ref[c % each, half * height : (half + 1) * height]
            lines[put, pl.ds(base + wide - lon, lon)] = lasts[s][c]
    for p in range(parts):
        fetch(2 * p).wait()
        fetch(2 * p + 1).wait()
        right = held[2 * p * block : (2 * p + 2) * block]
        acc = lax.dot_general(lines[...], right, NT, preferred_element_type=F32)
        for j in (2 * p, 2 * p + 1):
            for k in range(strips):
                if j >= 4:
                    flush(j - 4, k).wait()
                begin = (j % 2) * block + k * LANES
                for c in range(channels):
                    stage[j % 4, k, pl.ds(c, height, stride=channels), :] = acc[c * height : (c + 1) * height, begin : begin + LANES]
                flush(j, k).start()
    for j in range(max(0, 2 * parts - 4), 2 * parts):
        for k in range(strips):
            flush(j, k).wait()


def swap(value, axis, mask):
    count = lax.axis_size(axis)
    return lax.ppermute(value, axis, [(i, i ^ mask) for i in range(count)])


def neighbours(value, axis, parity):
    count = lax.axis_size(axis)
    pairs = []
    for i in range(parity, count - 1, 2):
        pairs += [(i, i + 1), (i + 1, i)]
    return lax.ppermute(value, axis, pairs)


def shape_of(shape, dtype=F32):
    return jax.ShapeDtypeStruct(shape, dtype)


def whole(shape):
    return pl.BlockSpec(shape, lambda *_: (0,) * len(shape))


VMEM_SPEC = pl.BlockSpec(memory_space=pltpu.VMEM)
SMEM_SPEC = pl.BlockSpec(memory_space=pltpu.SMEM)
ANY_SPEC = pl.BlockSpec(memory_space=pl.ANY)


def shards(final_sens, courant, limiter, directions, nest_sens, box_lon, box_lat, eof, lat_filter, lon_filter):
    channels, lon_block, lat_block = final_sens.shape
    fields, levels = limiter.shape[1], courant.shape[2]
    rows_count, cols_count = lax.axis_size("row"), lax.axis_size("col")
    me_row, me_col = lax.axis_index("row"), lax.axis_index("col")
    ids = jnp.stack(
        [
            me_row,
            me_col,
            me_row % 2,
            me_col % 2,
            me_row * 0,
            me_row * 0 + lon_block,
            box_lon[0] - me_col * lon_block,
            box_lat[0] - me_row * lat_block,
            me_col % 2,
        ]
    ).astype(jnp.int32)
    lat_part = lat_filter.shape[0] // cols_count
    share = channels // rows_count
    tall = min(BAND, lon_block)
    n_bands = lon_block // tall

    height = lon_filter.shape[0] // 2
    gathered = [lax.dynamic_slice_in_dim(lon_filter, (me_col % 2) * height, height, 0)]
    orders = [2**k for k in range(10) if 2**k < rows_count]
    turns = (orders, orders[::-1])
    owners = [(0, 0)]

    def gather(stage, pieces):
        pairs = []
        for i in range(rows_count * cols_count):
            row, col = divmod(i, cols_count)
            pairs.append((i, (row ^ turns[col % 2][stage]) * cols_count + col))
        return [lax.ppermute(piece, ("row", "col"), pairs) for piece in pieces]

    direct = []
    for stage in range(len(orders)):
        direct += gather(stage, gathered[:1])

    nest = jnp.transpose(nest_sens, (0, 2, 1))
    fine_lat, fine_lon = nest.shape[1:]
    coarse = pl.pallas_call(
        coarse_sums,
        out_shape=shape_of((fine_lon // RATIO, channels * fine_lat // RATIO)),
        in_specs=[SMEM_SPEC, VMEM_SPEC],
        out_specs=VMEM_SPEC,
        scratch_shapes=[pltpu.VMEM((channels * fine_lat, fine_lon), F32)],
        name="coarse",
    )(ids, nest)
    masks = [(0, 0)]
    stages = [("col", m) for m in (2**k for k in range(1, 10)) if m < cols_count]
    stages += [("row", m) for m in (2**k for k in range(10)) if m < rows_count]
    stages += [("col", 1)]

    def spread(held, count, last=False):
        nonlocal stages, masks
        for axis, mask in stages[:count]:
            other = swap(held, axis, mask)
            held = (held, other) if last else jnp.concatenate([held, other], axis=0)
            masks = masks + [(r ^ mask, c) if axis == "row" else (r, c ^ mask) for r, c in masks]
        stages = stages[count:]
        return held

    def after(value, *others):
        return lax.optimization_barrier((value, *others))[0]

    held = spread(coarse[None], 2)

    mu = final_sens.reshape(fields, levels, lon_block, lat_block)
    call = pl.pallas_call(
        first_step,
        grid=(levels,),
        out_shape=(
            shape_of(mu.shape),
            shape_of((tall, LANES)),
            shape_of((tall, LANES)),
            shape_of((tall, LANES)),
            shape_of((levels + 1, 2 * fields, lat_block)),
            shape_of((levels, 2 * fields, lat_block)),
            shape_of((levels, 2 * fields, lat_block)),
        ),
        in_specs=[
            pl.BlockSpec((fields, 1, lon_block, lat_block), lambda l: (0, l, 0, 0)),
            pl.BlockSpec((2, 2, 1, lon_block, lat_block), lambda l: (0, 0, l, 0, 0)),
            whole(limiter.shape),
            whole(directions.shape),
        ],
        out_specs=(
            pl.BlockSpec((fields, 1, lon_block, lat_block), lambda l: (0, l, 0, 0)),
            whole((tall, LANES)),
            whole((tall, LANES)),
            whole((tall, LANES)),
            whole((levels + 1, 2 * fields, lat_block)),
            whole((levels, 2 * fields, lat_block)),
            whole((levels, 2 * fields, lat_block)),
        ),
        scratch_shapes=[
            pltpu.VMEM((fields, lon_block, lat_block), F32),
            pltpu.VMEM((lon_block, lat_block), F32),
            pltpu.VMEM((lon_block, lat_block), F32),
            pltpu.VMEM((fields, lon_block, LANES), F32),
        ],
        name="first_step",
    )
    mu1, ef, em, ew, xr, xm, xw = call(mu, courant, limiter, directions)
    held = spread(after(held, ef), 1)
    efa, efb = neighbours(ef, "row", 0), neighbours(ef, "row", 1)
    xra, xrb = neighbours(xr, "col", 0), neighbours(xr, "col", 1)
    held = spread(after(held, efa, efb, xra, xrb), len(stages) - 1)
    size = channels * SUB
    call = pl.pallas_call(
        functools.partial(rims, lon_block, rows_count),
        out_shape=(
            shape_of(ef.shape),
            shape_of(xm.shape),
            shape_of(ef.shape),
            shape_of(xm.shape),
            shape_of((size, size), BF16),
            shape_of((size, size), BF16),
        ),
        in_specs=[SMEM_SPEC] + [VMEM_SPEC] * 9,
        out_specs=(VMEM_SPEC,) * 6,
        name="rims",
    )
    e2, x2, m1, x1, kh, kl = call(ids, efa, efb, xra, xrb, em, ew, xm, xw, eof)
    e2a, e2b = neighbours(e2, "row", 0), neighbours(e2, "row", 1)
    x2a, x2b = neighbours(x2, "col", 0), neighbours(x2, "col", 1)
    held = spread(held, 1, True)
    box = pl.pallas_call(
        functools.partial(arrange, masks, fine_lat // RATIO),
        out_shape=shape_of((lon_block, rows_count * coarse.shape[1])),
        in_specs=[SMEM_SPEC, VMEM_SPEC, VMEM_SPEC],
        out_specs=VMEM_SPEC,
        scratch_shapes=[pltpu.VMEM((cols_count * coarse.shape[0], rows_count * coarse.shape[1]), F32)],
        name="arrange",
    )(ids, *held)

    top = lon_block // SUB - 1

    def control(band, halves, kl, cut=1, part=0, held=()):
        size_two = min(GROUP, tall) // cut
        groups = tall // size_two // cut
        fine = size_two // SUB

        def at(g):
            return (band * cut + part) * groups + g

        def low(g):
            return jnp.maximum(at(g) * fine - 1, 0)

        def high(g):
            return jnp.minimum(at(g) * fine + fine, top)

        depth = share // halves
        return pl.pallas_call(
            functools.partial(second_step, band * tall + part * (tall // cut), rows_count, len(held)),
            grid=(groups,),
            out_shape=(shape_of((depth, tall, lat_block), BF16),) * (rows_count * halves),
            in_specs=[
                SMEM_SPEC,
                pl.BlockSpec((fields, levels, size_two, lat_block), lambda g: (0, 0, at(g), 0)),
                pl.BlockSpec((fields, levels, SUB, lat_block), lambda g: (0, 0, low(g), 0)),
                pl.BlockSpec((fields, levels, SUB, lat_block), lambda g: (0, 0, high(g), 0)),
                pl.BlockSpec((1, 2, levels, size_two, lat_block), lambda g: (0, 0, 0, at(g), 0)),
                pl.BlockSpec((1, 1, levels, SUB, lat_block), lambda g: (0, 0, 0, low(g), 0)),
                pl.BlockSpec((1, 1, levels, SUB, lat_block), lambda g: (0, 0, 0, high(g), 0)),
                pl.BlockSpec((1, fields, size_two, lat_block), lambda g: (0, 0, at(g), 0)),
                pl.BlockSpec((1, fields, SUB, lat_block), lambda g: (0, 0, low(g), 0)),
                pl.BlockSpec((1, fields, SUB, lat_block), lambda g: (0, 0, high(g), 0)),
                pl.BlockSpec((1, 2, size_two, lat_block), lambda g: (0, 0, at(g), 0)),
                pl.BlockSpec((1, 1, SUB, lat_block), lambda g: (0, 0, low(g), 0)),
                pl.BlockSpec((1, 1, SUB, lat_block), lambda g: (0, 0, high(g), 0)),
                whole(m1.shape),
                whole(x1.shape),
                whole(e2.shape),
                whole(e2.shape),
                whole(x2.shape),
                whole(x2.shape),
                pl.BlockSpec((size_two, box.shape[1]), lambda g: (at(g), 0)),
                whole(kh.shape),
                whole(kl.shape),
            ]
            + [ANY_SPEC] * len(held),
            out_specs=(pl.BlockSpec((depth, size_two, lat_block), lambda g: (0, part * groups + g, 0)),) * (rows_count * halves),
            input_output_aliases={22 + i: i for i in range(len(held))},
            scratch_shapes=[
                pltpu.VMEM((fields, size_two + 2 * SUB, lat_block), F32),
                pltpu.VMEM((size_two + 2 * SUB, lat_block), F32),
                pltpu.VMEM((size_two, lat_block), F32),
                pltpu.VMEM((tall, LANES), F32),
                pltpu.VMEM((fine, channels * SUB, lat_block), F32),
            ],
            name="second_step",
        )(ids, mu1, mu1, mu1, courant, courant, courant, limiter, limiter, limiter, directions, directions, directions,
          m1, x1, e2a, e2b, x2a, x2b, box, kh, kl, *held)

    def to_rows(pieces):
        moved = [pieces[0]]
        for s in range(1, rows_count):
            moved.append(swap(pieces[s], "row", s))
        return moved

    def smooth(pieces, start, height, token):
        count = pieces[0].shape[0]
        filt = lat_filter if token is None else after(lat_filter, token)
        call = pl.pallas_call(
            functools.partial(lat_filter_part, start, height, count, rows_count, cols_count),
            out_shape=(shape_of((count, height, tall), BF16),) * cols_count,
            in_specs=[SMEM_SPEC] + [VMEM_SPEC] * (rows_count + 1),
            out_specs=(VMEM_SPEC,) * cols_count,
            name="lat_filter",
        )
        outs = call(ids, *pieces, filt)
        moved = {}
        for s in range(cols_count - 1, 0, -1):
            moved[s] = swap(outs[s], "col", s)
        return [outs[0]] + [moved[s] for s in range(1, cols_count)], outs[-1]

    firsts = []
    sent = []
    order = None
    token = None
    for band in range(n_bands):
        final = band == n_bands - 1
        halves = 1 if final else 2
        if band:
            kl = after(kl, order)
            outs = control(band, halves, kl, 2)
            token = outs[0]
            outs = control(band, halves, kl, 2, 1, outs)
        else:
            outs = control(band, halves, kl)
        order = outs[-1]
        for h in range(halves):
            sent.append(to_rows([outs[s * halves + h] for s in range(rows_count)]))

    for pieces in sent[:-1]:
        moved, token = smooth(pieces, 0, lat_part, token)
        firsts += moved
    half_height = lat_part // 2
    lasts = []
    for h in range(2):
        early = token
        moved, token = smooth(sent[-1], h * half_height, half_height, token)
        lasts.append(moved)
    for stage in range(len(orders)):
        gathered += [direct[stage]] + gather(stage, [after(piece, early) for piece in gathered[1:]])
        owners += [(a ^ turns[0][stage], b ^ turns[1][stage]) for a, b in owners]
    filters = []
    for j, piece in enumerate(gathered):
        late = j and j == len(gathered) - 1
        filters += [piece, swap(after(piece, token if late else early), "col", 1)]

    n_lon = cols_count * lon_block
    rows = share * half_height
    if lon_block % LANES:
        stacked = jnp.stack([jnp.concatenate([lasts[0][s], lasts[1][s]], axis=1) for s in range(cols_count)])
        lines = jnp.take(stacked, me_col ^ jnp.arange(cols_count), axis=0)
        lines = jnp.transpose(lines, (2, 1, 0, 3)).reshape(lat_part, share, n_lon)
        whole_filter = jnp.zeros((n_lon, n_lon), BF16)
        for j, piece in enumerate(filters):
            side = me_col % 2 if j % 2 == 0 else 1 - me_col % 2
            owner = (me_row ^ jnp.where(side == 0, *owners[j // 2])) * 2 + side
            whole_filter = lax.dynamic_update_slice_in_dim(whole_filter, piece, owner * height, 0)
        return jnp.einsum("lci,oi->lco", lines, whole_filter, preferred_element_type=F32)
    out = None
    for h in range(2):
        aliased = out is not None
        operands = (ids, *firsts, *lasts[h], *filters) + ((out,) if aliased else ())
        call = pl.pallas_call(
            functools.partial(lon_filter_part, h, half_height, cols_count, rows_count, len(firsts), aliased, owners),
            out_shape=shape_of((2 * rows, n_lon)),
            in_specs=[SMEM_SPEC] + [VMEM_SPEC] * (len(firsts) + cols_count) + [ANY_SPEC] * (2 * rows_count + aliased),
            out_specs=ANY_SPEC,
            scratch_shapes=[
                pltpu.VMEM((rows, n_lon), BF16),
                pltpu.VMEM((4, height // LANES, rows, LANES), F32),
                pltpu.SemaphoreType.DMA((4, height // LANES)),
                pltpu.VMEM((2 * rows_count * height, n_lon), BF16),
                pltpu.SemaphoreType.DMA((2 * rows_count,)),
            ],
            input_output_aliases={len(operands) - 1: 0} if aliased else {},
            name="lon_filter",
        )
        out = call(*operands)
    return out.reshape(lat_part, share, n_lon)


def solution(mesh):
    placed = (
        P(None, "col", "row"),
        P(None, None, None, "col", "row"),
        P(None, None, "col", "row"),
        P(None, None, "col", "row"),
        P(None, "col", "row"),
        P(),
        P(),
        P(),
        P(),
        P("row", None),
    )
    return jax.shard_map(shards, mesh=mesh, in_specs=placed, out_specs=P("col", "row", None), check_vma=False)
```

```python
import functools

import jax
import jax.numpy as jnp
from jax import lax
from jax.experimental import pallas as pl
from jax.experimental.pallas import tpu as pltpu
from jax.sharding import PartitionSpec as P


RATIO = 3
BOXX = 256
BOXY = 32
LANES = 128
SUB = 8
BAND = 128
GROUP = 128
GROUP_ONE = 128
UNROLL_ONE = 2
UNROLL_TWO = 2
F32 = jnp.float32
BF16 = jnp.bfloat16
NT = (((1,), (1,)), ((), ()))
HIGHEST = lax.Precision.HIGHEST


def lanes_of(shape):
    return lax.broadcasted_iota(jnp.int32, shape, len(shape) - 1)


def sublanes_of(shape):
    return lax.broadcasted_iota(jnp.int32, shape, len(shape) - 2)


def split(value):
    return [value[:, k * LANES : (k + 1) * LANES] for k in range(value.shape[1] // LANES)]


def rows_at(start):
    return pl.ds(pl.multiple_of(start, SUB), SUB)


def x_fluxes(damped, coef, east):
    flux = coef * damped
    part = east * flux
    return part, flux - part


def stencil(mu, px, qx, up_x, down_x, damped, coef, north, halo_up, halo_down):
    flux = coef * damped
    py = north * flux
    qy = flux - py
    base = mu - px + qx - py + qy + up_x - down_x
    lane = lanes_of((SUB, LANES))
    last, first = lane == LANES - 1, lane == 0
    py, qy, base = split(py), split(qy), split(base)
    rolled_up = [pltpu.roll(v, LANES - 1, 1) for v in py]
    rolled_down = [pltpu.roll(v, 1, 1) for v in qy]
    count = len(base)
    out = []
    for k in range(count):
        above = rolled_up[k + 1] if k + 1 < count else halo_up
        below = rolled_down[k - 1] if k > 0 else halo_down
        out.append(base[k] + jnp.where(last, above, rolled_up[k]) - jnp.where(first, below, rolled_down[k]))
    return out, py, qy


def shifted(px_here, px_next, qx_prev, qx_here):
    sub = sublanes_of(px_here.shape)
    up = jnp.where(sub == SUB - 1, pltpu.roll(px_next, SUB - 1, 0), pltpu.roll(px_here, SUB - 1, 0))
    down = jnp.where(sub == 0, pltpu.roll(qx_prev, 1, 0), pltpu.roll(qx_here, 1, 0))
    return up, down


def first_step(mu_ref, cour_ref, lim_ref, dir_ref, out_ref, ef_ref, em_ref, ew_ref, xr_ref, xm_ref, xw_ref, damp, east, north, rim):
    level = pl.program_id(0)
    fields, _, rows, width = mu_ref.shape
    tiles = width // LANES
    size = min(GROUP_ONE, rows)
    groups = rows // size
    tall = ef_ref.shape[0]
    lane = lanes_of((SUB, LANES))
    last = lane == LANES - 1
    edge = slice((tiles - 1) * LANES, tiles * LANES)

    @pl.when(level == 0)
    def _():
        for ref in (ef_ref, em_ref, ew_ref, xr_ref):
            ref[...] = jnp.zeros_like(ref)

        def prepare(tile, carry):
            at = rows_at(tile * SUB)
            east[at] = dir_ref[1, 0, at].astype(F32)
            north[at] = dir_ref[1, 1, at].astype(F32)
            side = jnp.where(last, 1 - dir_ref[0, 1, at, edge], dir_ref[0, 1, at, :LANES]).astype(F32)
            for f in range(fields):
                damp[f, at] = 0.5 + 0.5 * lim_ref[1, f, at].astype(F32)
                flag = jnp.where(last, lim_ref[0, f, at, edge], lim_ref[0, f, at, :LANES]).astype(F32)
                rim[f, at] = side * (0.5 + 0.5 * flag)
            return carry

        lax.fori_loop(0, rows // SUB, prepare, 0)

    def group(index, carry):
        f, g = index // groups, lax.rem(index, groups)
        base = g * size
        inside = size // SUB
        starts = [jnp.maximum(base - SUB, 0)] + [base + SUB * t for t in range(inside)] + [jnp.minimum(base + size, rows - SUB)]
        keep_low = jnp.where(g > 0, 1.0, 0.0).astype(F32)
        keep_high = jnp.where(g < groups - 1, 1.0, 0.0).astype(F32)
        slot = level * fields + f
        none = jnp.zeros((SUB, LANES), F32)
        mus = [mu_ref[f, 0, rows_at(s)] for s in starts]
        damped = [m * damp[f, rows_at(s)] for m, s in zip(mus, starts)]
        pq = [x_fluxes(m, cour_ref[1, 0, 0, rows_at(s)], east[rows_at(s)]) for m, s in zip(damped, starts)]
        px = [v[0] for v in pq]
        qx = [v[1] for v in pq]
        qx[0] = qx[0] * keep_low
        px[-1] = px[-1] * keep_high
        for t in range(inside):
            at = rows_at(starts[t + 1])
            up, down = shifted(px[t + 1], px[t + 2], qx[t], qx[t + 1])
            new, py, qy = stencil(
                mus[t + 1], px[t + 1], qx[t + 1], up, down, damped[t + 1], cour_ref[1, 1, 0, at], north[at], none, none
            )
            for k in range(tiles):
                out_ref[f, 0, at, k * LANES : (k + 1) * LANES] = new[k]
            band = starts[t + 1] // tall
            turn = (2 * slot + 1 + band * 64) & (LANES - 1)
            mine = (lane // 2) == slot + 32 * band
            weight = jnp.where(last, cour_ref[0, 1, 0, at, edge], cour_ref[0, 1, 0, at, :LANES]) * rim[f, at]
            place = rows_at(lax.rem(starts[t + 1], tall))
            values = (jnp.where(last, qy[-1], py[0]), jnp.where(last, new[-1], new[0]), weight)
            for ref, value in zip((ef_ref, em_ref, ew_ref), values):
                ref[place] = jnp.where(mine, pltpu.roll(value, turn, 1), ref[place])
        return carry

    def groups_at(index, carry):
        for u in range(UNROLL_ONE):
            group(index + u * (fields // UNROLL_ONE) * groups, carry)
        return carry

    lax.fori_loop(0, fields * groups // UNROLL_ONE, groups_at, 0)

    low, high = slice(0, SUB), slice(rows - SUB, rows)
    for f in range(fields):
        slot = level * fields + f
        turn = 2 * slot + 1
        mine = (lane // 2) == slot
        px, _ = x_fluxes(mu_ref[f, 0, low] * damp[f, low], cour_ref[1, 0, 0, low], east[low])
        _, qx = x_fluxes(mu_ref[f, 0, high] * damp[f, high], cour_ref[1, 0, 0, high], east[high])
        xr_ref[level, f : f + 1] = px[:1]
        xr_ref[level, fields + f : fields + f + 1] = qx[SUB - 1 :]
        px_edge = pltpu.roll(jnp.where(last, px[:, edge], px[:, :LANES]), turn, 1)
        qx_edge = pltpu.roll(jnp.where(last, qx[:, edge], qx[:, :LANES]), turn, 1)
        corner = xr_ref.shape[0] - 1
        xr_ref[corner, 0:1, :LANES] = jnp.where(mine, px_edge, jnp.broadcast_to(xr_ref[corner, 0:1, :LANES], (SUB, LANES)))[:1]
        xr_ref[corner, 4:5, :LANES] = jnp.where(mine, qx_edge, jnp.broadcast_to(xr_ref[corner, 4:5, :LANES], (SUB, LANES)))[SUB - 1 :]
        xm_ref[level, f : f + 1] = out_ref[f, 0, low][:1]
        xm_ref[level, fields + f : fields + f + 1] = out_ref[f, 0, high][SUB - 1 :]
        for at, part, row in ((low, 0, 0), (high, 1, SUB - 1)):
            way = dir_ref[0, 0, at].astype(F32)
            way = 1.0 - way if part else way
            value = way * (0.5 + 0.5 * lim_ref[0, f, at].astype(F32)) * cour_ref[0, 0, 0, at]
            xw_ref[level, part * fields + f : part * fields + f + 1] = value[row : row + 1]


def pick(first, a, b):
    return jnp.where(first, a, b)


def rims(rows, parts, ids, efa_ref, efb_ref, xra_ref, xrb_ref, em_ref, ew_ref, xm_ref, xw_ref, eof_ref, e2_ref, x2_ref, m1_ref, x1_ref, kh_ref, kl_ref):
    me_row = ids[0]
    even_row, even_col = ids[2] == 0, ids[3] == 0
    levels, twice, width = xm_ref.shape
    fields = twice // 2
    tiles = width // LANES
    tall = em_ref.shape[0]
    top_band = (rows - 1) // tall
    lane = lanes_of((tall, LANES))
    sub = sublanes_of((tall, LANES))
    up = pick(even_row, efa_ref[...], efb_ref[...])
    down = pick(even_row, efb_ref[...], efa_ref[...])
    merged = jnp.where(lane % 2 == 1, up, -pltpu.roll(down, 2, 1))
    m1_ref[...] = merged
    fixed = em_ref[...] + jnp.where(lane % 2 == 0, pltpu.roll(up, LANES - 1, 1), -pltpu.roll(down, 1, 1))
    corner = xra_ref.shape[0] - 1
    ca, cb = xra_ref[corner, :, :LANES], xrb_ref[corner, :, :LANES]
    corner_up = pick(even_col, ca, cb)[0:1]
    corner_down = pick(even_col, cb, ca)[4:5]
    if top_band:
        corner_up = pltpu.roll(jnp.broadcast_to(corner_up, (SUB, LANES)), 64 * top_band, 1)[:1]
    fixed = fixed + jnp.where(sub == tall - 1, corner_up, 0.0) - jnp.where(sub == 0, corner_down, 0.0)
    e2_ref[...] = ew_ref[...] * fixed

    lane8 = lanes_of((twice, LANES))
    sub8 = sublanes_of((twice, LANES))
    ends = jnp.where(sub8 < fields, jnp.broadcast_to(merged[0:1], (twice, LANES)), jnp.broadcast_to(merged[tall - 1 :], (twice, LANES)))
    wide = sublanes_of((twice, width))
    for level in range(levels):
        a, b = xra_ref[level], xrb_ref[level]
        halo = jnp.where(wide < fields, pick(even_col, a, b), -pick(even_col, b, a))
        x1_ref[level] = halo
        target = 2 * (level * fields + sub8 % fields) + 1 + jnp.where(sub8 >= fields, 64 * top_band, 0)
        at_last = jnp.sum(jnp.where(lane8 == target, ends, 0.0), axis=1, keepdims=True)
        at_first = jnp.sum(jnp.where(lane8 == (target + 1) % LANES, ends, 0.0), axis=1, keepdims=True)
        here = split(xm_ref[level] + pltpu.roll(halo, fields, 0))
        here[-1] = here[-1] + jnp.where(lane8 == LANES - 1, at_last, 0.0)
        here[0] = here[0] + jnp.where(lane8 == 0, at_first, 0.0)
        for k in range(tiles):
            at = slice(k * LANES, (k + 1) * LANES)
            x2_ref[level, :, at] = xw_ref[level, :, at] * here[k]

    channels = eof_ref.shape[0]
    size = kh_ref.shape[0]
    share = channels // parts
    i = lax.broadcasted_iota(jnp.int32, (size, channels), 0) // SUB
    chosen = ((i // share) ^ me_row) * share + i % share
    left = (lax.broadcasted_iota(jnp.int32, (size, channels), 1) == chosen).astype(F32)
    j = lax.broadcasted_iota(jnp.int32, (channels, size), 1) // SUB
    right = (lax.broadcasted_iota(jnp.int32, (channels, size), 0) == j).astype(F32)
    mixed = jnp.dot(left, eof_ref[...], precision=HIGHEST, preferred_element_type=F32)
    spread = jnp.dot(mixed, right, precision=HIGHEST, preferred_element_type=F32)
    same = (lax.broadcasted_iota(jnp.int32, (size, size), 0) - lax.broadcasted_iota(jnp.int32, (size, size), 1)) % SUB == 0
    spread = jnp.where(same, spread, 0.0)
    high = spread.astype(BF16)
    kh_ref[...] = high
    kl_ref[...] = (spread - high.astype(F32)).astype(BF16)


def second_step(
    offset, parts, n_held, ids, mu_ref, mu_low, mu_high, cour_ref, cx_low, cx_high, lim_ref, lim_low, lim_high, dir_ref, dir_low, dir_high,
    m1_ref, x1_ref, e2a_ref, e2b_ref, x2a_ref, x2b_ref, box_ref, kh_ref, kl_ref, *rest,
):
    outs, (damp, east, north, m2_ref, mixed) = rest[n_held:-5], rest[-5:]
    g = pl.program_id(0)
    fields, levels, _, width = mu_ref.shape
    rows = ids[5]
    tall = m1_ref.shape[0]
    even_row, even_col = ids[2] == 0, ids[3] == 0
    tiles = width // LANES
    size = mu_ref.shape[2]
    inside = size // SUB
    lane = lanes_of((SUB, LANES))
    sub = sublanes_of((SUB, width))
    last, first = lane == LANES - 1, lane == 0

    @pl.when(g == 0)
    def _():
        wide = lanes_of((tall, LANES))
        up = pick(even_row, e2a_ref[...], e2b_ref[...])
        down = pick(even_row, e2b_ref[...], e2a_ref[...])
        m2_ref[...] = jnp.where(wide % 2 == 1, up, -pltpu.roll(down, 2, 1))

    lims = [(lim_low, 0)] + [(lim_ref, SUB * t) for t in range(inside)] + [(lim_high, 0)]
    dirs = [(dir_low, 0)] + [(dir_ref, SUB * t) for t in range(inside)] + [(dir_high, 0)]
    mus = [(mu_low, 0)] + [(mu_ref, SUB * t) for t in range(inside)] + [(mu_high, 0)]
    cxs = [(cx_low, 0)] + [(cour_ref, SUB * t) for t in range(inside)] + [(cx_high, 0)]
    for t in range(inside + 2):
        put = slice(SUB * t, SUB * (t + 1))
        ref, r = dirs[t]
        east[put] = ref[0, 0, r : r + SUB].astype(F32)
        if 0 < t <= inside:
            north[SUB * (t - 1) : SUB * t] = ref[0, 1, r : r + SUB].astype(F32)
        ref, r = lims[t]
        for f in range(fields):
            damp[f, put] = 0.5 + 0.5 * ref[0, f, r : r + SUB].astype(F32)

    base = offset + g * size
    starts = [jnp.maximum(base - SUB, 0)] + [base + SUB * t for t in range(inside)] + [jnp.minimum(base + size, rows - SUB)]
    bands = [s // tall for s in starts]
    places = [lax.rem(s, tall) for s in starts]
    at_start = base == 0
    at_end = base + size == rows
    lat_at = ids[7]
    box_lats = box_ref.shape[1] // (fields * levels * parts)
    per_tile = LANES // box_lats
    total = parts * box_lats
    inner = [((lane + LANES * k - lat_at) >= 0) & ((lane + LANES * k - lat_at) < total) for k in range(tiles)]

    def channel(index, carry):
        f, level = index // levels, lax.rem(index, levels)
        slot = level * fields + f
        vals, damped, px, qx = [], [], [], []
        for t in range(inside + 2):
            ref, r = mus[t]
            value = ref[f, level, r : r + SUB]
            fix = pltpu.roll(m1_ref[rows_at(places[t])], (126 - 2 * slot - 64 * bands[t]) & (LANES - 1), 1)
            pieces = split(value)
            pieces[-1] = pieces[-1] + jnp.where(last, fix, 0.0)
            pieces[0] = pieces[0] + jnp.where(first, fix, 0.0)
            value = jnp.concatenate(pieces, axis=1)
            if t == 1:
                value = value + jnp.where((sub == 0) & at_start, x1_ref[level, pl.ds(fields + f, 1)], 0.0)
            if t == inside:
                value = value + jnp.where((sub == SUB - 1) & at_end, x1_ref[level, pl.ds(f, 1)], 0.0)
            ref, r = cxs[t]
            weighed = value * damp[f, SUB * t : SUB * (t + 1)]
            p, q = x_fluxes(weighed, ref[0, 0, level, r : r + SUB], east[SUB * t : SUB * (t + 1)])
            vals.append(value)
            damped.append(weighed)
            px.append(p)
            qx.append(q)
        halo_low = pick(even_col, x2b_ref[level, pl.ds(fields + f, 1)], x2a_ref[level, pl.ds(fields + f, 1)])
        halo_high = pick(even_col, x2a_ref[level, pl.ds(f, 1)], x2b_ref[level, pl.ds(f, 1)])
        qx[0] = jnp.where(at_start, jnp.broadcast_to(halo_low, (SUB, width)), qx[0])
        px[-1] = jnp.where(at_end, jnp.broadcast_to(halo_high, (SUB, width)), px[-1])
        box_tile = pl.multiple_of((index // per_tile * parts + lax.rem(index, parts)) * LANES, LANES)
        box_turn = (lat_at - lax.rem(index, per_tile) * box_lats) & (LANES - 1)
        put = rows_at(index * SUB)
        for t in range(inside):
            mine = slice(SUB * t, SUB * (t + 1))
            up, down = shifted(px[t + 1], px[t + 2], qx[t], qx[t + 1])
            halo = pltpu.roll(m2_ref[rows_at(places[t + 1])], (126 - 2 * slot - 64 * bands[t + 1]) & (LANES - 1), 1)
            new, _, _ = stencil(
                vals[t + 1], px[t + 1], qx[t + 1], up, down, damped[t + 1], cour_ref[0, 1, level, mine], north[mine], halo, -halo
            )
            moved = pltpu.roll(box_ref[mine, pl.ds(box_tile, LANES)], box_turn, 1)
            for k in range(tiles):
                mixed[t, put, k * LANES : (k + 1) * LANES] = new[k] + jnp.where(inner[k], moved, 0.0)
        return carry

    def channels_at(index, carry):
        for u in range(UNROLL_TWO):
            channel(index * UNROLL_TWO + u, carry)
        return carry

    lax.fori_loop(0, fields * levels // UNROLL_TWO, channels_at, 0)

    channels = fields * levels
    share = channels // parts
    per = len(outs) // parts
    depth = share // per
    for v in range(inside // 2):
        both = []
        for t in (2 * v, 2 * v + 1):
            full = mixed[t]
            high = full.astype(BF16)
            low = (full - high.astype(F32)).astype(BF16)
            result = jnp.dot(kh_ref[...], high, preferred_element_type=F32)
            result += jnp.dot(kl_ref[...], high, preferred_element_type=F32)
            result += jnp.dot(kh_ref[...], low, preferred_element_type=F32)
            both.append(result)
        for c in range(channels):
            at = slice(c * SUB, (c + 1) * SUB)
            pair = jnp.concatenate([both[0][at], both[1][at]], axis=0).astype(BF16)
            outs[(c // share) * per + (c % share) // depth][c % depth, 2 * SUB * v : 2 * SUB * (v + 1)] = pair


def coarse_sums(ids, nest_ref, out_ref, held):
    channels, fine_lat, fine_lon = nest_ref.shape
    lon = ids[1] * fine_lon + lax.broadcasted_iota(jnp.int32, (fine_lat, fine_lon), 1)
    lat = ids[0] * fine_lat + lax.broadcasted_iota(jnp.int32, (fine_lat, fine_lon), 0)
    edge = (lon < RATIO) | (lon >= RATIO * BOXX - RATIO) | (lat < RATIO) | (lat >= RATIO * BOXY - RATIO)
    weight = jnp.where(edge, 1.0, 1.0 / (RATIO * RATIO)).astype(F32)
    for c in range(channels):
        held[c * fine_lat : (c + 1) * fine_lat] = nest_ref[c] * weight
    count = channels * fine_lat // RATIO
    sums = held[pl.ds(0, count, stride=RATIO)]
    for a in range(1, RATIO):
        sums = sums + held[pl.ds(a, count, stride=RATIO)]
    shape = (fine_lon // RATIO, fine_lon)
    select = (lax.broadcasted_iota(jnp.int32, shape, 1) // RATIO == lax.broadcasted_iota(jnp.int32, shape, 0)).astype(F32)
    result = lax.dot_general(select, sums, NT, precision=HIGHEST, preferred_element_type=F32)
    for k, piece in enumerate(split(result)):
        out_ref[:, k * LANES : (k + 1) * LANES] = pltpu.roll(piece, (ids[0] * (fine_lat // RATIO)) & (LANES - 1), 1)


def arrange(masks, lats, ids, near_ref, far_ref, out_ref, box):
    half, slab, wide = near_ref.shape
    rows = out_ref.shape[0]
    for p, (row_mask, col_mask) in enumerate(masks):
        at = pl.multiple_of((ids[1] ^ col_mask) * slab, SUB)
        to = pl.multiple_of((ids[0] ^ row_mask) * wide, LANES)
        box[pl.ds(at, slab), pl.ds(to, wide)] = near_ref[p] if p < half else far_ref[p - half]
    height = box.shape[0]
    away = ids[6]
    row = lax.broadcasted_iota(jnp.int32, (rows, LANES), 0) - away
    inside = (row >= 0) & (row < height)
    turn = lax.rem(lax.rem(away, height) + height, height)
    parts = box.shape[1] // wide
    slot = lanes_of((height, LANES)) // lats
    for k in range(wide // LANES):
        pieces = [box[:, r * wide + k * LANES : r * wide + (k + 1) * LANES] for r in range(parts)]
        for m in range(parts):
            value = pieces[0]
            for r in range(1, parts):
                value = jnp.where((slot - m) % parts == r, pieces[r], value)
            at = (k * parts + m) * LANES
            out_ref[:, at : at + LANES] = jnp.where(inside, pltpu.roll(value, turn, 0)[:rows], 0.0)


def lat_filter_part(start, height, count, parts, cols, ids, *refs):
    pieces, filt, outs = refs[:parts], refs[parts], refs[parts + 1 :]
    lat_block = pieces[0].shape[2]
    lon = pieces[0].shape[1]
    lat_part = filt.shape[0] // cols
    step = 2
    for p in range(count // step):
        right = [ref[step * p : step * (p + 1)].reshape(step * lon, lat_block) for ref in pieces]
        for s0 in range(0, cols, 4):
            acc = None
            for r in range(parts):
                at = pl.ds(pl.multiple_of((ids[0] ^ r) * lat_block, LANES), lat_block)
                left = jnp.concatenate(
                    [
                        filt[pl.ds(pl.multiple_of((ids[1] ^ s) * lat_part + start, 16), height), at]
                        for s in range(s0, min(s0 + 4, cols))
                    ],
                    axis=0,
                )
                term = lax.dot_general(left, right[r], NT, preferred_element_type=F32)
                acc = term if acc is None else acc + term
            for s in range(s0, min(s0 + 4, cols)):
                for c in range(step):
                    value = acc[(s - s0) * height : (s - s0 + 1) * height, c * lon : (c + 1) * lon]
                    outs[s][step * p + c] = value.astype(BF16)


def lon_filter_part(half, height, cols, parts, n_first, aliased, owners, ids, *refs):
    firsts = refs[:n_first]
    lasts = refs[n_first : n_first + cols]
    filters = refs[n_first + cols : n_first + cols + 2 * parts]
    rest = refs[n_first + cols + 2 * parts + (1 if aliased else 0) :]
    out, lines, stage, sem, held, in_sem = rest
    channels, _, lon = lasts[0].shape
    wide = lines.shape[1] // cols
    rows = channels * height
    block = filters[0].shape[0]
    strips = block // LANES

    def flush(j, k):
        side = ids[8] if j % 2 == 0 else 1 - ids[8]
        even, odd = owners[j // 2]
        owner = (ids[0] ^ jnp.where(side == 0, even, odd)) * 2 + side
        at = pl.ds(pl.multiple_of(owner * block + k * LANES, LANES), LANES)
        slot = j % 4
        return pltpu.make_async_copy(stage.at[slot, k], out.at[pl.ds(half * rows, rows), at], sem.at[slot, k])

    def fetch(j):
        return pltpu.make_async_copy(filters[j], held.at[pl.ds(j * block, block)], in_sem.at[j])

    fetch(0).start()
    fetch(1).start()
    for s in range(cols):
        base = pl.multiple_of((ids[1] ^ s) * wide, LANES)
        for c in range(channels):
            put = slice(c * height, (c + 1) * height)
            for b in range(wide // lon - 1):
                groups = n_first // cols // (wide // lon - 1)
                each = channels // groups
                ref = firsts[(b * groups + c // each) * cols + s]
                lines[put, pl.ds(base + b * lon, lon)] = ref[c % each, half * height : (half + 1) * height]
            lines[put, pl.ds(base + wide - lon, lon)] = lasts[s][c]
    for p in range(parts):
        fetch(2 * p).wait()
        fetch(2 * p + 1).wait()
        if p + 1 < parts:
            fetch(2 * p + 2).start()
            fetch(2 * p + 3).start()
        right = held[2 * p * block : (2 * p + 2) * block]
        acc = lax.dot_general(lines[...], right, NT, preferred_element_type=F32)
        for j in (2 * p, 2 * p + 1):
            for k in range(strips):
                if j >= 4:
                    flush(j - 4, k).wait()
                begin = (j % 2) * block + k * LANES
                for c in range(channels):
                    stage[j % 4, k, pl.ds(c, height, stride=channels), :] = acc[c * height : (c + 1) * height, begin : begin + LANES]
                flush(j, k).start()
    for j in range(max(0, 2 * parts - 4), 2 * parts):
        for k in range(strips):
            flush(j, k).wait()


def swap(value, axis, mask):
    count = lax.axis_size(axis)
    return lax.ppermute(value, axis, [(i, i ^ mask) for i in range(count)])


def neighbours(value, axis, parity):
    count = lax.axis_size(axis)
    pairs = []
    for i in range(parity, count - 1, 2):
        pairs += [(i, i + 1), (i + 1, i)]
    return lax.ppermute(value, axis, pairs)


def shape_of(shape, dtype=F32):
    return jax.ShapeDtypeStruct(shape, dtype)


def whole(shape):
    return pl.BlockSpec(shape, lambda *_: (0,) * len(shape))


VMEM_SPEC = pl.BlockSpec(memory_space=pltpu.VMEM)
SMEM_SPEC = pl.BlockSpec(memory_space=pltpu.SMEM)
ANY_SPEC = pl.BlockSpec(memory_space=pl.ANY)


def shards(final_sens, courant, limiter, directions, nest_sens, box_lon, box_lat, eof, lat_filter, lon_filter):
    channels, lon_block, lat_block = final_sens.shape
    fields, levels = limiter.shape[1], courant.shape[2]
    rows_count, cols_count = lax.axis_size("row"), lax.axis_size("col")
    me_row, me_col = lax.axis_index("row"), lax.axis_index("col")
    ids = jnp.stack(
        [
            me_row,
            me_col,
            me_row % 2,
            me_col % 2,
            me_row * 0,
            me_row * 0 + lon_block,
            box_lon[0] - me_col * lon_block,
            box_lat[0] - me_row * lat_block,
            me_col % 2,
        ]
    ).astype(jnp.int32)
    lat_part = lat_filter.shape[0] // cols_count
    share = channels // rows_count
    tall = min(BAND, lon_block)
    n_bands = lon_block // tall

    height = lon_filter.shape[0] // 2
    gathered = [lax.dynamic_slice_in_dim(lon_filter, (me_col % 2) * height, height, 0)]
    orders = [2**k for k in range(10) if 2**k < rows_count]
    turns = (orders, orders[::-1])
    owners = [(0, 0)]

    def gather(stage, pieces):
        pairs = []
        for i in range(rows_count * cols_count):
            row, col = divmod(i, cols_count)
            pairs.append((i, (row ^ turns[col % 2][stage]) * cols_count + col))
        return [lax.ppermute(piece, ("row", "col"), pairs) for piece in pieces]

    direct = []
    for stage in range(len(orders)):
        direct += gather(stage, gathered[:1])

    nest = jnp.transpose(nest_sens, (0, 2, 1))
    fine_lat, fine_lon = nest.shape[1:]
    coarse = pl.pallas_call(
        coarse_sums,
        out_shape=shape_of((fine_lon // RATIO, channels * fine_lat // RATIO)),
        in_specs=[SMEM_SPEC, VMEM_SPEC],
        out_specs=VMEM_SPEC,
        scratch_shapes=[pltpu.VMEM((channels * fine_lat, fine_lon), F32)],
        name="coarse",
    )(ids, nest)
    masks = [(0, 0)]
    stages = [("col", m) for m in (2**k for k in range(1, 10)) if m < cols_count]
    stages += [("row", m) for m in (2**k for k in range(10)) if m < rows_count]
    stages += [("col", 1)]

    def spread(held, count, last=False):
        nonlocal stages, masks
        for axis, mask in stages[:count]:
            other = swap(held, axis, mask)
            held = (held, other) if last else jnp.concatenate([held, other], axis=0)
            masks = masks + [(r ^ mask, c) if axis == "row" else (r, c ^ mask) for r, c in masks]
        stages = stages[count:]
        return held

    def after(value, *others):
        return lax.optimization_barrier((value, *others))[0]

    held = spread(coarse[None], 2)

    mu = final_sens.reshape(fields, levels, lon_block, lat_block)
    call = pl.pallas_call(
        first_step,
        grid=(levels,),
        out_shape=(
            shape_of(mu.shape),
            shape_of((tall, LANES)),
            shape_of((tall, LANES)),
            shape_of((tall, LANES)),
            shape_of((levels + 1, 2 * fields, lat_block)),
            shape_of((levels, 2 * fields, lat_block)),
            shape_of((levels, 2 * fields, lat_block)),
        ),
        in_specs=[
            pl.BlockSpec((fields, 1, lon_block, lat_block), lambda l: (0, l, 0, 0)),
            pl.BlockSpec((2, 2, 1, lon_block, lat_block), lambda l: (0, 0, l, 0, 0)),
            whole(limiter.shape),
            whole(directions.shape),
        ],
        out_specs=(
            pl.BlockSpec((fields, 1, lon_block, lat_block), lambda l: (0, l, 0, 0)),
            whole((tall, LANES)),
            whole((tall, LANES)),
            whole((tall, LANES)),
            whole((levels + 1, 2 * fields, lat_block)),
            whole((levels, 2 * fields, lat_block)),
            whole((levels, 2 * fields, lat_block)),
        ),
        scratch_shapes=[
            pltpu.VMEM((fields, lon_block, lat_block), F32),
            pltpu.VMEM((lon_block, lat_block), F32),
            pltpu.VMEM((lon_block, lat_block), F32),
            pltpu.VMEM((fields, lon_block, LANES), F32),
        ],
        name="first_step",
    )
    mu1, ef, em, ew, xr, xm, xw = call(mu, courant, limiter, directions)
    held = spread(after(held, ef), 1)
    efa, efb = neighbours(ef, "row", 0), neighbours(ef, "row", 1)
    xra, xrb = neighbours(xr, "col", 0), neighbours(xr, "col", 1)
    held = spread(after(held, efa, efb, xra, xrb), len(stages) - 1)
    size = channels * SUB
    call = pl.pallas_call(
        functools.partial(rims, lon_block, rows_count),
        out_shape=(
            shape_of(ef.shape),
            shape_of(xm.shape),
            shape_of(ef.shape),
            shape_of(xm.shape),
            shape_of((size, size), BF16),
            shape_of((size, size), BF16),
        ),
        in_specs=[SMEM_SPEC] + [VMEM_SPEC] * 9,
        out_specs=(VMEM_SPEC,) * 6,
        name="rims",
    )
    e2, x2, m1, x1, kh, kl = call(ids, efa, efb, xra, xrb, em, ew, xm, xw, eof)
    e2a, e2b = neighbours(e2, "row", 0), neighbours(e2, "row", 1)
    x2a, x2b = neighbours(x2, "col", 0), neighbours(x2, "col", 1)
    held = spread(held, 1, True)
    box = pl.pallas_call(
        functools.partial(arrange, masks, fine_lat // RATIO),
        out_shape=shape_of((lon_block, rows_count * coarse.shape[1])),
        in_specs=[SMEM_SPEC, VMEM_SPEC, VMEM_SPEC],
        out_specs=VMEM_SPEC,
        scratch_shapes=[pltpu.VMEM((cols_count * coarse.shape[0], rows_count * coarse.shape[1]), F32)],
        name="arrange",
    )(ids, *held)

    top = lon_block // SUB - 1

    def control(band, halves, kl, cut=1, part=0, held=()):
        size_two = min(GROUP, tall) // cut
        groups = tall // size_two // cut
        fine = size_two // SUB

        def at(g):
            return (band * cut + part) * groups + g

        def low(g):
            return jnp.maximum(at(g) * fine - 1, 0)

        def high(g):
            return jnp.minimum(at(g) * fine + fine, top)

        depth = share // halves
        return pl.pallas_call(
            functools.partial(second_step, band * tall + part * (tall // cut), rows_count, len(held)),
            grid=(groups,),
            out_shape=(shape_of((depth, tall, lat_block), BF16),) * (rows_count * halves),
            in_specs=[
                SMEM_SPEC,
                pl.BlockSpec((fields, levels, size_two, lat_block), lambda g: (0, 0, at(g), 0)),
                pl.BlockSpec((fields, levels, SUB, lat_block), lambda g: (0, 0, low(g), 0)),
                pl.BlockSpec((fields, levels, SUB, lat_block), lambda g: (0, 0, high(g), 0)),
                pl.BlockSpec((1, 2, levels, size_two, lat_block), lambda g: (0, 0, 0, at(g), 0)),
                pl.BlockSpec((1, 1, levels, SUB, lat_block), lambda g: (0, 0, 0, low(g), 0)),
                pl.BlockSpec((1, 1, levels, SUB, lat_block), lambda g: (0, 0, 0, high(g), 0)),
                pl.BlockSpec((1, fields, size_two, lat_block), lambda g: (0, 0, at(g), 0)),
                pl.BlockSpec((1, fields, SUB, lat_block), lambda g: (0, 0, low(g), 0)),
                pl.BlockSpec((1, fields, SUB, lat_block), lambda g: (0, 0, high(g), 0)),
                pl.BlockSpec((1, 2, size_two, lat_block), lambda g: (0, 0, at(g), 0)),
                pl.BlockSpec((1, 1, SUB, lat_block), lambda g: (0, 0, low(g), 0)),
                pl.BlockSpec((1, 1, SUB, lat_block), lambda g: (0, 0, high(g), 0)),
                whole(m1.shape),
                whole(x1.shape),
                whole(e2.shape),
                whole(e2.shape),
                whole(x2.shape),
                whole(x2.shape),
                pl.BlockSpec((size_two, box.shape[1]), lambda g: (at(g), 0)),
                whole(kh.shape),
                whole(kl.shape),
            ]
            + [ANY_SPEC] * len(held),
            out_specs=(pl.BlockSpec((depth, size_two, lat_block), lambda g: (0, part * groups + g, 0)),) * (rows_count * halves),
            input_output_aliases={22 + i: i for i in range(len(held))},
            scratch_shapes=[
                pltpu.VMEM((fields, size_two + 2 * SUB, lat_block), F32),
                pltpu.VMEM((size_two + 2 * SUB, lat_block), F32),
                pltpu.VMEM((size_two, lat_block), F32),
                pltpu.VMEM((tall, LANES), F32),
                pltpu.VMEM((fine, channels * SUB, lat_block), F32),
            ],
            name="second_step",
        )(ids, mu1, mu1, mu1, courant, courant, courant, limiter, limiter, limiter, directions, directions, directions,
          m1, x1, e2a, e2b, x2a, x2b, box, kh, kl, *held)

    def to_rows(pieces):
        moved = [pieces[0]]
        for s in range(1, rows_count):
            moved.append(swap(pieces[s], "row", s))
        return moved

    def smooth(pieces, start, height, token):
        count = pieces[0].shape[0]
        filt = lat_filter if token is None else after(lat_filter, token)
        call = pl.pallas_call(
            functools.partial(lat_filter_part, start, height, count, rows_count, cols_count),
            out_shape=(shape_of((count, height, tall), BF16),) * cols_count,
            in_specs=[SMEM_SPEC] + [VMEM_SPEC] * (rows_count + 1),
            out_specs=(VMEM_SPEC,) * cols_count,
            name="lat_filter",
        )
        outs = call(ids, *pieces, filt)
        moved = {}
        for s in range(cols_count - 1, 0, -1):
            moved[s] = swap(outs[s], "col", s)
        return [outs[0]] + [moved[s] for s in range(1, cols_count)], outs[-1]

    firsts = []
    sent = []
    order = None
    token = None
    for band in range(n_bands):
        final = band == n_bands - 1
        halves = 1 if final else 2
        if band:
            kl = after(kl, order)
            outs = control(band, halves, kl, 2)
            token = outs[0]
            outs = control(band, halves, kl, 2, 1, outs)
        else:
            outs = control(band, halves, kl)
        order = outs[-1]
        for h in range(halves):
            sent.append(to_rows([outs[s * halves + h] for s in range(rows_count)]))

    for pieces in sent[:-1]:
        moved, token = smooth(pieces, 0, lat_part, token)
        firsts += moved
    half_height = lat_part // 2
    lasts = []
    for h in range(2):
        early = token
        moved, token = smooth(sent[-1], h * half_height, half_height, token)
        lasts.append(moved)
    for stage in range(len(orders)):
        gathered += [direct[stage]] + gather(stage, [after(piece, early) for piece in gathered[1:]])
        owners += [(a ^ turns[0][stage], b ^ turns[1][stage]) for a, b in owners]
    filters = []
    for j, piece in enumerate(gathered):
        late = j and j == len(gathered) - 1
        filters += [piece, swap(after(piece, token if late else early), "col", 1)]

    n_lon = cols_count * lon_block
    rows = share * half_height
    if lon_block % LANES:
        stacked = jnp.stack([jnp.concatenate([lasts[0][s], lasts[1][s]], axis=1) for s in range(cols_count)])
        lines = jnp.take(stacked, me_col ^ jnp.arange(cols_count), axis=0)
        lines = jnp.transpose(lines, (2, 1, 0, 3)).reshape(lat_part, share, n_lon)
        whole_filter = jnp.zeros((n_lon, n_lon), BF16)
        for j, piece in enumerate(filters):
            side = me_col % 2 if j % 2 == 0 else 1 - me_col % 2
            owner = (me_row ^ jnp.where(side == 0, *owners[j // 2])) * 2 + side
            whole_filter = lax.dynamic_update_slice_in_dim(whole_filter, piece, owner * height, 0)
        return jnp.einsum("lci,oi->lco", lines, whole_filter, preferred_element_type=F32)
    out = None
    for h in range(2):
        aliased = out is not None
        operands = (ids, *firsts, *lasts[h], *filters) + ((out,) if aliased else ())
        call = pl.pallas_call(
            functools.partial(lon_filter_part, h, half_height, cols_count, rows_count, len(firsts), aliased, owners),
            out_shape=shape_of((2 * rows, n_lon)),
            in_specs=[SMEM_SPEC] + [VMEM_SPEC] * (len(firsts) + cols_count) + [ANY_SPEC] * (2 * rows_count + aliased),
            out_specs=ANY_SPEC,
            scratch_shapes=[
                pltpu.VMEM((rows, n_lon), BF16),
                pltpu.VMEM((4, height // LANES, rows, LANES), F32),
                pltpu.SemaphoreType.DMA((4, height // LANES)),
                pltpu.VMEM((2 * rows_count * height, n_lon), BF16),
                pltpu.SemaphoreType.DMA((2 * rows_count,)),
            ],
            input_output_aliases={len(operands) - 1: 0} if aliased else {},
            name="lon_filter",
        )
        out = call(*operands)
    return out.reshape(lat_part, share, n_lon)


def solution(mesh):
    placed = (
        P(None, "col", "row"),
        P(None, None, None, "col", "row"),
        P(None, None, "col", "row"),
        P(None, None, "col", "row"),
        P(None, "col", "row"),
        P(),
        P(),
        P(),
        P(),
        P("row", None),
    )
    return jax.shard_map(shards, mesh=mesh, in_specs=placed, out_specs=P("col", "row", None), check_vma=False)
```
